32 devices in a mesh: shard: 4 (over x, core), rep: 8 (over z, y).
Axes of the slice: x: 2, y: 2, z: 4, core: 2. Of those that a mesh axis runs over, the one named last changes fastest.
Arguments:
- tokens: bfloat16 [96, 197, 512], P(('shard', 'rep')), may hold values from -21 to 21
- cotangent: bfloat16 [96, 197, 512], P(('shard', 'rep')), may hold values from -6 to 6
- gain_one: bfloat16 [512], P('shard'), may hold values from 0.5 to 1.5
- w_query: bfloat16 [512, 512], P('shard'), may hold values from -0.25 to 0.25
- w_key: bfloat16 [512, 512], P('shard'), may hold values from -0.25 to 0.25
- w_value: bfloat16 [512, 512], P('shard'), may hold values from -0.25 to 0.25
- w_output: bfloat16 [512, 512], P('shard'), may hold values from -0.75 to 0.75
- gain_two: bfloat16 [512], P('shard'), may hold values from 0.5 to 1.5
- w_router: bfloat16 [512, 4], P('shard'), may hold values from -0.25 to 0.25
- w_in: bfloat16 [4, 512, 2048], P('shard'), may hold values from -0.25 to 0.25
- w_out: bfloat16 [4, 2048, 512], P('shard'), may hold values from -0.25 to 0.25
- routes: int32 [96, 197, 2], P(('shard', 'rep')), may hold values from 0 to 3, all different within a row
Outputs:
- output: bfloat16 [96, 197, 512], P(('shard', 'rep'))
- grad_tokens: bfloat16 [96, 197, 512], P(('shard', 'rep'))
- grad_gain_one: float32 [512], P('shard')
- grad_query: float32 [512, 512], P('shard')
- grad_key: float32 [512, 512], P('shard')
- grad_value: float32 [512, 512], P('shard')
- grad_output: float32 [512, 512], P('shard')
- grad_gain_two: float32 [512], P('shard')
- grad_router: float32 [512, 4], P('shard')
- grad_w_in: float32 [4, 512, 2048], P('shard')
- grad_w_out: float32 [4, 2048, 512], P('shard')
- rms_stream: float32 [], replicated
- rms_attn: float32 [], replicated
- rms_moe: float32 [], replicated
The draws below stay inside these ranges and needn't reach their ends.
Inputs may be any that keep to these rules, and one draw needn't show every extreme that they name: `routes`: each token names two different experts, and every expert is named by some token.
All inputs are finite; a program needn't handle non-finite values.
Results may differ from the reference program's by a relative error of at most 0.017.
Values may be sent and summed in bfloat16 or wider, within the bound.
No kernel may reach another device: no remote copies, remote signals or barrier semaphores. Data moves between devices by JAX's collectives and lax.ppermute only.
A program may use at most 256 MiB of HBM per device.

```python
import math
import jax
import jax.numpy as jnp
from jax import lax

D = 512
HEADS = 8
HEAD_DIM = 64
F = 2048
EXPERTS = 4
SEQ = 197
IMAGES = 96


def draw_tokens(key, part):
    key_common, second = jax.random.split(key, 2)
    position = jnp.arange(IMAGES, dtype=jnp.float32) / max(IMAGES - 1, 1)
    image_scale = jnp.exp(jnp.log(3.0) * position)[:, None, None]
    mixing = position[:, None, None]
    common = jnp.clip(jax.random.normal(key_common, (IMAGES, 1, D), jnp.float32), -3.0, 3.0)
    rough_part = jnp.clip(jax.random.normal(second, (IMAGES, SEQ, D), jnp.float32), -4.0, 4.0)
    factor = jnp.ones((IMAGES, SEQ, 1), jnp.float32)
    return (image_scale * factor * (mixing * common + rough_part)).astype(jnp.bfloat16)


def shard_levels(key, dims, cuts, smallest, largest):
    gain = 1.0
    for axis_at, blocks in cuts:
        steps = jax.random.uniform(jax.random.fold_in(jax.random.fold_in(key, 6), axis_at), (blocks,), jnp.float32, smallest / len(cuts), largest / len(cuts))
        gain = gain * jnp.repeat(jnp.exp(steps), dims[axis_at] // blocks).reshape((-1,) + (1,) * (len(dims) - 1 - axis_at))
    return gain


def distinct(stream_key, rows, number_of, top, lift):
    ranking = jax.random.permutation(jax.random.fold_in(stream_key, 1), number_of)
    favour = ranking
    for power in range(3):
        favour = favour * favour // number_of
    favour = favour * lift // number_of
    tickets = jax.random.randint(jax.random.fold_in(stream_key, 2), (rows, number_of), 0, 4096) + favour
    fixed_rows = jax.random.permutation(jax.random.fold_in(stream_key, 3), rows)[jnp.arange(number_of) % rows]
    tickets = jnp.where(jnp.arange(rows)[:, None] == fixed_rows[None, :], 1 << 14, tickets)
    merit = tickets * number_of + jnp.arange(number_of)
    return lax.top_k(merit.astype(jnp.int32), top)[1].astype(jnp.int32)


def bell_draw(rng, dims, width, reach, pieces=(), kind=jnp.bfloat16):
    gain = shard_levels(rng, dims, pieces, -0.22, 0.18) if pieces else 1.0
    values = jax.random.normal(rng, dims, jnp.float32) * width * gain
    return jnp.minimum(jnp.maximum(values, -reach), reach).astype(kind)


def setup_inputs(seed: int = 0) -> dict:
    keys = jax.random.split(jax.random.key(seed), 13)
    tokens = draw_tokens(jax.random.fold_in(keys[12], 71), 0)
    cotangent = bell_draw(keys[1], (IMAGES, SEQ, D), 1.0, 6.0, ((0, 32),))
    gain_one = jnp.clip(1.0 + 0.1 * jax.random.normal(keys[2], (D,), jnp.float32), 0.5, 1.5).astype(jnp.bfloat16)
    w_query = bell_draw(keys[3], (D, D), D ** -0.5, 0.25, ((0, 4),))
    w_key = bell_draw(keys[4], (D, D), D ** -0.5, 0.25, ((0, 4),))
    w_value = bell_draw(keys[5], (D, D), D ** -0.5, 0.25, ((0, 4),))
    w_output = bell_draw(keys[6], (D, D), (D // 8) ** -0.5, 0.75, ((0, 4),))
    gain_two = jnp.clip(1.0 + 0.1 * jax.random.normal(keys[7], (D,), jnp.float32), 0.5, 1.5).astype(jnp.bfloat16)
    w_router = bell_draw(keys[8], (D, EXPERTS), D ** -0.5, 0.25, ((0, 4),))
    w_in = bell_draw(keys[9], (EXPERTS, D, F), D ** -0.5, 0.25, ((0, 4),))
    w_out = bell_draw(keys[10], (EXPERTS, F, D), (F // 4) ** -0.5, 0.25, ((0, 4),))
    routes = distinct(keys[11], IMAGES * SEQ, EXPERTS, 2, 0).reshape((IMAGES, SEQ, 2))
    return {"tokens": tokens, "cotangent": cotangent, "gain_one": gain_one, "w_query": w_query, "w_key": w_key, "w_value": w_value, "w_output": w_output, "gain_two": gain_two, "w_router": w_router, "w_in": w_in, "w_out": w_out, "routes": routes}


EPSILON = 1e-06

@jax.custom_vjp
def low(v):
    return lax.optimization_barrier(v.astype(jnp.bfloat16)).astype(jnp.float32)

@jax.custom_vjp
def low_back(v):
    return v

def low_keep(v):
    return (low(v), None)

def low_pass(kept, grad):
    return (grad,)

def back_keep(v):
    return (v, None)

def back_low(kept, grad):
    return (low(grad),)
low.defvjp(low_keep, low_pass)
low_back.defvjp(back_keep, back_low)

def product(left_side, right_side):
    return jnp.dot(left_side, right_side, precision=lax.Precision.HIGHEST)

def norm_layer(values, norm_gain):
    center = values - lax.optimization_barrier(jnp.mean(values, axis=-1, keepdims=True))
    spread = lax.optimization_barrier(jnp.mean(center * center, axis=-1, keepdims=True))
    return center * lax.rsqrt(spread + EPSILON) * norm_gain

def exact_gelu(values):
    return jax.nn.gelu(values, approximate=False)

def forward(hidden_in, gain_one, w_query, w_key, w_value, w_output, gain_two, w_router, w_in, w_out, route_block):
    images = hidden_in.shape[0]
    flat_rows = hidden_in.reshape(images * SEQ, D)
    factor = HEAD_DIM ** (-0.5)
    input_one = low(norm_layer(flat_rows, gain_one))
    query_rows = low(low_back(product(input_one, w_query))).reshape(images, SEQ, HEADS, HEAD_DIM)
    key_rows = low(low_back(product(input_one, w_key))).reshape(images, SEQ, HEADS, HEAD_DIM)
    value_rows = low(low_back(product(input_one, w_value))).reshape(images, SEQ, HEADS, HEAD_DIM)
    scores = low_back(jnp.einsum('bqhk,bshk->bhqs', query_rows, key_rows, precision=lax.Precision.HIGHEST) * factor)
    attn_probs = low(jax.nn.softmax(scores, axis=-1))
    mixed = jnp.einsum('bhqs,bshk->bqhk', attn_probs, value_rows, precision=lax.Precision.HIGHEST)
    mixed = low(low_back(mixed.reshape(images * SEQ, D)))
    attn_out = low_back(product(mixed, w_output))
    after_attn = flat_rows + attn_out
    input_two = low(norm_layer(after_attn, gain_two))
    logits = low_back(product(input_two, w_router))
    router_probs = jax.nn.softmax(logits, axis=-1)
    expert_ids = jnp.arange(EXPERTS, dtype=jnp.int32)
    chosen = lax.optimization_barrier(jnp.sum((route_block.reshape(images * SEQ, 2)[:, :, None] == expert_ids[None, None, :]).astype(jnp.float32), axis=1))
    combine = router_probs * chosen
    pre_act = low_back(jnp.einsum('td,edf->tef', input_two, w_in, precision=lax.Precision.HIGHEST))
    activated = low(exact_gelu(pre_act))
    expert_out = low_back(jnp.einsum('tef,efd->ted', activated, w_out, precision=lax.Precision.HIGHEST))
    moe_out = lax.optimization_barrier(jnp.sum(combine[:, :, None] * expert_out, axis=1))
    result = after_attn + moe_out
    return (result.reshape(images, SEQ, D), (attn_out, moe_out))

def reference(tokens, cotangent, gain_one, w_query, w_key, w_value, w_output, gain_two, w_router, w_in, w_out, routes):
    params = tuple((weight.astype(jnp.float32) for weight in (gain_one, w_query, w_key, w_value, w_output, gain_two, w_router, w_in, w_out)))
    group_size = math.gcd(IMAGES, 16)
    steps_count = IMAGES // group_size
    token_groups = tokens.astype(jnp.float32).reshape(steps_count, group_size, SEQ, D)
    cot_groups = cotangent.astype(jnp.float32).reshape(steps_count, group_size, SEQ, D)
    route_groups = routes.reshape(steps_count, group_size, SEQ, 2)

    def one_group(running, group_block):
        token_block, cot_block, route_block = group_block

        def wrapped(hidden_in, *weights):
            return forward(hidden_in, *weights, route_block)
        result, pullback, extras = jax.vjp(wrapped, token_block, *params, has_aux=True)
        gradients = pullback(cot_block)
        square_sums = jnp.stack([jnp.sum(result * result), jnp.sum(extras[0] * extras[0]), jnp.sum(extras[1] * extras[1])])
        totals = tuple((earlier + update for earlier, update in zip(running[0], gradients[1:])))
        return ((totals, running[1] + square_sums), (result.astype(jnp.bfloat16), gradients[0].astype(jnp.bfloat16)))
    initial = (tuple((jnp.zeros(weight.shape, jnp.float32) for weight in params)), jnp.zeros((3,), jnp.float32))
    finals, outputs = lax.scan(one_group, initial, (token_groups, cot_groups, route_groups))
    grad_list, square_total = finals
    count_all = float(IMAGES * SEQ * D)
    roots = jnp.sqrt(square_total / count_all)
    output = outputs[0].reshape(IMAGES, SEQ, D)
    grad_tokens = outputs[1].reshape(IMAGES, SEQ, D)
    return (output, grad_tokens, grad_list[0], grad_list[1], grad_list[2], grad_list[3], grad_list[4], grad_list[5], grad_list[6], grad_list[7], grad_list[8], roots[0], roots[1], roots[2])
```

```python
import functools

import jax
import jax.numpy as jnp
from jax import lax
from jax.experimental import pallas as pl
from jax.experimental.pallas import tpu as pltpu
from jax.sharding import PartitionSpec as P

HEADS = 8
HEAD_DIM = 64
EPSILON = 1e-06
LANES = 128
TAIL = 16
MASK_ROW = 8
VMEM_LIMIT = 60 * 1024 * 1024

BF16 = jnp.bfloat16
F32 = jnp.float32

ERF_P = 0.3275911
ERF_A = (0.254829592, -0.284496736, 1.421413741, -1.453152027, 1.061405429)
LOG2E = 1.4426950408889634
ROOT_HALF = 0.7071067811865476
INV_ROOT_2PI = 0.3989422804014327


def round_up(value, multiple):
    return (value + multiple - 1) // multiple * multiple


def nn(a, b):
    return lax.dot_general(a, b, (((1,), (0,)), ((), ())), preferred_element_type=F32)


def nt(a, b):
    return lax.dot_general(a, b, (((1,), (1,)), ((), ())), preferred_element_type=F32)


def tn(a, b):
    return lax.dot_general(a, b, (((0,), (0,)), ((), ())), preferred_element_type=F32)


def norm_stats(values):
    center = values - jnp.mean(values, axis=-1, keepdims=True)
    inverse = lax.rsqrt(jnp.mean(center * center, axis=-1, keepdims=True) + EPSILON)
    return center * inverse, inverse


def norm_back(grad_normed, normed, inverse):
    mean_plain = jnp.mean(grad_normed, axis=-1, keepdims=True)
    mean_cross = jnp.mean(grad_normed * normed, axis=-1, keepdims=True)
    return inverse * (grad_normed - mean_plain - normed * mean_cross)


def gelu_pair(u):
    bell = jnp.exp2(u * u * (-0.5 * LOG2E))
    t = 1.0 / (1.0 + (ERF_P * ROOT_HALF) * jnp.abs(u))
    a1, a2, a3, a4, a5 = (0.5 * a for a in ERF_A)
    tail = t * (a1 + t * (a2 + t * (a3 + t * (a4 + t * a5)))) * bell
    cdf = jnp.where(u < 0.0, tail, 1.0 - tail)
    return u * cdf, cdf + u * (bell * INV_ROOT_2PI)


def split_heads(pair):
    low = lax.broadcasted_iota(jnp.int32, pair.shape, 1) < HEAD_DIM
    zero = jnp.zeros_like(pair)
    return jnp.concatenate([jnp.where(low, pair, zero), jnp.where(low, zero, pair)], axis=0)


def join_heads(stacked):
    rows = stacked.shape[0] // 2
    low = lax.broadcasted_iota(jnp.int32, (rows, stacked.shape[1]), 1) < HEAD_DIM
    return jnp.where(low, stacked[:rows], stacked[rows:])


def params():
    return pltpu.CompilerParams(vmem_limit_bytes=VMEM_LIMIT)


def cost(flops, nbytes, trans=0):
    return pl.CostEstimate(flops=int(flops), bytes_accessed=int(nbytes), transcendentals=int(trans))


def whole(shape):
    return pl.BlockSpec(shape, lambda *_: (0,) * len(shape))


SMEM_SPEC = pl.BlockSpec(memory_space=pltpu.SMEM)


def pack_kernel(wq, wk, wv, wo, g1, g2, wr, masks, cot, wp, gp, *, seq, pad):
    d = wq.shape[1]
    rows = wq.shape[0]
    for n, w in enumerate((wq, wk, wv, wo)):
        wp[0:rows, n * d : (n + 1) * d] = w[...]
    router = jnp.concatenate(
        [wr[...].astype(F32), jnp.zeros((rows, LANES - wr.shape[1]), F32)], axis=1
    )
    router = router.T[0:TAIL, :]
    row = lax.broadcasted_iota(jnp.int32, (TAIL, LANES), 0)
    head = jnp.where(row == 4, g1[...].astype(F32), router)
    head = jnp.where(row == 5, g2[...].astype(F32), head)
    wp[rows : rows + TAIL, :] = jnp.zeros((TAIL, wp.shape[1]), BF16)
    tokens = masks.shape[1]
    wp[rows : rows + TAIL, 0:tokens] = masks[...].astype(BF16)
    wp[rows : rows + TAIL, 0:LANES] = (head + masks[:, 0:LANES]).astype(BF16)
    gp[...] = jnp.zeros(gp.shape, BF16)
    for i in range(cot.shape[0]):
        gp[i * pad : i * pad + seq, :] = cot[i]


def turn_kernel(w1, w2, w1t, w2t):
    w1t[...] = w1[...].T
    w2t[...] = w2[...].T


def attn_fwd_kernel(idx, tok, w0, w1, w2, w3, wfull, rt, qkv, p, o, a1, h1, a2, ssq, *, seq):
    i = pl.program_id(0)
    pad, d = tok.shape[1], tok.shape[2]
    keys = qkv.shape[1]
    rows = w0.shape[0] - TAIL

    @pl.when(i == 0)
    def _():
        for n, w in enumerate((w0, w1, w2, w3)):
            at = pl.multiple_of(idx[n] * rows, rows)
            wfull[pl.ds(at, rows), :] = w[0:rows, :]
            rt[:, pl.ds(at, rows)] = w[rows : rows + TAIL, 0:rows].astype(F32)
        for ref in (o, a1, a2):
            ref[...] = jnp.zeros(ref.shape, ref.dtype)
        ssq[...] = jnp.zeros(ssq.shape, F32)

    here = pl.ds(pl.multiple_of(i * pad, TAIL), pad)
    valid = lax.broadcasted_iota(jnp.int32, (pad, 1), 0) < seq
    x = jnp.where(valid, tok[0].astype(F32), 0.0)
    n1, _ = norm_stats(x)
    in_one = (n1 * rt[4:5, :]).astype(BF16)
    a1[here, :] = in_one
    proj = nn(in_one, wfull[:, 0 : 3 * d])
    qkv[0, 0:pad, 0:d] = (proj[:, 0:d].astype(BF16).astype(F32) * HEAD_DIM**-0.5).astype(BF16)
    qkv[0, 0:pad, d:] = proj[:, d:].astype(BF16)
    qkv[0, pad:keys, :] = jnp.zeros((keys - pad, 3 * d), BF16)
    column = lax.broadcasted_iota(jnp.int32, (1, keys), 1) < seq
    for hp in range(HEADS // 2):
        lanes = slice(LANES * hp, LANES * (hp + 1))
        stacked = split_heads(qkv[0, 0:pad, lanes])
        scores = nt(stacked, qkv[0, :, d + LANES * hp : d + LANES * (hp + 1)])
        scores = jnp.where(column, scores, -1e30)
        raised = jnp.exp(scores - jnp.max(scores, axis=-1, keepdims=True))
        probs = (raised * (1.0 / jnp.sum(raised, axis=-1, keepdims=True))).astype(BF16)
        p[0, hp] = probs
        mixed = nn(probs, qkv[0, :, 2 * d + LANES * hp : 2 * d + LANES * (hp + 1)])
        o[here, lanes] = join_heads(mixed).astype(BF16)
    attn = jnp.where(valid, nn(o[here, :], wfull[:, 3 * d : 4 * d]), 0.0)
    ssq[0:1, :] += jnp.sum(attn * attn, axis=0, keepdims=True)
    after = x + attn
    h1[0] = after
    n2, _ = norm_stats(after)
    a2[here, :] = (n2 * rt[5:6, :]).astype(BF16)


def attn_fwd(idx, tokens, packs, seq, pad, keys, block):
    images, _, d = tokens.shape
    rows = packs[0].shape[0]
    out_shape = (
        jax.ShapeDtypeStruct((d, 4 * d), BF16),
        jax.ShapeDtypeStruct((TAIL, d), F32),
        jax.ShapeDtypeStruct((images, keys, 3 * d), BF16),
        jax.ShapeDtypeStruct((images, HEADS // 2, 2 * pad, keys), BF16),
        jax.ShapeDtypeStruct((block, d), BF16),
        jax.ShapeDtypeStruct((block, d), BF16),
        jax.ShapeDtypeStruct((images, pad, d), F32),
        jax.ShapeDtypeStruct((block, d), BF16),
        jax.ShapeDtypeStruct((8, d), F32),
    )
    return pl.pallas_call(
        functools.partial(attn_fwd_kernel, seq=seq),
        grid=(images,),
        out_shape=out_shape,
        in_specs=[SMEM_SPEC, pl.BlockSpec((1, pad, d), lambda i: (i, 0, 0))]
        + [whole((rows, 4 * d))] * 4,
        out_specs=(
            whole((d, 4 * d)),
            whole((TAIL, d)),
            pl.BlockSpec((1, keys, 3 * d), lambda i: (i, 0, 0)),
            pl.BlockSpec((1, HEADS // 2, 2 * pad, keys), lambda i: (i, 0, 0, 0)),
            whole((block, d)),
            whole((block, d)),
            pl.BlockSpec((1, pad, d), lambda i: (i, 0, 0)),
            whole((block, d)),
            whole((8, d)),
        ),
        compiler_params=params(),
        cost_estimate=cost(images * (8 * pad * d * d + 4 * pad * keys * d * 2), 10e6, 1.3e6),
    )(idx, tokens, *packs)


def expert_fwd_kernel(idx, a2a, a2b, ga, gb, w1t, rt, ma, mb, *rest, first):
    if first:
        zc, cgp, gwo, pr, a2s, gs = rest
    else:
        prev, zc, cgp, gwo, pr, a2s, gs = rest
    block = a2a.shape[0]
    both = 2 * block

    @pl.when(pl.program_id(0) == 0)
    def _():
        a2s[0:block, :] = a2a[...]
        a2s[block:both, :] = a2b[...]
        gs[0:block, :] = ga[...]
        gs[block:both, :] = gb[...]
        row = lax.broadcasted_iota(jnp.int32, (TAIL, both), 0)
        logits = jnp.where(row < 4, nt(rt[...].astype(BF16), a2s[...]), -1e30)
        raised = jnp.exp(logits - jnp.max(logits, axis=0, keepdims=True))
        probs = raised / jnp.sum(raised, axis=0, keepdims=True)
        masks = jnp.concatenate([ma[...], mb[...]], axis=1).astype(F32)
        mine = jnp.sum(jnp.where(row == MASK_ROW + idx[0], masks, 0.0), axis=0, keepdims=True)
        share = jnp.sum(jnp.where(row == idx[0], probs, 0.0), axis=0, keepdims=True)
        pr[...] = jnp.where(row == MASK_ROW, mine * share, probs)

    u = nt(w1t[...], a2s[...])
    act, slope = gelu_pair(u)
    weight = pr[MASK_ROW : MASK_ROW + 1, :]
    zcv = (act * weight).astype(BF16)
    zc[...] = zcv
    cgp[...] = (slope * weight).astype(BF16)
    grad = nn(zcv, gs[...])
    if first:
        gwo[...] = grad
    else:
        gwo[...] = (prev[...] + grad).astype(BF16)


def expert_fwd(idx, a2s, gs, w1t, rt, packs, prev):
    block, d = a2s[0].shape
    f = w1t.shape[0]
    step = 512
    first = prev is None
    rows = packs[0].shape[0] - TAIL
    mask_spec = pl.BlockSpec((TAIL, block), lambda j: (rows // TAIL, 0))
    in_specs = [SMEM_SPEC] + [whole((block, d))] * 4
    in_specs += [pl.BlockSpec((step, d), lambda j: (j, 0)), whole((TAIL, d)), mask_spec, mask_spec]
    operands = [idx, *a2s, *gs, w1t, rt, *packs]
    if not first:
        in_specs.append(pl.BlockSpec((step, d), lambda j: (j, 0)))
        operands.append(prev)
    return pl.pallas_call(
        functools.partial(expert_fwd_kernel, first=first),
        grid=(f // step,),
        out_shape=(
            jax.ShapeDtypeStruct((f, 2 * block), BF16),
            jax.ShapeDtypeStruct((f, 2 * block), BF16),
            jax.ShapeDtypeStruct((f, d), F32 if first else BF16),
            jax.ShapeDtypeStruct((TAIL, 2 * block), F32),
        ),
        in_specs=in_specs,
        out_specs=(
            pl.BlockSpec((step, 2 * block), lambda j: (j, 0)),
            pl.BlockSpec((step, 2 * block), lambda j: (j, 0)),
            pl.BlockSpec((step, d), lambda j: (j, 0)),
            whole((TAIL, 2 * block)),
        ),
        scratch_shapes=[pltpu.VMEM((2 * block, d), BF16), pltpu.VMEM((2 * block, d), BF16)],
        compiler_params=params(),
        cost_estimate=cost(8 * block * d * f, 20e6, 4 * block * f),
    )(*operands)


def expert_bwd_kernel(idx, a2a, a2b, ga, gb, zc, cgp, w2, w1, rt, pr, *rest, first, last):
    if first:
        gwi, da, db, gr, a2s, a2t, gs, total, dcomb = rest
    else:
        prev, gwi, da, db, gr, a2s, a2t, gs, total, dcomb = rest
    block = a2a.shape[0]
    both = 2 * block
    j = pl.program_id(0)

    @pl.when(j == 0)
    def _():
        a2s[0:block, :] = a2a[...]
        a2s[block:both, :] = a2b[...]
        a2t[...] = a2s[...].T
        gs[0:block, :] = ga[...]
        gs[block:both, :] = gb[...]
        total[...] = jnp.zeros(total.shape, F32)
        dcomb[...] = jnp.zeros(dcomb.shape, F32)

    dz = nt(w2[...], gs[...])
    dcomb[0:1, :] += jnp.sum(zc[...].astype(F32) * dz, axis=0, keepdims=True)
    du = (cgp[...].astype(F32) * dz).astype(BF16)
    grad = nt(a2t[...], du)
    if first:
        gwi[...] = grad
    else:
        gwi[...] = (prev[...] + grad).astype(BF16)
    total[...] += nn(w1[...], du)

    @pl.when(j == pl.num_programs(0) - 1)
    def _():
        row = lax.broadcasted_iota(jnp.int32, (TAIL, both), 0)
        own = (row == idx[0]).astype(F32)
        dlogits = jnp.where(row < 4, dcomb[0:1, :] * (own - pr[...]), 0.0).astype(BF16)
        gr[...] = nn(dlogits, a2s[...])
        result = (total[...] + tn(rt[...].astype(BF16), dlogits)).astype(BF16)
        da[...] = result[:, 0:block]
        db[...] = result[:, block:both]


def expert_bwd(idx, a2s, gs, zc, cgp, w2, w1, rt, pr, prev):
    block, d = a2s[0].shape
    f = w2.shape[0]
    step = 512
    first = prev is None
    in_specs = [SMEM_SPEC] + [whole((block, d))] * 4
    in_specs += [pl.BlockSpec((step, 2 * block), lambda j: (j, 0))] * 2
    in_specs += [
        pl.BlockSpec((step, d), lambda j: (j, 0)),
        pl.BlockSpec((d, step), lambda j: (0, j)),
        whole((TAIL, d)),
        whole((TAIL, 2 * block)),
    ]
    operands = [idx, *a2s, *gs, zc, cgp, w2, w1, rt, pr]
    if not first:
        in_specs.append(pl.BlockSpec((d, step), lambda j: (0, j)))
        operands.append(prev)
    return pl.pallas_call(
        functools.partial(expert_bwd_kernel, first=first, last=not first),
        grid=(f // step,),
        out_shape=(
            jax.ShapeDtypeStruct((d, f), F32 if first else BF16),
            jax.ShapeDtypeStruct((d, block), BF16),
            jax.ShapeDtypeStruct((d, block), BF16),
            jax.ShapeDtypeStruct((TAIL, d), F32),
        ),
        in_specs=in_specs,
        out_specs=(
            pl.BlockSpec((d, step), lambda j: (0, j)),
            whole((d, block)),
            whole((d, block)),
            whole((TAIL, d)),
        ),
        scratch_shapes=[
            pltpu.VMEM((2 * block, d), BF16),
            pltpu.VMEM((d, 2 * block), BF16),
            pltpu.VMEM((2 * block, d), BF16),
            pltpu.VMEM((d, 2 * block), F32),
            pltpu.VMEM((8, 2 * block), F32),
        ],
        compiler_params=params(),
        cost_estimate=cost(12 * block * d * f, 20e6),
    )(*operands)


def expert_out_kernel(w2t, zc, y):
    y[...] = nn(w2t[...], zc[...]).astype(BF16)


def expert_out(w2t, zc, part):
    d, f = w2t.shape
    block = zc.shape[1] // 2
    return pl.pallas_call(
        expert_out_kernel,
        grid=(1,),
        out_shape=jax.ShapeDtypeStruct((d, block), BF16),
        in_specs=[whole((d, f)), pl.BlockSpec((f, block), lambda i: (0, part))],
        out_specs=whole((d, block)),
        compiler_params=params(),
        cost_estimate=cost(2 * d * f * block, 5e6),
    )(w2t, zc)


def attn_bwd_kernel(
    idx, tok, g, da0, da1, da2, h1, qkv, p, o, a1, wfull, rt, gra, grb,
    gtok, pack_send, pack_keep,
    da, dattn_all, dqkv, gains, grads, *, seq,
):
    i = pl.program_id(0)
    pad, d = tok.shape[1], tok.shape[2]
    rows = d // 4

    @pl.when(i == 0)
    def _():
        summed = da0[...].astype(F32) + da1[...].astype(F32) + da2[...].astype(F32)
        da[...] = summed.T
        dattn_all[...] = jnp.zeros(dattn_all.shape, BF16)
        dqkv[...] = jnp.zeros(dqkv.shape, BF16)
        gains[...] = jnp.zeros(gains.shape, F32)

    here = pl.ds(pl.multiple_of(i * pad, TAIL), pad)
    valid = lax.broadcasted_iota(jnp.int32, (pad, 1), 0) < seq
    n2, r2 = norm_stats(h1[0])
    din = da[here, :]
    gains[1:2, :] += jnp.sum(din * n2, axis=0, keepdims=True)
    dh1 = g[here, :].astype(F32) + norm_back(din * rt[5:6, :], n2, r2)
    dattn = dh1.astype(BF16)
    dattn_all[here, :] = dattn
    do = nt(dattn, wfull[:, 3 * d : 4 * d]).astype(BF16)
    for hp in range(HEADS // 2):
        lanes = slice(LANES * hp, LANES * (hp + 1))
        klanes = slice(d + LANES * hp, d + LANES * (hp + 1))
        vlanes = slice(2 * d + LANES * hp, 2 * d + LANES * (hp + 1))
        do2 = split_heads(do[:, lanes])
        dp = nt(do2, qkv[0, :, vlanes])
        probs = p[0, hp]
        wide = probs.astype(F32)
        ds = (wide * (dp - jnp.sum(dp * wide, axis=-1, keepdims=True))).astype(BF16)
        dqkv[here, vlanes] = tn(probs, do2)[0:pad].astype(BF16)
        dq = join_heads(nn(ds, qkv[0, :, klanes]))
        dqkv[here, lanes] = (dq * HEAD_DIM**-0.5).astype(BF16)
        dqkv[here, klanes] = tn(ds, split_heads(qkv[0, 0:pad, lanes]))[0:pad].astype(BF16)
    din1 = nt(dqkv[here, :], wfull[:, 0 : 3 * d])
    x = jnp.where(valid, tok[0].astype(F32), 0.0)
    n1, r1 = norm_stats(x)
    gains[0:1, :] += jnp.sum(din1 * n1, axis=0, keepdims=True)
    gtok[0] = (dh1 + norm_back(din1 * rt[4:5, :], n1, r1)).astype(BF16)

    @pl.when(i == pl.num_programs(0) - 1)
    def _():
        grads[:, 0 : 3 * d] = tn(a1[...], dqkv[...]).astype(BF16)
        grads[:, 3 * d : 4 * d] = tn(o[...], dattn_all[...]).astype(BF16)
        row = lax.broadcasted_iota(jnp.int32, (TAIL, d), 0)
        tail = jnp.where(row < 4, gra[...] + grb[...], 0.0)
        tail = jnp.where(row == 4, gains[0:1, :], tail)
        gains[...] = jnp.where(row == 5, gains[1:2, :], tail)
        for n, (ref, slot) in enumerate(
            ((pack_keep, 0), (pack_send, 0), (pack_keep, 1), (pack_send, 1))
        ):
            at = pl.multiple_of(idx[n] * rows, rows)
            ref[slot, 0:rows, :] = grads[pl.ds(at, rows), :]
            ref[slot, rows : rows + TAIL, :] = jnp.zeros((TAIL, 4 * d), BF16)
            ref[slot, rows : rows + TAIL, 0:rows] = gains[:, pl.ds(at, rows)].astype(BF16)


def attn_bwd(idx, tokens, g, das, h1, qkv, p, o, a1, wfull, rt, grs, seq, pad):
    images, _, d = tokens.shape
    block = g.shape[0]
    keys = qkv.shape[1]
    rows = d // 4 + TAIL
    image = lambda i: (i, 0, 0)
    return pl.pallas_call(
        functools.partial(attn_bwd_kernel, seq=seq),
        grid=(images,),
        out_shape=(
            jax.ShapeDtypeStruct(tokens.shape, BF16),
            jax.ShapeDtypeStruct((2, rows, 4 * d), BF16),
            jax.ShapeDtypeStruct((2, rows, 4 * d), BF16),
        ),
        in_specs=[SMEM_SPEC, pl.BlockSpec((1, pad, d), image), whole((block, d))]
        + [whole((d, block))] * 3
        + [
            pl.BlockSpec((1, pad, d), image),
            pl.BlockSpec((1, keys, 3 * d), image),
            pl.BlockSpec((1, HEADS // 2, 2 * pad, keys), lambda i: (i, 0, 0, 0)),
            whole((block, d)),
            whole((block, d)),
            whole((d, 4 * d)),
            whole((TAIL, d)),
            whole((TAIL, d)),
            whole((TAIL, d)),
        ],
        out_specs=(
            pl.BlockSpec((1, pad, d), image),
            whole((2, rows, 4 * d)),
            whole((2, rows, 4 * d)),
        ),
        scratch_shapes=[
            pltpu.VMEM((block, d), F32),
            pltpu.VMEM((block, d), BF16),
            pltpu.VMEM((block, 3 * d), BF16),
            pltpu.VMEM((TAIL, d), F32),
            pltpu.VMEM((d, 4 * d), BF16),
        ],
        compiler_params=params(),
        cost_estimate=cost(images * (16 * pad * d * d + 8 * pad * keys * d * 2), 15e6),
    )(idx, tokens, g, *das, h1, qkv, p, o, a1, wfull, rt, *grs)


def output_kernel(h1, y0, y1, y2, out, sums, moe):
    i = pl.program_id(0)
    pad = h1.shape[1]

    @pl.when(i == 0)
    def _():
        moe[...] = (y0[...].astype(F32) + y1[...].astype(F32) + y2[...].astype(F32)).T
        sums[...] = jnp.zeros(sums.shape, F32)

    branch = moe[pl.ds(pl.multiple_of(i * pad, TAIL), pad), :]
    result = h1[0] + branch
    sums[0:1, :] += jnp.sum(result * result, axis=0, keepdims=True)
    sums[1:2, :] += jnp.sum(branch * branch, axis=0, keepdims=True)
    out[0] = result.astype(BF16)


def output(h1, ys, seq):
    images, pad, d = h1.shape
    block = ys[0].shape[1]
    return pl.pallas_call(
        output_kernel,
        grid=(images,),
        out_shape=(
            jax.ShapeDtypeStruct((images, seq, d), BF16),
            jax.ShapeDtypeStruct((8, d), F32),
        ),
        in_specs=[pl.BlockSpec((1, pad, d), lambda i: (i, 0, 0))] + [whole((d, block))] * 3,
        out_specs=(pl.BlockSpec((1, pad, d), lambda i: (i, 0, 0)), whole((8, d))),
        scratch_shapes=[pltpu.VMEM((block, d), F32)],
        compiler_params=params(),
        cost_estimate=cost(10 * block * d, 5e6),
    )(h1, *ys)


def local(
    tokens,
    cotangent,
    gain_one,
    w_query,
    w_key,
    w_value,
    w_output,
    gain_two,
    w_router,
    w_in,
    w_out,
    routes,
):
    images, seq, d = tokens.shape
    experts = lax.axis_size("shard")
    pad = round_up(seq, TAIL)
    keys = round_up(seq, LANES)
    block = round_up(images * pad, LANES)
    rows = w_query.shape[0]
    me = lax.axis_index("shard")
    idx = jnp.stack([me, me ^ 1, me ^ 2, me ^ 3]).astype(jnp.int32)
    core = lambda a: lax.ppermute(a, "shard", [(s, s ^ 1) for s in range(experts)])
    chip = lambda a: lax.ppermute(a, "shard", [(s, s ^ 2) for s in range(experts)])

    chosen = (routes[:, :, :, None] == jnp.arange(experts, dtype=jnp.int32)).any(axis=2)
    chosen = jnp.pad(chosen.astype(F32), ((0, 0), (0, pad - seq), (0, 0)))
    chosen = chosen.reshape(images * pad, experts).T
    masks = jnp.pad(
        chosen, ((MASK_ROW, TAIL - MASK_ROW - experts), (0, block - images * pad))
    )
    wp, gp = pl.pallas_call(
        functools.partial(pack_kernel, seq=seq, pad=pad),
        out_shape=(
            jax.ShapeDtypeStruct((rows + TAIL, 4 * d), BF16),
            jax.ShapeDtypeStruct((block, d), BF16),
        ),
        compiler_params=params(),
        cost_estimate=cost(1e6, 3e6),
    )(
        w_query, w_key, w_value, w_output,
        gain_one.reshape(1, rows), gain_two.reshape(1, rows), w_router, masks, cotangent,
    )
    wx = chip(wp)
    gx = chip(gp)
    packs = (wp, core(wp), wx, core(wx))
    gs = (gp, core(gp), gx, core(gx))
    w1, w2 = w_in[0], w_out[0]
    w1t, w2t = pl.pallas_call(
        turn_kernel,
        out_shape=(
            jax.ShapeDtypeStruct(w1.shape[::-1], BF16),
            jax.ShapeDtypeStruct(w2.shape[::-1], BF16),
        ),
        compiler_params=params(),
        cost_estimate=cost(1e6, 8e6),
    )(w1, w2)
    wfull, rt, qkv, p, o, a1, h1, a2, ssq_attn = attn_fwd(
        idx, tokens, packs, seq, pad, keys, block
    )
    ax = chip(a2)
    near, far = (a2, core(a2)), (ax, core(ax))

    zc1, cgp1, gwo1, pr1 = expert_fwd(idx, near, gs[:2], w1t, rt, packs[:2], None)
    zc2, cgp2, gwo, pr2 = expert_fwd(idx, far, gs[2:], w1t, rt, packs[2:], gwo1)
    gwo = lax.psum(gwo, "rep")
    gwi2, dax, daxc, gr2 = expert_bwd(idx, far, gs[2:], zc2, cgp2, w2, w1, rt, pr2, None)
    gwi, da, dac, gr1 = expert_bwd(idx, near, gs[:2], zc1, cgp1, w2, w1, rt, pr1, gwi2)
    gwi = lax.psum(gwi, "rep")
    da_core = core(dac)
    da_chip = chip(dax + core(daxc))
    yx, yxc = expert_out(w2t, zc2, 0), expert_out(w2t, zc2, 1)
    y, yc = expert_out(w2t, zc1, 0), expert_out(w2t, zc1, 1)
    y_core = core(yc)
    y_chip = chip(yx + core(yxc))
    grad_tokens, send, keep = attn_bwd(
        idx, tokens, gp, (da, da_core, da_chip), h1, qkv, p, o, a1, wfull, rt, (gr1, gr2), seq, pad
    )
    out, sums = output(h1, (y, y_core, y_chip), seq)
    got = core(send)
    pack = keep[0] + got[0] + chip(keep[1] + got[1])
    pack = lax.psum(pack, "rep").astype(F32)
    local_sums = jnp.stack([jnp.sum(sums[0]), jnp.sum(ssq_attn[0]), jnp.sum(sums[1])])
    total_sums = lax.psum(local_sums, ("shard", "rep"))
    count_all = float(lax.axis_size("shard") * lax.axis_size("rep") * images * seq * d)
    roots = jnp.sqrt(total_sums / count_all)
    return (
        out,
        grad_tokens,
        pack[rows + 4, 0:rows],
        pack[0:rows, 0:d],
        pack[0:rows, d : 2 * d],
        pack[0:rows, 2 * d : 3 * d],
        pack[0:rows, 3 * d : 4 * d],
        pack[rows + 5, 0:rows],
        pack[rows : rows + experts, 0:rows].T,
        gwi.astype(F32)[None],
        gwo.astype(F32)[None],
        roots[0],
        roots[1],
        roots[2],
    )


def solution(mesh):
    spread = P(("shard", "rep"), None, None)
    matrix = P("shard", None)
    stack = P("shard", None, None)
    vector = P("shard")
    return jax.shard_map(
        local,
        mesh=mesh,
        in_specs=(
            spread, spread, vector, matrix, matrix, matrix, matrix, vector, matrix, stack, stack, spread,
        ),
        out_specs=(
            spread, spread, vector, matrix, matrix, matrix, matrix, vector, matrix, stack, stack, P(), P(), P(),
        ),
        check_vma=False,
    )
```

```python
import functools

import jax
import jax.numpy as jnp
from jax import lax
from jax.experimental import pallas as pl
from jax.experimental.pallas import tpu as pltpu
from jax.sharding import PartitionSpec as P

HEADS = 8
HEAD_DIM = 64
EPSILON = 1e-06
LANES = 128
TAIL = 16
MASK_ROW = 8
VMEM_LIMIT = 60 * 1024 * 1024

BF16 = jnp.bfloat16
F32 = jnp.float32

LOG2E = 1.4426950408889634
ROOT_HALF = 0.7071067811865476
INV_ROOT_2PI = 0.3989422804014327


def round_up(value, multiple):
    return (value + multiple - 1) // multiple * multiple


def nn(a, b):
    return lax.dot_general(a, b, (((1,), (0,)), ((), ())), preferred_element_type=F32)


def nt(a, b):
    return lax.dot_general(a, b, (((1,), (1,)), ((), ())), preferred_element_type=F32)


def tn(a, b):
    return lax.dot_general(a, b, (((0,), (0,)), ((), ())), preferred_element_type=F32)


def norm_stats(values):
    center = values - jnp.mean(values, axis=-1, keepdims=True)
    inverse = lax.rsqrt(jnp.mean(center * center, axis=-1, keepdims=True) + EPSILON)
    return center * inverse, inverse


def norm_back(grad_normed, normed, inverse):
    mean_plain = jnp.mean(grad_normed, axis=-1, keepdims=True)
    mean_cross = jnp.mean(grad_normed * normed, axis=-1, keepdims=True)
    return inverse * (grad_normed - mean_plain - normed * mean_cross)


def gelu_pair(u):
    cdf = 0.5 * lax.erf(u * ROOT_HALF) + 0.5
    return u * cdf, cdf + u * (jnp.exp2(u * u * (-0.5 * LOG2E)) * INV_ROOT_2PI)


def split_heads(pair):
    low = lax.broadcasted_iota(jnp.int32, pair.shape, 1) < HEAD_DIM
    zero = jnp.zeros_like(pair)
    return jnp.concatenate([jnp.where(low, pair, zero), jnp.where(low, zero, pair)], axis=0)


def join_heads(stacked):
    rows = stacked.shape[0] // 2
    low = lax.broadcasted_iota(jnp.int32, (rows, stacked.shape[1]), 1) < HEAD_DIM
    return jnp.where(low, stacked[:rows], stacked[rows:])


def after(value, *first):
    return lax.optimization_barrier((value, *first))[0]


def params():
    return pltpu.CompilerParams(vmem_limit_bytes=VMEM_LIMIT)


def cost(flops, nbytes, trans=0):
    return pl.CostEstimate(flops=int(flops), bytes_accessed=int(nbytes), transcendentals=int(trans))


def whole(shape):
    return pl.BlockSpec(shape, lambda *_: (0,) * len(shape))


SMEM_SPEC = pl.BlockSpec(memory_space=pltpu.SMEM)


def pack_kernel(wq, wk, wv, wo, g1, g2, wr, masks, cot, wp, gp, *, seq, pad):
    d = wq.shape[1]
    rows = wq.shape[0]
    for n, w in enumerate((wq, wk, wv, wo)):
        wp[0:rows, n * d : (n + 1) * d] = w[...]
    router = jnp.concatenate(
        [wr[...].astype(F32), jnp.zeros((TAIL - wr.shape[0], LANES), F32)], axis=0
    )
    row = lax.broadcasted_iota(jnp.int32, (TAIL, LANES), 0)
    head = jnp.where(row == 4, g1[...].astype(F32), router)
    head = jnp.where(row == 5, g2[...].astype(F32), head)
    wp[rows : rows + TAIL, :] = jnp.zeros((TAIL, wp.shape[1]), BF16)
    tokens = masks.shape[1]
    wp[rows : rows + TAIL, 0:tokens] = masks[...].astype(BF16)
    wp[rows : rows + TAIL, 0:LANES] = (head + masks[:, 0:LANES]).astype(BF16)
    gp[...] = jnp.zeros(gp.shape, BF16)
    for i in range(cot.shape[0]):
        gp[i * pad : i * pad + seq, :] = cot[i]


def attn_fwd_kernel(idx, tok, w0, w1, w2, w3, wfull, rt, qkv, p, o, a1, h1, a2, ssq, *, seq):
    i = pl.program_id(0)
    pad, d = tok.shape[1], tok.shape[2]
    keys = qkv.shape[1]
    rows = w0.shape[0] - TAIL

    @pl.when(i == 0)
    def _():
        for n, w in enumerate((w0, w1, w2, w3)):
            at = pl.multiple_of(idx[n] * rows, rows)
            wfull[pl.ds(at, rows), :] = w[0:rows, :]
            rt[:, pl.ds(at, rows)] = w[rows : rows + TAIL, 0:rows].astype(F32)
        for ref in (o, a1, a2):
            ref[...] = jnp.zeros(ref.shape, ref.dtype)
        ssq[...] = jnp.zeros(ssq.shape, F32)

    here = pl.ds(pl.multiple_of(i * pad, TAIL), pad)
    valid = lax.broadcasted_iota(jnp.int32, (pad, 1), 0) < seq
    x = jnp.where(valid, tok[0].astype(F32), 0.0)
    n1, _ = norm_stats(x)
    in_one = (n1 * rt[4:5, :]).astype(BF16)
    a1[here, :] = in_one
    proj = nn(in_one, wfull[:, 0 : 3 * d])
    qkv[0, 0:pad, 0:d] = (proj[:, 0:d].astype(BF16).astype(F32) * HEAD_DIM**-0.5).astype(BF16)
    qkv[0, 0:pad, d:] = proj[:, d:].astype(BF16)
    qkv[0, pad:keys, :] = jnp.zeros((keys - pad, 3 * d), BF16)
    column = lax.broadcasted_iota(jnp.int32, (1, keys), 1) < seq
    for hp in range(HEADS // 2):
        lanes = slice(LANES * hp, LANES * (hp + 1))
        stacked = split_heads(qkv[0, 0:pad, lanes])
        scores = nt(stacked, qkv[0, :, d + LANES * hp : d + LANES * (hp + 1)])
        scores = jnp.where(column, scores, -1e30)
        raised = jnp.exp(scores - jnp.max(scores, axis=-1, keepdims=True))
        probs = (raised * (1.0 / jnp.sum(raised, axis=-1, keepdims=True))).astype(BF16)
        p[0, hp] = probs
        mixed = nn(probs, qkv[0, :, 2 * d + LANES * hp : 2 * d + LANES * (hp + 1)])
        o[here, lanes] = join_heads(mixed).astype(BF16)
    attn = jnp.where(valid, nn(o[here, :], wfull[:, 3 * d : 4 * d]), 0.0)
    ssq[0:1, :] += jnp.sum(attn * attn, axis=0, keepdims=True)
    after = x + attn
    h1[0] = after
    n2, _ = norm_stats(after)
    a2[here, :] = (n2 * rt[5:6, :]).astype(BF16)


def attn_fwd(idx, tokens, packs, seq, pad, keys, block):
    images, _, d = tokens.shape
    rows = packs[0].shape[0]
    out_shape = (
        jax.ShapeDtypeStruct((d, 4 * d), BF16),
        jax.ShapeDtypeStruct((TAIL, d), F32),
        jax.ShapeDtypeStruct((images, keys, 3 * d), BF16),
        jax.ShapeDtypeStruct((images, HEADS // 2, 2 * pad, keys), BF16),
        jax.ShapeDtypeStruct((block, d), BF16),
        jax.ShapeDtypeStruct((block, d), BF16),
        jax.ShapeDtypeStruct((images, pad, d), F32),
        jax.ShapeDtypeStruct((block, d), BF16),
        jax.ShapeDtypeStruct((8, d), F32),
    )
    return pl.pallas_call(
        functools.partial(attn_fwd_kernel, seq=seq),
        grid=(images,),
        out_shape=out_shape,
        in_specs=[SMEM_SPEC, pl.BlockSpec((1, pad, d), lambda i: (i, 0, 0))]
        + [whole((rows, 4 * d))] * 4,
        out_specs=(
            whole((d, 4 * d)),
            whole((TAIL, d)),
            pl.BlockSpec((1, keys, 3 * d), lambda i: (i, 0, 0)),
            pl.BlockSpec((1, HEADS // 2, 2 * pad, keys), lambda i: (i, 0, 0, 0)),
            whole((block, d)),
            whole((block, d)),
            pl.BlockSpec((1, pad, d), lambda i: (i, 0, 0)),
            whole((block, d)),
            whole((8, d)),
        ),
        compiler_params=params(),
        cost_estimate=cost(images * (8 * pad * d * d + 4 * pad * keys * d * 2), 10e6, 1.3e6),
    )(idx, tokens, *packs)


def route(idx, a2s, rt, ma, mb):
    both = a2s.shape[0]
    row = lax.broadcasted_iota(jnp.int32, (TAIL, both), 0)
    logits = jnp.where(row < 4, nt(rt[...].astype(BF16), a2s[...]), -1e30)
    raised = jnp.exp(logits - jnp.max(logits, axis=0, keepdims=True))
    share = raised / jnp.sum(raised, axis=0, keepdims=True)
    masks = jnp.concatenate([ma[...], mb[...]], axis=1).astype(F32)
    chosen = jnp.sum(jnp.where(row == MASK_ROW + idx[0], masks, 0.0), axis=0, keepdims=True)
    mine = jnp.sum(jnp.where(row == idx[0], share, 0.0), axis=0, keepdims=True)
    return jnp.where(row == MASK_ROW, chosen * mine, share).T


def fold_lanes(wide):
    parts = [wide[:, n : n + LANES] for n in range(0, wide.shape[1], LANES)]
    return sum(parts[1:], parts[0])


def gather_rows(a2a, a2b, ga, gb, a2s, gs):
    block = a2a.shape[0]
    a2s[0:block, :] = a2a[...]
    a2s[block:, :] = a2b[...]
    gs[0:block, :] = ga[...]
    gs[block:, :] = gb[...]


def finish_rows(idx, probs, dcomb, total, a2s, rt, da, db, gr):
    block = da.shape[0]
    lane = lax.broadcasted_iota(jnp.int32, (2 * block, TAIL), 1)
    own = (lane == idx[0]).astype(F32)
    inner = jnp.sum(dcomb[...], axis=1, keepdims=True)
    dlogits = jnp.where(lane < 4, inner * (own - probs[...]), 0.0).astype(BF16)
    gr[...] = tn(dlogits, a2s[...])
    result = (total[...] + nn(dlogits, rt[...].astype(BF16))).astype(BF16)
    da[...] = result[0:block]
    db[...] = result[block:]


def expert_kernel(
    idx, a2a, a2b, ga, gb, w1, w2, rt, ma, mb,
    zc, du, da, db, gr, a2s, gs, probs, dcomb, total,
):
    j = pl.program_id(0)

    @pl.when(j == 0)
    def _():
        gather_rows(a2a, a2b, ga, gb, a2s, gs)
        probs[...] = route(idx, a2s, rt, ma, mb)
        total[...] = jnp.zeros(total.shape, F32)
        dcomb[...] = jnp.zeros(dcomb.shape, F32)

    act, slope = gelu_pair(nn(a2s[...], w1[...]))
    scale = probs[:, MASK_ROW : MASK_ROW + 1]
    mixed = (act * scale).astype(BF16)
    zc[...] = mixed
    dz = nt(gs[...], w2[...])
    dcomb[...] += fold_lanes(mixed.astype(F32) * dz)
    grad = (slope * scale * dz).astype(BF16)
    du[...] = grad
    total[...] += nt(grad, w1[...])

    @pl.when(j == pl.num_programs(0) - 1)
    def _():
        finish_rows(idx, probs, dcomb, total, a2s, rt, da, db, gr)


def expert_specs(block, d, f, rows):
    step = f // 4
    columns = pl.BlockSpec((2 * block, step), lambda j: (0, j))
    w1 = pl.BlockSpec((d, step), lambda j: (0, j))
    w2 = pl.BlockSpec((step, d), lambda j: (j, 0))
    masks = pl.BlockSpec((TAIL, block), lambda j: (rows // TAIL, 0))
    return columns, w1, w2, masks


def expert(idx, a2s, gs, w1, w2, rt, packs):
    block, d = a2s[0].shape
    f = w1.shape[1]
    both = 2 * block
    columns, w1_spec, w2_spec, masks = expert_specs(block, d, f, packs[0].shape[0] - TAIL)
    return pl.pallas_call(
        expert_kernel,
        grid=(4,),
        out_shape=(
            jax.ShapeDtypeStruct((both, f), BF16),
            jax.ShapeDtypeStruct((both, f), BF16),
            jax.ShapeDtypeStruct((block, d), BF16),
            jax.ShapeDtypeStruct((block, d), BF16),
            jax.ShapeDtypeStruct((TAIL, d), F32),
            jax.ShapeDtypeStruct((both, d), BF16),
            jax.ShapeDtypeStruct((both, d), BF16),
        ),
        in_specs=[SMEM_SPEC]
        + [whole((block, d))] * 4
        + [w1_spec, w2_spec, whole((TAIL, d)), masks, masks],
        out_specs=(columns, columns)
        + (whole((block, d)),) * 2
        + (whole((TAIL, d)),)
        + (whole((both, d)),) * 2,
        scratch_shapes=[
            pltpu.VMEM((both, TAIL), F32),
            pltpu.VMEM((both, LANES), F32),
            pltpu.VMEM((both, d), F32),
        ],
        compiler_params=params(),
        cost_estimate=cost(6 * both * d * f, 25e6, 2 * both * f),
    )(idx, *a2s, *gs, w1, w2, rt, *packs)


def grads_kernel(zn, zf, gn, gf, an, af, dn, df, out):
    j = pl.program_id(0)

    @pl.when(j < 4)
    def _():
        out[...] = (tn(zn[...], gn[...]) + tn(zf[...], gf[...])).astype(BF16)

    @pl.when(j >= 4)
    def _():
        out[...] = (tn(an[...], dn[...]) + tn(af[...], df[...])).astype(BF16)


def expert_grads(zn, zf, gn, gf, an, af, dn, df):
    both, f = zn.shape
    d = gn.shape[1]
    step = f // 4
    early = pl.BlockSpec((both, step), lambda j: (0, jnp.minimum(j, 3)))
    late = pl.BlockSpec((both, step), lambda j: (0, jnp.maximum(j - 4, 0)))
    flat = pl.BlockSpec((both, d), lambda j: (0, 0))
    return pl.pallas_call(
        grads_kernel,
        grid=(8,),
        out_shape=jax.ShapeDtypeStruct((2 * f, d), BF16),
        in_specs=[early] * 2 + [flat] * 4 + [late] * 2,
        out_specs=pl.BlockSpec((step, d), lambda j: (j, 0)),
        compiler_params=params(),
        cost_estimate=cost(8 * both * d * f, 25e6),
    )(zn, zf, gn, gf, an, af, dn, df)


def place_kernel(grads, gwo, gwi):
    j = pl.program_id(0)

    @pl.when(j < 4)
    def _():
        gwo[0] = grads[...].astype(F32)

    @pl.when(j >= 4)
    def _():
        gwi[0] = grads[...].astype(F32)


def place(grads):
    rows, d = grads.shape
    f = rows // 2
    step = f // 4
    return pl.pallas_call(
        place_kernel,
        grid=(8,),
        out_shape=(
            jax.ShapeDtypeStruct((1, f, d), F32),
            jax.ShapeDtypeStruct((1, d, f), F32),
        ),
        in_specs=[pl.BlockSpec((step, d), lambda j: (j, 0))],
        out_specs=(
            pl.BlockSpec((1, step, d), lambda j: (0, jnp.minimum(j, 3), 0)),
            pl.BlockSpec((1, d, step), lambda j: (0, 0, jnp.maximum(j - 4, 0))),
        ),
        compiler_params=params(),
        cost_estimate=cost(1e6, 12e6),
    )(grads)


def expert_out_kernel(zc, w2, ya, yb, total):
    j = pl.program_id(0)
    part = nn(zc[...], w2[...])

    @pl.when(j == 0)
    def _():
        total[...] = part

    @pl.when(j > 0)
    def _():
        total[...] += part

    @pl.when(j == pl.num_programs(0) - 1)
    def _():
        block = ya.shape[0]
        ya[...] = total[0:block, :].astype(BF16)
        yb[...] = total[block:, :].astype(BF16)


def expert_out(zc, w2):
    both, f = zc.shape
    d = w2.shape[1]
    step = f // 4
    return pl.pallas_call(
        expert_out_kernel,
        grid=(4,),
        out_shape=[jax.ShapeDtypeStruct((both // 2, d), BF16)] * 2,
        in_specs=[
            pl.BlockSpec((both, step), lambda j: (0, j)),
            pl.BlockSpec((step, d), lambda j: (j, 0)),
        ],
        out_specs=[whole((both // 2, d))] * 2,
        scratch_shapes=[pltpu.VMEM((both, d), F32)],
        compiler_params=params(),
        cost_estimate=cost(2 * d * f * both, 8e6),
    )(zc, w2)


def attn_bwd_kernel(
    idx, tok, g, da0, da1, da2, h1, qkv, p, o, a1, wfull, rt, gra, grb,
    gtok, pack_send, pack_keep,
    da, dattn_all, dqkv, gains, grads, *, seq,
):
    i = pl.program_id(0)
    pad, d = tok.shape[1], tok.shape[2]
    rows = d // 4

    @pl.when(i == 0)
    def _():
        da[...] = da0[...].astype(F32) + da1[...].astype(F32) + da2[...].astype(F32)
        dattn_all[...] = jnp.zeros(dattn_all.shape, BF16)
        dqkv[...] = jnp.zeros(dqkv.shape, BF16)
        gains[...] = jnp.zeros(gains.shape, F32)

    here = pl.ds(pl.multiple_of(i * pad, TAIL), pad)
    valid = lax.broadcasted_iota(jnp.int32, (pad, 1), 0) < seq
    n2, r2 = norm_stats(h1[0])
    din = da[here, :]
    gains[1:2, :] += jnp.sum(din * n2, axis=0, keepdims=True)
    dh1 = g[here, :].astype(F32) + norm_back(din * rt[5:6, :], n2, r2)
    dattn = dh1.astype(BF16)
    dattn_all[here, :] = dattn
    do = nt(dattn, wfull[:, 3 * d : 4 * d]).astype(BF16)
    for hp in range(HEADS // 2):
        lanes = slice(LANES * hp, LANES * (hp + 1))
        klanes = slice(d + LANES * hp, d + LANES * (hp + 1))
        vlanes = slice(2 * d + LANES * hp, 2 * d + LANES * (hp + 1))
        do2 = split_heads(do[:, lanes])
        dp = nt(do2, qkv[0, :, vlanes])
        probs = p[0, hp]
        wide = probs.astype(F32)
        ds = (wide * (dp - jnp.sum(dp * wide, axis=-1, keepdims=True))).astype(BF16)
        dqkv[here, vlanes] = tn(probs, do2)[0:pad].astype(BF16)
        dq = join_heads(nn(ds, qkv[0, :, klanes]))
        dqkv[here, lanes] = (dq * HEAD_DIM**-0.5).astype(BF16)
        dqkv[here, klanes] = tn(ds, split_heads(qkv[0, 0:pad, lanes]))[0:pad].astype(BF16)
    din1 = nt(dqkv[here, :], wfull[:, 0 : 3 * d])
    x = jnp.where(valid, tok[0].astype(F32), 0.0)
    n1, r1 = norm_stats(x)
    gains[0:1, :] += jnp.sum(din1 * n1, axis=0, keepdims=True)
    gtok[0] = (dh1 + norm_back(din1 * rt[4:5, :], n1, r1)).astype(BF16)

    @pl.when(i == pl.num_programs(0) - 1)
    def _():
        grads[:, 0 : 3 * d] = tn(a1[...], dqkv[...]).astype(BF16)
        grads[:, 3 * d : 4 * d] = tn(o[...], dattn_all[...]).astype(BF16)
        row = lax.broadcasted_iota(jnp.int32, (TAIL, d), 0)
        tail = jnp.where(row < 4, gra[...] + grb[...], 0.0)
        tail = jnp.where(row == 4, gains[0:1, :], tail)
        gains[...] = jnp.where(row == 5, gains[1:2, :], tail)
        for n, (ref, slot) in enumerate(
            ((pack_keep, 0), (pack_send, 0), (pack_keep, 1), (pack_send, 1))
        ):
            at = pl.multiple_of(idx[n] * rows, rows)
            ref[slot, :, 0 : 4 * d] = grads[pl.ds(at, rows), :]
            ref[slot, :, 4 * d :] = jnp.zeros((rows, LANES), BF16)
            ref[slot, 0:TAIL, 4 * d :] = gains[:, pl.ds(at, rows)].astype(BF16)


def attn_bwd(idx, tokens, g, das, h1, qkv, p, o, a1, wfull, rt, grs, seq, pad):
    images, _, d = tokens.shape
    block = g.shape[0]
    keys = qkv.shape[1]
    rows = d // 4
    image = lambda i: (i, 0, 0)
    return pl.pallas_call(
        functools.partial(attn_bwd_kernel, seq=seq),
        grid=(images,),
        out_shape=(
            jax.ShapeDtypeStruct(tokens.shape, BF16),
            jax.ShapeDtypeStruct((2, rows, 4 * d + LANES), BF16),
            jax.ShapeDtypeStruct((2, rows, 4 * d + LANES), BF16),
        ),
        in_specs=[SMEM_SPEC, pl.BlockSpec((1, pad, d), image), whole((block, d))]
        + [whole((block, d))] * 3
        + [
            pl.BlockSpec((1, pad, d), image),
            pl.BlockSpec((1, keys, 3 * d), image),
            pl.BlockSpec((1, HEADS // 2, 2 * pad, keys), lambda i: (i, 0, 0, 0)),
            whole((block, d)),
            whole((block, d)),
            whole((d, 4 * d)),
            whole((TAIL, d)),
            whole((TAIL, d)),
            whole((TAIL, d)),
        ],
        out_specs=(
            pl.BlockSpec((1, pad, d), image),
            whole((2, rows, 4 * d + LANES)),
            whole((2, rows, 4 * d + LANES)),
        ),
        scratch_shapes=[
            pltpu.VMEM((block, d), F32),
            pltpu.VMEM((block, d), BF16),
            pltpu.VMEM((block, 3 * d), BF16),
            pltpu.VMEM((TAIL, d), F32),
            pltpu.VMEM((d, 4 * d), BF16),
        ],
        compiler_params=params(),
        cost_estimate=cost(images * (16 * pad * d * d + 8 * pad * keys * d * 2), 15e6),
    )(idx, tokens, g, *das, h1, qkv, p, o, a1, wfull, rt, *grs)


def output_kernel(h1, y0, y1, y2, ssq, out, sums, moe):
    i = pl.program_id(0)
    pad = h1.shape[1]

    @pl.when(i == 0)
    def _():
        moe[...] = y0[...].astype(F32) + y1[...].astype(F32) + y2[...].astype(F32)
        sums[...] = jnp.zeros(sums.shape, F32)
        sums[1:2, :] = fold_lanes(ssq[0:1, :])

    branch = moe[pl.ds(pl.multiple_of(i * pad, TAIL), pad), :]
    result = h1[0] + branch
    sums[0:1, :] += fold_lanes(jnp.sum(result * result, axis=0, keepdims=True))
    sums[2:3, :] += fold_lanes(jnp.sum(branch * branch, axis=0, keepdims=True))
    out[0] = result.astype(BF16)


def output(h1, ys, ssq, seq):
    images, pad, d = h1.shape
    block = ys[0].shape[0]
    return pl.pallas_call(
        output_kernel,
        grid=(images,),
        out_shape=(
            jax.ShapeDtypeStruct((images, seq, d), BF16),
            jax.ShapeDtypeStruct((8, LANES), F32),
        ),
        in_specs=[pl.BlockSpec((1, pad, d), lambda i: (i, 0, 0))] + [whole((block, d))] * 3 + [whole((8, d))],
        out_specs=(pl.BlockSpec((1, pad, d), lambda i: (i, 0, 0)), whole((8, LANES))),
        scratch_shapes=[pltpu.VMEM((block, d), F32)],
        compiler_params=params(),
        cost_estimate=cost(10 * block * d, 5e6),
    )(h1, *ys, ssq)


def scatter_rows(a, axes, count):
    rows, width = a.shape
    return lax.all_to_all(a.reshape(count, rows // count, width), axes, 0, 0, tiled=True)


def add_rows(parts):
    summed = jnp.sum(parts.astype(F32), axis=0).astype(BF16)
    return jnp.broadcast_to(summed[None], parts.shape)


def collect_rows(spread, axes):
    count, rows, width = spread.shape
    return lax.all_to_all(spread, axes, 0, 0, tiled=True).reshape(count * rows, width)


def local(
    tokens,
    cotangent,
    gain_one,
    w_query,
    w_key,
    w_value,
    w_output,
    gain_two,
    w_router,
    w_in,
    w_out,
    routes,
):
    images, seq, d = tokens.shape
    experts = lax.axis_size("shard")
    pad = round_up(seq, TAIL)
    keys = round_up(seq, LANES)
    block = round_up(images * pad, LANES)
    rows = w_query.shape[0]
    me = lax.axis_index("shard")
    reps = lax.axis_size("line") * lax.axis_size("pair")
    idx = jnp.stack([me, me ^ 1, me ^ 2, me ^ 3]).astype(jnp.int32)
    core = lambda a: lax.ppermute(a, "shard", [(s, s ^ 1) for s in range(experts)])
    chip = lambda a: lax.ppermute(a, "shard", [(s, s ^ 2) for s in range(experts)])

    chosen = (routes[:, :, :, None] == jnp.arange(experts, dtype=jnp.int32)).any(axis=2)
    chosen = jnp.pad(chosen.astype(F32), ((0, 0), (0, pad - seq), (0, 0)))
    chosen = chosen.reshape(images * pad, experts).T
    masks = jnp.pad(
        chosen, ((MASK_ROW, TAIL - MASK_ROW - experts), (0, block - images * pad))
    )
    wp, gp = pl.pallas_call(
        functools.partial(pack_kernel, seq=seq, pad=pad),
        out_shape=(
            jax.ShapeDtypeStruct((rows + TAIL, 4 * d), BF16),
            jax.ShapeDtypeStruct((block, d), BF16),
        ),
        compiler_params=params(),
        cost_estimate=cost(1e6, 3e6),
    )(
        w_query, w_key, w_value, w_output,
        gain_one.reshape(1, rows), gain_two.reshape(1, rows), w_router.T, masks, cotangent,
    )
    wx = chip(wp)
    gx = chip(gp)
    packs = (wp, core(wp), wx, core(wx))
    gs = (gp, core(gp), gx, core(gx))
    w1, w2 = w_in[0], w_out[0]
    wfull, rt, qkv, p, o, a1, h1, a2, ssq = attn_fwd(
        idx, tokens, packs, seq, pad, keys, block
    )
    ax = chip(a2)
    replicas = ("line", "pair")
    zn, dun, da, dac, grn, an, gn = expert(
        idx, (a2, core(a2)), gs[:2], w1, w2, rt, packs[:2]
    )
    ax = after(ax, zn)
    zf, duf, dax, daxc, grf, af, gf = expert(
        idx, (ax, core(ax)), gs[2:], w1, w2, rt, packs[2:]
    )
    da_far = dax + core(daxc)
    replicas = ("line", "pair")
    grads_part = expert_grads(zn, zf, after(gn, da_far), gf, an, af, dun, duf)
    grads_slice = lax.psum_scatter(grads_part, replicas, scatter_dimension=0, tiled=True)
    grad_tokens, send, keep = attn_bwd(
        idx, tokens, gp, (da, core(dac), chip(da_far)), after(h1, grads_part),
        qkv, p, o, a1, wfull, rt, (grn, grf), seq, pad,
    )
    got = core(send)
    pack_far = keep[1] + got[1]
    yx, yxc = expert_out(after(zf, pack_far), w2)
    y_far = yx + core(yxc)
    y, yc = expert_out(after(zn, y_far), w2)
    pack = (
        after(keep, y)[0].astype(F32) + got[0].astype(F32) + chip(pack_far).astype(F32)
    ).astype(BF16)
    out, sums = output(after(h1, pack), (y, core(yc), chip(y_far)), ssq, seq)
    pack = scatter_rows(pack, replicas, reps)
    pack = add_rows(after(pack, out))
    grads = lax.all_gather(
        after(grads_slice, pack), replicas, axis=0, tiled=True
    )
    pack = collect_rows(pack, replicas).astype(F32)
    sums = jnp.broadcast_to(after(sums, pack)[None], (experts * reps, *sums.shape))
    sums = lax.all_to_all(sums, ("shard", *replicas), 0, 0, tiled=True)
    totals = jnp.sum(sums, axis=(0, 2))
    gwo, gwi = place(grads)
    roots = jnp.sqrt(totals / float(experts * reps * images * seq * d))
    tail = pack[:, 4 * d :]
    tail = pack[:, 4 * d :]
    return (
        out,
        grad_tokens,
        tail[4],
        pack[:, 0:d],
        pack[:, d : 2 * d],
        pack[:, 2 * d : 3 * d],
        pack[:, 3 * d : 4 * d],
        tail[5],
        tail[0:experts].T,
        gwi,
        gwo,
        roots[0],
        roots[1],
        roots[2],
    )


def solution(mesh):
    shards, reps = mesh.shape["shard"], mesh.shape["rep"]
    mesh = jax.sharding.Mesh(
        mesh.devices.reshape(shards, reps // 2, 2), ("shard", "line", "pair")
    )
    spread = P(("shard", "line", "pair"), None, None)
    matrix = P("shard", None)
    stack = P("shard", None, None)
    vector = P("shard")
    return jax.shard_map(
        local,
        mesh=mesh,
        in_specs=(
            spread, spread, vector, matrix, matrix, matrix, matrix, vector, matrix, stack, stack, spread,
        ),
        out_specs=(
            spread, spread, vector, matrix, matrix, matrix, matrix, vector, matrix, stack, stack, P(), P(), P(),
        ),
        check_vma=False,
    )
```

```python
import functools

import jax
import jax.numpy as jnp
from jax import lax
from jax.experimental import pallas as pl
from jax.experimental.pallas import tpu as pltpu
from jax.sharding import PartitionSpec as P

HEADS = 8
HEAD_DIM = 64
EPSILON = 1e-06
LANES = 128
TAIL = 16
MASK_ROW = 8
LONG = 1e11

BF16 = jnp.bfloat16
F32 = jnp.float32

LOG2E = 1.4426950408889634
ROOT_HALF = 0.7071067811865476
INV_ROOT_2PI = 0.3989422804014327


def round_up(value, multiple):
    return (value + multiple - 1) // multiple * multiple


def nn(a, b):
    return lax.dot_general(a, b, (((1,), (0,)), ((), ())), preferred_element_type=F32)


def nt(a, b):
    return lax.dot_general(a, b, (((1,), (1,)), ((), ())), preferred_element_type=F32)


def tn(a, b):
    return lax.dot_general(a, b, (((0,), (0,)), ((), ())), preferred_element_type=F32)


def norm_stats(values):
    center = values - jnp.mean(values, axis=-1, keepdims=True)
    inverse = lax.rsqrt(jnp.mean(center * center, axis=-1, keepdims=True) + EPSILON)
    return center * inverse, inverse


def norm_back(grad_normed, normed, inverse):
    mean_plain = jnp.mean(grad_normed, axis=-1, keepdims=True)
    mean_cross = jnp.mean(grad_normed * normed, axis=-1, keepdims=True)
    return inverse * (grad_normed - mean_plain - normed * mean_cross)


def gelu_pair(u):
    cdf = 0.5 * lax.erf(u * ROOT_HALF) + 0.5
    return u * cdf, cdf + u * (jnp.exp2(u * u * (-0.5 * LOG2E)) * INV_ROOT_2PI)


def split_heads(pair):
    low = lax.broadcasted_iota(jnp.int32, pair.shape, 1) < HEAD_DIM
    zero = jnp.zeros_like(pair)
    return jnp.concatenate([jnp.where(low, pair, zero), jnp.where(low, zero, pair)], axis=0)


def join_heads(stacked):
    rows = stacked.shape[0] // 2
    low = lax.broadcasted_iota(jnp.int32, (rows, stacked.shape[1]), 1) < HEAD_DIM
    return jnp.where(low, stacked[:rows], stacked[rows:])


def after(value, *first):
    return lax.optimization_barrier((value, *first))[0]


def stay(array):
    return pltpu.with_memory_space_constraint(array, pltpu.HBM)


def params(mebibytes=60):
    return pltpu.CompilerParams(vmem_limit_bytes=mebibytes * 1024 * 1024)


def cost(flops, nbytes, trans=0):
    return pl.CostEstimate(flops=int(flops), bytes_accessed=int(nbytes), transcendentals=int(trans))


def whole(shape):
    return pl.BlockSpec(shape, lambda *_: (0,) * len(shape))


SMEM_SPEC = pl.BlockSpec(memory_space=pltpu.SMEM)
VMEM_SPEC = pl.BlockSpec(memory_space=pltpu.VMEM)


def pack_kernel(wq, wk, wv, wo, g1, g2, wr, masks, cot, wp, gp, *, seq, pad):
    d = wq.shape[1]
    rows = wq.shape[0]
    for n, w in enumerate((wq, wk, wv, wo)):
        wp[0:rows, n * d : (n + 1) * d] = w[...]
    router = jnp.concatenate(
        [wr[...].astype(F32), jnp.zeros((TAIL - wr.shape[0], LANES), F32)], axis=0
    )
    row = lax.broadcasted_iota(jnp.int32, (TAIL, LANES), 0)
    head = jnp.where(row == 4, g1[...].astype(F32), router)
    head = jnp.where(row == 5, g2[...].astype(F32), head)
    wp[rows : rows + TAIL, :] = jnp.zeros((TAIL, wp.shape[1]), BF16)
    tokens = masks.shape[1]
    wp[rows : rows + TAIL, 0:tokens] = masks[...].astype(BF16)
    wp[rows : rows + TAIL, 0:LANES] = (head + masks[:, 0:LANES]).astype(BF16)
    gp[...] = jnp.zeros(gp.shape, BF16)
    for i in range(cot.shape[0]):
        gp[i * pad : i * pad + seq, :] = cot[i]


def attn_fwd_kernel(
    idx, tok, w0, w1, w2, w3, wfull, rt, mn, mf, qkv, p, o, a1, h1, a2, ssq, *, seq
):
    i = pl.program_id(0)
    pad, d = tok.shape[1], tok.shape[2]
    keys = qkv.shape[1]
    rows = w0.shape[0] - TAIL

    @pl.when(i == 0)
    def _():
        for n, w in enumerate((w0, w1, w2, w3)):
            at = pl.multiple_of(idx[n] * rows, rows)
            wfull[pl.ds(at, rows), :] = w[0:rows, :]
            rt[:, pl.ds(at, rows)] = w[rows : rows + TAIL, 0:rows].astype(F32)
            block = a1.shape[0]
            masks = mn if n < 2 else mf
            masks[:, n % 2 * block : (n % 2 + 1) * block] = w[rows : rows + TAIL, 0:block]
        for ref in (o, a1, a2):
            ref[...] = jnp.zeros(ref.shape, ref.dtype)
        ssq[...] = jnp.zeros(ssq.shape, F32)

    here = pl.ds(pl.multiple_of(i * pad, TAIL), pad)
    valid = lax.broadcasted_iota(jnp.int32, (pad, 1), 0) < seq
    x = jnp.where(valid, tok[0].astype(F32), 0.0)
    n1, _ = norm_stats(x)
    in_one = (n1 * rt[4:5, :]).astype(BF16)
    a1[here, :] = in_one
    proj = nn(in_one, wfull[:, 0 : 3 * d])
    qkv[0, 0:pad, 0:d] = (proj[:, 0:d].astype(BF16).astype(F32) * HEAD_DIM**-0.5).astype(BF16)
    qkv[0, 0:pad, d:] = proj[:, d:].astype(BF16)
    qkv[0, pad:keys, :] = jnp.zeros((keys - pad, 3 * d), BF16)
    column = lax.broadcasted_iota(jnp.int32, (1, keys), 1) < seq
    for hp in range(HEADS // 2):
        lanes = slice(LANES * hp, LANES * (hp + 1))
        stacked = split_heads(qkv[0, 0:pad, lanes])
        scores = nt(stacked, qkv[0, :, d + LANES * hp : d + LANES * (hp + 1)])
        scores = jnp.where(column, scores, -1e30)
        raised = jnp.exp(scores - jnp.max(scores, axis=-1, keepdims=True))
        probs = (raised * (1.0 / jnp.sum(raised, axis=-1, keepdims=True))).astype(BF16)
        p[0, hp] = probs
        mixed = nn(probs, qkv[0, :, 2 * d + LANES * hp : 2 * d + LANES * (hp + 1)])
        o[here, lanes] = join_heads(mixed).astype(BF16)
    attn = jnp.where(valid, nn(o[here, :], wfull[:, 3 * d : 4 * d]), 0.0)
    ssq[0:1, :] += jnp.sum(attn * attn, axis=0, keepdims=True)
    after = x + attn
    h1[0] = after
    n2, _ = norm_stats(after)
    a2[here, :] = (n2 * rt[5:6, :]).astype(BF16)


def attn_fwd(idx, tokens, packs, seq, pad, keys, block):
    images, _, d = tokens.shape
    rows = packs[0].shape[0]
    out_shape = (
        pltpu.HBM((d, 4 * d), BF16),
        jax.ShapeDtypeStruct((TAIL, d), F32),
        jax.ShapeDtypeStruct((TAIL, 2 * block), BF16),
        jax.ShapeDtypeStruct((TAIL, 2 * block), BF16),
        pltpu.HBM((images, keys, 3 * d), BF16),
        pltpu.HBM((images, HEADS // 2, 2 * pad, keys), BF16),
        pltpu.HBM((block, d), BF16),
        pltpu.HBM((block, d), BF16),
        pltpu.HBM((images, pad, d), F32),
        pltpu.VMEM((block, d), BF16),
        jax.ShapeDtypeStruct((8, d), F32),
    )
    return pl.pallas_call(
        functools.partial(attn_fwd_kernel, seq=seq),
        grid=(images,),
        out_shape=out_shape,
        in_specs=[SMEM_SPEC, pl.BlockSpec((1, pad, d), lambda i: (i, 0, 0))]
        + [VMEM_SPEC] * 4,
        out_specs=(
            whole((d, 4 * d)),
            whole((TAIL, d)),
            whole((TAIL, 2 * block)),
            whole((TAIL, 2 * block)),
            pl.BlockSpec((1, keys, 3 * d), lambda i: (i, 0, 0)),
            pl.BlockSpec((1, HEADS // 2, 2 * pad, keys), lambda i: (i, 0, 0, 0)),
            whole((block, d)),
            whole((block, d)),
            pl.BlockSpec((1, pad, d), lambda i: (i, 0, 0)),
            VMEM_SPEC,
            whole((8, d)),
        ),
        compiler_params=params(40),
        cost_estimate=cost(images * (8 * pad * d * d + 4 * pad * keys * d * 2), 10e6, 1.3e6),
    )(idx, stay(tokens), *packs)


def route(idx, a2s, rt, masks):
    both = a2s.shape[0]
    row = lax.broadcasted_iota(jnp.int32, (TAIL, both), 0)
    logits = jnp.where(row < 4, nt(rt[...].astype(BF16), a2s[...]), -1e30)
    raised = jnp.exp(logits - jnp.max(logits, axis=0, keepdims=True))
    share = raised / jnp.sum(raised, axis=0, keepdims=True)
    chosen = jnp.where(row == MASK_ROW + idx[0], masks[...].astype(F32), 0.0)
    chosen = jnp.sum(chosen, axis=0, keepdims=True)
    mine = jnp.sum(jnp.where(row == idx[0], share, 0.0), axis=0, keepdims=True)
    return jnp.where(row == MASK_ROW, chosen * mine, share).T


def fold_lanes(wide):
    parts = [wide[:, n : n + LANES] for n in range(0, wide.shape[1], LANES)]
    return sum(parts[1:], parts[0])


def gather_rows(a2a, a2b, ga, gb, a2s, gs):
    block = a2a.shape[0]
    a2s[0:block, :] = a2a[...]
    a2s[block:, :] = a2b[...]
    gs[0:block, :] = ga[...]
    gs[block:, :] = gb[...]


def finish_rows(idx, probs, dcomb, total, a2s, rt, da, db, gr):
    block = da.shape[0]
    lane = lax.broadcasted_iota(jnp.int32, (2 * block, TAIL), 1)
    own = (lane == idx[0]).astype(F32)
    inner = jnp.sum(dcomb[...], axis=1, keepdims=True)
    dlogits = jnp.where(lane < 4, inner * (own - probs[...]), 0.0).astype(BF16)
    gr[...] = tn(dlogits, a2s[...])
    result = (total[...] + nn(dlogits, rt[...].astype(BF16))).astype(BF16)
    da[...] = result[0:block]
    db[...] = result[block:]


def expert_kernel(
    idx, a2a, a2b, ga, gb, w1, w2, rt, masks,
    zc, du, da, db, gr, a2s, gs, probs, dcomb, total,
):
    j = pl.program_id(0)

    @pl.when(j == 0)
    def _():
        gather_rows(a2a, a2b, ga, gb, a2s, gs)
        probs[...] = route(idx, a2s, rt, masks)
        total[...] = jnp.zeros(total.shape, F32)
        dcomb[...] = jnp.zeros(dcomb.shape, F32)

    act, slope = gelu_pair(nn(a2s[...], w1[...]))
    scale = probs[:, MASK_ROW : MASK_ROW + 1]
    mixed = (act * scale).astype(BF16)
    here = pl.ds(pl.multiple_of(j * w1.shape[1], LANES), w1.shape[1])
    zc[:, here] = mixed
    dz = nt(gs[...], w2[...])
    dcomb[...] += fold_lanes(mixed.astype(F32) * dz)
    grad = (slope * scale * dz).astype(BF16)
    du[:, here] = grad
    total[...] += nt(grad, w1[...])

    @pl.when(j == pl.num_programs(0) - 1)
    def _():
        finish_rows(idx, probs, dcomb, total, a2s, rt, da, db, gr)


def expert(idx, a2s, gs, w1, w2, rt, masks):
    block, d = a2s[0].shape
    f = w1.shape[1]
    both = 2 * block
    w1_spec = pl.BlockSpec((d, f // 4), lambda j: (0, j))
    w2_spec = pl.BlockSpec((f // 4, d), lambda j: (j, 0))
    return pl.pallas_call(
        expert_kernel,
        grid=(4,),
        out_shape=(
            pltpu.VMEM((both, f), BF16),
            pltpu.VMEM((both, f), BF16),
            pltpu.VMEM((block, d), BF16),
            pltpu.VMEM((block, d), BF16),
            jax.ShapeDtypeStruct((TAIL, d), F32),
            pltpu.VMEM((both, d), BF16),
            pltpu.VMEM((both, d), BF16),
        ),
        in_specs=[SMEM_SPEC]
        + [VMEM_SPEC] * 4
        + [w1_spec, w2_spec, VMEM_SPEC, VMEM_SPEC],
        out_specs=(VMEM_SPEC,) * 4 + (whole((TAIL, d)),) + (VMEM_SPEC,) * 2,
        scratch_shapes=[
            pltpu.VMEM((both, TAIL), F32),
            pltpu.VMEM((both, LANES), F32),
            pltpu.VMEM((both, d), F32),
        ],
        compiler_params=params(26),
        cost_estimate=cost(6 * both * d * f, 25e6, 2 * both * f),
    )(idx, *a2s, *gs, stay(w1), stay(w2), rt, masks)


def grads_kernel(zn, zf, gn, gf, an, af, dn, df, out):
    j = pl.program_id(0)
    tall, d = out.shape

    @pl.when(j < 2)
    def _():
        here = pl.ds(pl.multiple_of(j * tall, LANES), tall)
        out[...] = (tn(zn[:, here], gn[...]) + tn(zf[:, here], gf[...])).astype(BF16)

    @pl.when(j >= 2)
    def _():
        for n in range(tall // d):
            here = pl.ds(pl.multiple_of((j - 2) * tall + n * d, LANES), d)
            grad = tn(an[...], dn[:, here]) + tn(af[...], df[:, here])
            out[n * d : (n + 1) * d, :] = grad.astype(BF16)


def expert_grads(zn, zf, gn, gf, an, af, dn, df):
    both, f = zn.shape
    d = gn.shape[1]
    step = f // 2
    return pl.pallas_call(
        grads_kernel,
        grid=(4,),
        out_shape=pltpu.HBM((2 * f, d), BF16),
        in_specs=[VMEM_SPEC] * 8,
        out_specs=pl.BlockSpec((step, d), lambda j: (j, 0)),
        compiler_params=params(16),
        cost_estimate=cost(8 * both * d * f, 25e6),
    )(zn, zf, gn, gf, an, af, dn, df)


def place_kernel(grads, gwo, gwi, gq, gk, gv, go, router, gain1, gain2, pack):
    j, count = pl.program_id(0), pl.num_programs(0)
    large = gwo.shape[1]
    small = grads.shape[1] - large
    pack[pl.ds(pl.multiple_of(j * small, 8), small), :] = grads[0, large:, :].astype(F32)

    @pl.when(j < count // 2)
    def _():
        gwo[0] = grads[0, 0:large, :].astype(F32)

    @pl.when(j >= count // 2)
    def _():
        gwi[0] = grads[0, 0:large, :].astype(F32)

    @pl.when(j == count - 1)
    def _():
        rows = gq.shape[0]
        for n, ref in enumerate((gq, gk, gv, go)):
            ref[...] = pack[n * rows : (n + 1) * rows, :]
        router[...] = pack[4 * rows : 4 * rows + 4, 0:rows]
        gain1[...] = pack[4 * rows + 4 : 4 * rows + 5, 0:rows]
        gain2[...] = pack[4 * rows + 5 : 4 * rows + 6, 0:rows]


def place(grads, f, rows):
    count, tall, d = grads.shape
    large = 2 * f // count
    half, runs = count // 2, d // large
    late = lambda j: jnp.maximum(j - half, 0)
    matrix = jax.ShapeDtypeStruct((rows, d), F32)
    return pl.pallas_call(
        place_kernel,
        grid=(count,),
        out_shape=(
            jax.ShapeDtypeStruct((1, f, d), F32),
            jax.ShapeDtypeStruct((1, d, f), F32),
            matrix,
            matrix,
            matrix,
            matrix,
            jax.ShapeDtypeStruct((4, rows), F32),
            jax.ShapeDtypeStruct((1, rows), F32),
            jax.ShapeDtypeStruct((1, rows), F32),
        ),
        in_specs=[pl.BlockSpec((1, tall, d), lambda j: (j, 0, 0))],
        out_specs=(
            pl.BlockSpec((1, large, d), lambda j: (0, jnp.minimum(j, half - 1), 0)),
            pl.BlockSpec((1, large, d), lambda j: (0, late(j) % runs, late(j) // runs)),
            *[whole((rows, d))] * 4,
            whole((4, rows)),
            whole((1, rows)),
            whole((1, rows)),
        ),
        scratch_shapes=[pltpu.VMEM((count * (tall - large), d), F32)],
        compiler_params=params(),
        cost_estimate=cost(1e6, 12e6),
    )(grads)


def expert_out_kernel(zn, zf, w2, y0, y1, y2, y3, near, far):
    j = pl.program_id(0)
    block = y0.shape[0]

    here = pl.ds(pl.multiple_of(j * w2.shape[0], LANES), w2.shape[0])

    @pl.when(j == 0)
    def _():
        near[...] = nn(zn[:, here], w2[...])
        far[...] = nn(zf[:, here], w2[...])

    @pl.when(j > 0)
    def _():
        near[...] += nn(zn[:, here], w2[...])
        far[...] += nn(zf[:, here], w2[...])

    @pl.when(j == pl.num_programs(0) - 1)
    def _():
        y0[...] = near[0:block, :].astype(BF16)
        y1[...] = near[block:, :].astype(BF16)
        y2[...] = far[0:block, :].astype(BF16)
        y3[...] = far[block:, :].astype(BF16)


def expert_out(zn, zf, w2):
    both, f = zn.shape
    d = w2.shape[1]
    step = f // 4
    return pl.pallas_call(
        expert_out_kernel,
        grid=(4,),
        out_shape=[jax.ShapeDtypeStruct((both // 2, d), BF16)] * 4,
        in_specs=[VMEM_SPEC] * 2
        + [pl.BlockSpec((step, d), lambda j: (j, 0))],
        out_specs=[whole((both // 2, d))] * 4,
        scratch_shapes=[pltpu.VMEM((both, d), F32)] * 2,
        compiler_params=params(24),
        cost_estimate=cost(4 * d * f * both, 16e6),
    )(zn, zf, stay(w2))


def attn_bwd_kernel(
    idx, tok, g, da0, da1, da2, h1, qkv, p, o, a1, wfull, rt, gra, grb,
    gtok, pack_send, pack_keep,
    da, dattn_all, dqkv, gains, grads, *, seq,
):
    i = pl.program_id(0)
    pad, d = tok.shape[1], tok.shape[2]
    rows = d // 4

    @pl.when(i == 0)
    def _():
        da[...] = da0[...].astype(F32) + da1[...].astype(F32) + da2[...].astype(F32)
        dattn_all[...] = jnp.zeros(dattn_all.shape, BF16)
        dqkv[...] = jnp.zeros(dqkv.shape, BF16)
        gains[...] = jnp.zeros(gains.shape, F32)

    here = pl.ds(pl.multiple_of(i * pad, TAIL), pad)
    valid = lax.broadcasted_iota(jnp.int32, (pad, 1), 0) < seq
    n2, r2 = norm_stats(h1[0])
    din = da[here, :]
    gains[1:2, :] += jnp.sum(din * n2, axis=0, keepdims=True)
    dh1 = g[here, :].astype(F32) + norm_back(din * rt[5:6, :], n2, r2)
    dattn = dh1.astype(BF16)
    dattn_all[here, :] = dattn
    do = nt(dattn, wfull[:, 3 * d : 4 * d]).astype(BF16)
    for hp in range(HEADS // 2):
        lanes = slice(LANES * hp, LANES * (hp + 1))
        klanes = slice(d + LANES * hp, d + LANES * (hp + 1))
        vlanes = slice(2 * d + LANES * hp, 2 * d + LANES * (hp + 1))
        do2 = split_heads(do[:, lanes])
        dp = nt(do2, qkv[0, :, vlanes])
        probs = p[0, hp]
        wide = probs.astype(F32)
        ds = (wide * (dp - jnp.sum(dp * wide, axis=-1, keepdims=True))).astype(BF16)
        dqkv[here, vlanes] = tn(probs, do2)[0:pad].astype(BF16)
        dq = join_heads(nn(ds, qkv[0, :, klanes]))
        dqkv[here, lanes] = (dq * HEAD_DIM**-0.5).astype(BF16)
        dqkv[here, klanes] = tn(ds, split_heads(qkv[0, 0:pad, lanes]))[0:pad].astype(BF16)
    din1 = nt(dqkv[here, :], wfull[:, 0 : 3 * d])
    x = jnp.where(valid, tok[0].astype(F32), 0.0)
    n1, r1 = norm_stats(x)
    gains[0:1, :] += jnp.sum(din1 * n1, axis=0, keepdims=True)
    gtok[0] = (dh1 + norm_back(din1 * rt[4:5, :], n1, r1)).astype(BF16)

    @pl.when(i == pl.num_programs(0) - 1)
    def _():
        grads[:, 0 : 3 * d] = tn(a1[...], dqkv[...]).astype(BF16)
        grads[:, 3 * d : 4 * d] = tn(o[...], dattn_all[...]).astype(BF16)
        row = lax.broadcasted_iota(jnp.int32, (TAIL, d), 0)
        tail = jnp.where(row < 4, gra[...] + grb[...], 0.0)
        tail = jnp.where(row == 4, gains[0:1, :], tail)
        gains[...] = jnp.where(row == 5, gains[1:2, :], tail)
        for n, (ref, slot) in enumerate(
            ((pack_keep, 0), (pack_send, 0), (pack_keep, 1), (pack_send, 1))
        ):
            at = pl.multiple_of(idx[n] * rows, rows)
            for m in range(4):
                ref[slot, m * rows : (m + 1) * rows, :] = grads[pl.ds(at, rows), m * d : (m + 1) * d]
            ref[slot, 4 * rows :, :] = jnp.zeros((ref.shape[1] - 4 * rows, d), BF16)
            ref[slot, 4 * rows : 4 * rows + TAIL, 0:rows] = gains[:, pl.ds(at, rows)].astype(BF16)


def attn_bwd(idx, tokens, g, das, h1, qkv, p, o, a1, wfull, rt, grs, seq, pad, pack_rows):
    images, _, d = tokens.shape
    block = g.shape[0]
    keys = qkv.shape[1]
    image = lambda i: (i, 0, 0)
    return pl.pallas_call(
        functools.partial(attn_bwd_kernel, seq=seq),
        grid=(images,),
        out_shape=(
            jax.ShapeDtypeStruct(tokens.shape, BF16),
            jax.ShapeDtypeStruct((2, pack_rows, d), BF16),
            jax.ShapeDtypeStruct((2, pack_rows, d), BF16),
        ),
        in_specs=[SMEM_SPEC, pl.BlockSpec((1, pad, d), image), whole((block, d))]
        + [VMEM_SPEC] * 3
        + [
            pl.BlockSpec((1, pad, d), image),
            pl.BlockSpec((1, keys, 3 * d), image),
            pl.BlockSpec((1, HEADS // 2, 2 * pad, keys), lambda i: (i, 0, 0, 0)),
            whole((block, d)),
            whole((block, d)),
            whole((d, 4 * d)),
            whole((TAIL, d)),
            whole((TAIL, d)),
            whole((TAIL, d)),
        ],
        out_specs=(
            pl.BlockSpec((1, pad, d), image),
            whole((2, pack_rows, d)),
            whole((2, pack_rows, d)),
        ),
        scratch_shapes=[
            pltpu.VMEM((block, d), F32),
            pltpu.VMEM((block, d), BF16),
            pltpu.VMEM((block, 3 * d), BF16),
            pltpu.VMEM((TAIL, d), F32),
            pltpu.VMEM((d, 4 * d), BF16),
        ],
        compiler_params=params(40),
        cost_estimate=cost(LONG, 15e6),
    )(
        idx, stay(tokens), stay(g), *das,
        *(stay(kept) for kept in (h1, qkv, p, o, a1, wfull)), rt, *grs,
    )


def output_kernel(h1, y0, y1, y2, ssq, out, sums, moe):
    i = pl.program_id(0)
    pad = h1.shape[1]

    @pl.when(i == 0)
    def _():
        moe[...] = y0[...].astype(F32) + y1[...].astype(F32) + y2[...].astype(F32)
        sums[...] = jnp.zeros(sums.shape, F32)
        sums[1:2, :] = fold_lanes(ssq[0:1, :])

    branch = moe[pl.ds(pl.multiple_of(i * pad, TAIL), pad), :]
    result = h1[0] + branch
    sums[0:1, :] += fold_lanes(jnp.sum(result * result, axis=0, keepdims=True))
    sums[2:3, :] += fold_lanes(jnp.sum(branch * branch, axis=0, keepdims=True))
    out[0] = result.astype(BF16)


def output(h1, ys, ssq, seq):
    images, pad, d = h1.shape
    block = ys[0].shape[0]
    return pl.pallas_call(
        output_kernel,
        grid=(images,),
        out_shape=(
            jax.ShapeDtypeStruct((images, seq, d), BF16),
            jax.ShapeDtypeStruct((8, LANES), F32),
        ),
        in_specs=[pl.BlockSpec((1, pad, d), lambda i: (i, 0, 0))] + [VMEM_SPEC] * 4,
        out_specs=(pl.BlockSpec((1, pad, d), lambda i: (i, 0, 0)), whole((8, LANES))),
        scratch_shapes=[pltpu.VMEM((block, d), F32)],
        compiler_params=params(16),
        cost_estimate=cost(10 * block * d, 5e6),
    )(stay(h1), *ys, ssq)


def scatter_rows(a, axes, groups):
    count = len(groups[0])
    parts = a.reshape(count, a.shape[0] // count, a.shape[1])
    return lax.all_to_all(parts, axes, 0, 0, tiled=True, axis_index_groups=groups)


def add_rows(parts):
    return jnp.sum(parts.astype(F32), axis=0).astype(BF16)


def local(
    tokens,
    cotangent,
    gain_one,
    w_query,
    w_key,
    w_value,
    w_output,
    gain_two,
    w_router,
    w_in,
    w_out,
    routes,
):
    images, seq, d = tokens.shape
    experts = lax.axis_size("shard")
    pad = round_up(seq, TAIL)
    keys = round_up(seq, LANES)
    block = round_up(images * pad, LANES)
    rows = w_query.shape[0]
    me = lax.axis_index("shard")
    reps = lax.axis_size("rep")
    everyone = ("shard", "rep")
    ring = [*range(0, reps, 2), *range(reps - 1, 0, -2)]
    rings = [[s * reps + r for r in ring] for s in range(experts)]
    idx = jnp.stack([me, me ^ 1, me ^ 2, me ^ 3]).astype(jnp.int32)
    core = lambda a: lax.ppermute(a, "shard", [(s, s ^ 1) for s in range(experts)])
    chip = lambda a: lax.ppermute(a, "shard", [(s, s ^ 2) for s in range(experts)])

    chosen = (routes[:, :, :, None] == jnp.arange(experts, dtype=jnp.int32)).any(axis=2)
    chosen = jnp.pad(chosen.astype(F32), ((0, 0), (0, pad - seq), (0, 0)))
    chosen = chosen.reshape(images * pad, experts).T
    masks = jnp.pad(
        chosen, ((MASK_ROW, TAIL - MASK_ROW - experts), (0, block - images * pad))
    )
    wp, gp = pl.pallas_call(
        functools.partial(pack_kernel, seq=seq, pad=pad),
        out_shape=(
            jax.ShapeDtypeStruct((rows + TAIL, 4 * d), BF16),
            jax.ShapeDtypeStruct((block, d), BF16),
        ),
        compiler_params=params(),
        cost_estimate=cost(1e6, 3e6),
    )(
        w_query, w_key, w_value, w_output,
        gain_one.reshape(1, rows), gain_two.reshape(1, rows), w_router.T, masks, cotangent,
    )
    wx = chip(wp)
    gx = chip(gp)
    packs = (wp, core(wp), wx, core(wx))
    gs = (gp, core(gp), gx, core(gx))
    w1, w2 = w_in[0], w_out[0]
    wfull, rt, masks_near, masks_far, qkv, p, o, a1, h1, a2, ssq = attn_fwd(
        idx, tokens, packs, seq, pad, keys, block
    )
    ax = chip(a2)
    zn, dun, da, dac, grn, an, gn = expert(
        idx, (a2, core(a2)), gs[:2], w1, w2, rt, masks_near
    )
    ax = after(ax, zn)
    zf, duf, dax, daxc, grf, af, gf = expert(
        idx, (ax, core(ax)), gs[2:], w1, w2, rt, masks_far
    )
    da_far = dax + core(daxc)
    grads_part = expert_grads(zn, zf, after(gn, da_far), gf, an, af, dun, duf)
    grads_slice = lax.psum_scatter(
        grads_part, everyone, scatter_dimension=0, tiled=True, axis_index_groups=rings
    )
    grad_tokens, send, keep = attn_bwd(
        idx, tokens, gp, (da, core(dac), chip(da_far)), after(h1, grads_part),
        qkv, p, o, a1, wfull, rt, (grn, grf), seq, pad, round_up(4 * rows + TAIL, 8 * reps),
    )
    got = core(send)
    pack_far = keep[1] + got[1]
    y, yc, yx, yxc = expert_out(after(zn, pack_far), zf, w2)
    pack = (
        after(keep, y)[0].astype(F32) + got[0].astype(F32) + chip(pack_far).astype(F32)
    ).astype(BF16)
    y_far = after(yx, pack) + core(yxc)
    pack = scatter_rows(pack, everyone, rings)
    grads = jnp.concatenate([grads_slice, add_rows(pack)], axis=0)
    grads = lax.all_gather(grads, everyone, axis=0, axis_index_groups=rings)
    out, sums = output(h1, (y, core(yc), chip(y_far)), ssq, seq)
    sums = jnp.broadcast_to(after(sums, pack)[None], (experts * reps, *sums.shape))
    sums = lax.all_to_all(sums, everyone, 0, 0, tiled=True)
    totals = jnp.sum(sums, axis=(0, 2))
    gwo, gwi, gq, gk, gv, go, router, gain1, gain2 = place(grads, w1.shape[1], rows)
    roots = jnp.sqrt(totals / float(experts * reps * images * seq * d))
    return (
        out,
        grad_tokens,
        gain1.reshape(rows),
        gq,
        gk,
        gv,
        go,
        gain2.reshape(rows),
        router.T,
        gwi,
        gwo,
        roots[0],
        roots[1],
        roots[2],
    )


def solution(mesh):
    spread = P(("shard", "rep"), None, None)
    matrix = P("shard", None)
    stack = P("shard", None, None)
    vector = P("shard")
    return jax.shard_map(
        local,
        mesh=mesh,
        in_specs=(
            spread, spread, vector, matrix, matrix, matrix, matrix, vector, matrix, stack, stack, spread,
        ),
        out_specs=(
            spread, spread, vector, matrix, matrix, matrix, matrix, vector, matrix, stack, stack, P(), P(), P(),
        ),
        check_vma=False,
    )
```

```python
import functools

import jax
import jax.numpy as jnp
from jax import lax
from jax.experimental import pallas as pl
from jax.experimental.pallas import tpu as pltpu
from jax.sharding import PartitionSpec as P

HEADS = 8
HEAD_DIM = 64
EPSILON = 1e-06
LANES = 128
TAIL = 16
HEAD = 8
LONG = 1e11

BF16 = jnp.bfloat16
F32 = jnp.float32

LOG2E = 1.4426950408889634
ROOT_HALF = 0.7071067811865476
INV_ROOT_2PI = 0.3989422804014327


def round_up(value, multiple):
    return (value + multiple - 1) // multiple * multiple


def nn(a, b):
    return lax.dot_general(a, b, (((1,), (0,)), ((), ())), preferred_element_type=F32)


def nt(a, b):
    return lax.dot_general(a, b, (((1,), (1,)), ((), ())), preferred_element_type=F32)


def tn(a, b):
    return lax.dot_general(a, b, (((0,), (0,)), ((), ())), preferred_element_type=F32)


def norm_stats(values):
    center = values - jnp.mean(values, axis=-1, keepdims=True)
    inverse = lax.rsqrt(jnp.mean(center * center, axis=-1, keepdims=True) + EPSILON)
    return center * inverse, inverse


def norm_back(grad_normed, normed, inverse):
    mean_plain = jnp.mean(grad_normed, axis=-1, keepdims=True)
    mean_cross = jnp.mean(grad_normed * normed, axis=-1, keepdims=True)
    return inverse * (grad_normed - mean_plain - normed * mean_cross)


def gelu_pair(u):
    cdf = 0.5 * lax.erf(u * ROOT_HALF) + 0.5
    return u * cdf, cdf + u * (jnp.exp2(u * u * (-0.5 * LOG2E)) * INV_ROOT_2PI)


def split_heads(pair):
    low = lax.broadcasted_iota(jnp.int32, pair.shape, 1) < HEAD_DIM
    zero = jnp.zeros_like(pair)
    return jnp.concatenate([jnp.where(low, pair, zero), jnp.where(low, zero, pair)], axis=0)


def join_heads(stacked):
    rows = stacked.shape[0] // 2
    low = lax.broadcasted_iota(jnp.int32, (rows, stacked.shape[1]), 1) < HEAD_DIM
    return jnp.where(low, stacked[:rows], stacked[rows:])


def after(value, *first):
    return lax.optimization_barrier((value, *first))[0]


def stay(array):
    return pltpu.with_memory_space_constraint(array, pltpu.HBM)


def params(mebibytes=60):
    return pltpu.CompilerParams(vmem_limit_bytes=mebibytes * 1024 * 1024)


def cost(flops, nbytes, trans=0):
    return pl.CostEstimate(flops=int(flops), bytes_accessed=int(nbytes), transcendentals=int(trans))


def whole(shape):
    return pl.BlockSpec(shape, lambda *_: (0,) * len(shape))


SMEM_SPEC = pl.BlockSpec(memory_space=pltpu.SMEM)
VMEM_SPEC = pl.BlockSpec(memory_space=pltpu.VMEM)
FAR_SPEC = pl.BlockSpec(memory_space=pl.ANY)


def pack_weights_kernel(wq, wk, wv, wo, g1, g2, wr, wp):
    rows, d = wq.shape
    for n, w in enumerate((wq, wk, wv, wo)):
        wp[0:rows, n * d : (n + 1) * d] = w[...]
    blank = jnp.zeros((HEAD - wr.shape[0], LANES), F32)
    head = jnp.concatenate([wr[...].astype(F32), blank], axis=0)
    row = lax.broadcasted_iota(jnp.int32, (HEAD, LANES), 0)
    head = jnp.where(row == 4, g1[...].astype(F32), head)
    head = jnp.where(row == 5, g2[...].astype(F32), head)
    wp[rows:, :] = jnp.zeros((HEAD, wp.shape[1]), BF16)
    wp[rows:, 0:LANES] = head.astype(BF16)


def pack_cotangent_kernel(cot, masks, gp, *, seq, pad):
    gp[...] = jnp.zeros(gp.shape, BF16)
    for i in range(cot.shape[0]):
        gp[i * pad : i * pad + seq, :] = cot[i]
    gp[gp.shape[0] - TAIL :, :] = masks[...]


def attn_fwd_kernel(
    idx, tok, w0, w1, w2, w3, wfull, rt, qkv, p, o, a1, h1, a2, ssq, *, seq
):
    i = pl.program_id(0)
    pad, d = tok.shape[1], tok.shape[2]
    keys = qkv.shape[1]
    rows = w0.shape[0] - HEAD

    @pl.when(i == 0)
    def _():
        for n, w in enumerate((w0, w1, w2, w3)):
            at = pl.multiple_of(idx[n] * rows, rows)
            wfull[pl.ds(at, rows), :] = w[0:rows, :]
            rt[0:HEAD, pl.ds(at, rows)] = w[rows:, 0:rows].astype(F32)
            rt[HEAD:, pl.ds(at, rows)] = jnp.zeros((TAIL - HEAD, rows), F32)
        for ref in (o, a1, a2):
            ref[...] = jnp.zeros(ref.shape, ref.dtype)
        ssq[...] = jnp.zeros(ssq.shape, F32)

    here = pl.ds(pl.multiple_of(i * pad, TAIL), pad)
    valid = lax.broadcasted_iota(jnp.int32, (pad, 1), 0) < seq
    x = jnp.where(valid, tok[0].astype(F32), 0.0)
    n1, _ = norm_stats(x)
    in_one = (n1 * rt[4:5, :]).astype(BF16)
    a1[here, :] = in_one
    proj = nn(in_one, wfull[:, 0 : 3 * d])
    qkv[0, 0:pad, 0:d] = (proj[:, 0:d].astype(BF16).astype(F32) * HEAD_DIM**-0.5).astype(BF16)
    qkv[0, 0:pad, d:] = proj[:, d:].astype(BF16)
    qkv[0, pad:keys, :] = jnp.zeros((keys - pad, 3 * d), BF16)
    column = lax.broadcasted_iota(jnp.int32, (1, keys), 1) < seq
    pairs = range(HEADS // 2)
    lanes = [slice(LANES * hp, LANES * (hp + 1)) for hp in pairs]
    scores = [
        nt(split_heads(qkv[0, 0:pad, lanes[hp]]), qkv[0, :, d + LANES * hp : d + LANES * (hp + 1)])
        for hp in pairs
    ]
    scores = [jnp.where(column, score, -1e30) for score in scores]
    tops = [jnp.max(score, axis=-1, keepdims=True) for score in scores]
    raised = [jnp.exp(score - top) for score, top in zip(scores, tops)]
    totals = [1.0 / jnp.sum(each, axis=-1, keepdims=True) for each in raised]
    for hp in pairs:
        p[0, hp] = (raised[hp] * totals[hp]).astype(BF16)
    for hp in pairs:
        mixed = nn(p[0, hp], qkv[0, :, 2 * d + LANES * hp : 2 * d + LANES * (hp + 1)])
        o[here, lanes[hp]] = join_heads(mixed).astype(BF16)
    attn = jnp.where(valid, nn(o[here, :], wfull[:, 3 * d : 4 * d]), 0.0)
    ssq[0:1, :] += jnp.sum(attn * attn, axis=0, keepdims=True)
    after = x + attn
    h1[0] = after
    n2, _ = norm_stats(after)
    a2[here, :] = (n2 * rt[5:6, :]).astype(BF16)


def attn_fwd(idx, tokens, packs, seq, pad, keys, block):
    images, _, d = tokens.shape
    out_shape = (
        pltpu.HBM((d, 4 * d), BF16),
        jax.ShapeDtypeStruct((TAIL, d), F32),
        pltpu.HBM((images, keys, 3 * d), BF16),
        pltpu.HBM((images, HEADS // 2, 2 * pad, keys), BF16),
        pltpu.HBM((block, d), BF16),
        pltpu.HBM((block, d), BF16),
        pltpu.HBM((images, pad, d), F32),
        pltpu.VMEM((block, d), BF16),
        jax.ShapeDtypeStruct((8, d), F32),
    )
    return pl.pallas_call(
        functools.partial(attn_fwd_kernel, seq=seq),
        grid=(images,),
        out_shape=out_shape,
        in_specs=[SMEM_SPEC, pl.BlockSpec((1, pad, d), lambda i: (i, 0, 0))]
        + [VMEM_SPEC] * 4,
        out_specs=(
            whole((d, 4 * d)),
            whole((TAIL, d)),
            pl.BlockSpec((1, keys, 3 * d), lambda i: (i, 0, 0)),
            pl.BlockSpec((1, HEADS // 2, 2 * pad, keys), lambda i: (i, 0, 0, 0)),
            whole((block, d)),
            whole((block, d)),
            pl.BlockSpec((1, pad, d), lambda i: (i, 0, 0)),
            VMEM_SPEC,
            whole((8, d)),
        ),
        compiler_params=params(40),
        cost_estimate=cost(1, 1),
    )(idx, stay(tokens), *packs)


def chosen_row(idx, ref, block):
    masks = ref[block:, :].astype(F32)
    row = lax.broadcasted_iota(jnp.int32, masks.shape, 0)
    parts = []
    for n in range(0, block, masks.shape[1]):
        wanted = row == n // masks.shape[1] * 4 + idx[0]
        line = jnp.sum(jnp.where(wanted, masks, 0.0), axis=0, keepdims=True)
        parts.append(line[:, 0 : min(block - n, masks.shape[1])])
    return jnp.concatenate(parts, axis=1)


def route(idx, a2s, rt, ga, gb):
    both = a2s.shape[0]
    row = lax.broadcasted_iota(jnp.int32, (TAIL, both), 0)
    logits = jnp.where(row < 4, nt(rt[...].astype(BF16), a2s[...]), -1e30)
    raised = jnp.exp(logits - jnp.max(logits, axis=0, keepdims=True))
    share = raised / jnp.sum(raised, axis=0, keepdims=True)
    block = both // 2
    chosen = jnp.concatenate([chosen_row(idx, ga, block), chosen_row(idx, gb, block)], axis=1)
    mine = jnp.sum(jnp.where(row == idx[0], share, 0.0), axis=0, keepdims=True)
    return jnp.where(row == HEAD, chosen * mine, share).T


def fold_lanes(wide):
    parts = [wide[:, n : n + LANES] for n in range(0, wide.shape[1], LANES)]
    return sum(parts[1:], parts[0])


def gather_rows(a2a, a2b, ga, gb, a2s, gs):
    block = a2a.shape[0]
    a2s[0:block, :] = a2a[...]
    a2s[block:, :] = a2b[...]
    gs[0:block, :] = ga[0:block, :]
    gs[block:, :] = gb[0:block, :]


def finish_rows(idx, probs, dcomb, total, a2s, rt, da, db, gr):
    block = da.shape[0]
    lane = lax.broadcasted_iota(jnp.int32, (2 * block, TAIL), 1)
    own = (lane == idx[0]).astype(F32)
    inner = jnp.sum(dcomb[...], axis=1, keepdims=True)
    dlogits = jnp.where(lane < 4, inner * (own - probs[...]), 0.0).astype(BF16)
    gr[...] = tn(dlogits, a2s[...])
    result = (total[...] + nn(dlogits, rt[...].astype(BF16))).astype(BF16)
    da[...] = result[0:block]
    db[...] = result[block:]


def expert_kernel(
    idx, a2a, a2b, ga, gb, w1_far, w2_far, rt,
    zc, du, da, db, gr, a2s, gs, w1, w2, probs, dcomb, total, sem1, sem2,
):
    step = w1.shape[2]
    loads = []
    for j in range(w1.shape[0]):
        here = pl.ds(j * step, step)
        loads.append(pltpu.make_async_copy(w1_far.at[:, here], w1.at[j], sem1.at[j]))
        loads.append(pltpu.make_async_copy(w2_far.at[here], w2.at[j], sem2.at[j]))
    for copy in loads:
        copy.start()
    gather_rows(a2a, a2b, ga, gb, a2s, gs)
    probs[...] = route(idx, a2s, rt, ga, gb)
    total[...] = jnp.zeros(total.shape, F32)
    dcomb[...] = jnp.zeros(dcomb.shape, F32)

    @pl.loop(0, w1.shape[0])
    def _(j):
        here = pl.ds(pl.multiple_of(j * step, LANES), step)
        pltpu.make_async_copy(w1_far.at[:, here], w1.at[j], sem1.at[j]).wait()
        pltpu.make_async_copy(w2_far.at[here], w2.at[j], sem2.at[j]).wait()
        halves = [slice(0, a2s.shape[0] // 2), slice(a2s.shape[0] // 2, a2s.shape[0])]
        us = [nn(a2s[r, :], w1[j]) for r in halves]
        dzs = [nt(gs[r, :], w2[j]) for r in halves]
        for r, u, dz in zip(halves, us, dzs):
            act, slope = gelu_pair(u)
            scale = probs[r, HEAD : HEAD + 1]
            mixed = (act * scale).astype(BF16)
            zc[r, here] = mixed
            dcomb[r, :] += fold_lanes(mixed.astype(F32) * dz)
            grad = (slope * scale * dz).astype(BF16)
            du[r, here] = grad
            total[r, :] += nt(grad, w1[j])

    finish_rows(idx, probs, dcomb, total, a2s, rt, da, db, gr)


def expert(idx, a2s, gs, w1, w2, rt, near):
    block, d = a2s[0].shape
    f = w1.shape[1]
    both = 2 * block
    step = f // 4
    return pl.pallas_call(
        expert_kernel,
        out_shape=(
            pltpu.VMEM((both, f), BF16),
            pltpu.VMEM((both, f), BF16),
            pltpu.HBM((block, d), BF16) if near else pltpu.VMEM((block, d), BF16),
            pltpu.VMEM((block, d), BF16),
            jax.ShapeDtypeStruct((TAIL, d), F32),
            pltpu.VMEM((both, d), BF16),
            pltpu.VMEM((both, d), BF16),
        ),
        in_specs=[SMEM_SPEC] + [VMEM_SPEC] * 4 + [FAR_SPEC] * 2 + [VMEM_SPEC],
        out_specs=(VMEM_SPEC,) * 2
        + (pl.BlockSpec((block, d), lambda: (0, 0)) if near else VMEM_SPEC,)
        + (VMEM_SPEC,) * 4,
        scratch_shapes=[
            pltpu.VMEM((4, d, step), BF16),
            pltpu.VMEM((4, step, d), BF16),
            pltpu.VMEM((both, TAIL), F32),
            pltpu.VMEM((both, LANES), F32),
            pltpu.VMEM((both, d), F32),
            pltpu.SemaphoreType.DMA((4,)),
            pltpu.SemaphoreType.DMA((4,)),
        ],
        compiler_params=params(26),
        cost_estimate=cost(6 * both * d * f, 25e6, 2 * both * f),
    )(idx, *a2s, *gs, stay(w1), stay(w2), rt)


def grads_kernel(zn, zf, gn, gf, an, af, dn, df, out, parts, sem):
    d = gn.shape[1]
    count, tall, _ = parts.shape
    half = count // 2

    @pl.loop(0, half)
    def _(j):
        here = pl.ds(pl.multiple_of(j * tall, LANES), tall)
        parts[j] = (tn(zn[:, here], gn[...]) + tn(zf[:, here], gf[...])).astype(BF16)
        pltpu.make_async_copy(parts.at[j], out.at[here], sem.at[j]).start()

    @pl.loop(half, count)
    def _(j):
        for n in range(tall // d):
            here = pl.ds(pl.multiple_of((j - half) * tall + n * d, LANES), d)
            grad = tn(an[...], dn[:, here]) + tn(af[...], df[:, here])
            parts[j, n * d : (n + 1) * d, :] = grad.astype(BF16)
        here = pl.ds(pl.multiple_of(j * tall, LANES), tall)
        pltpu.make_async_copy(parts.at[j], out.at[here], sem.at[j]).start()

    for j in range(count):
        pltpu.make_async_copy(parts.at[j], out.at[pl.ds(j * tall, tall)], sem.at[j]).wait()


def expert_grads(zn, zf, gn, gf, an, af, dn, df):
    both, f = zn.shape
    d = gn.shape[1]
    return pl.pallas_call(
        grads_kernel,
        out_shape=pltpu.HBM((2 * f, d), BF16),
        in_specs=[VMEM_SPEC] * 8,
        out_specs=FAR_SPEC,
        scratch_shapes=[
            pltpu.VMEM((4, f // 2, d), BF16),
            pltpu.SemaphoreType.DMA((4,)),
        ],
        compiler_params=params(16),
        cost_estimate=cost(8 * both * d * f, 25e6),
    )(zn, zf, gn, gf, an, af, dn, df)


def place_kernel(
    grads, gwo, gwi, gq, gk, gv, go, router, gain1, gain2,
    low, wide, low_pack, pack, in_sem, out_sem, pack_sem, back_sem,
):
    count, large, d = wide.shape
    small = low_pack.shape[1]
    rows = gq.shape[0]
    half, runs = count // 2, d // large
    loads, small_loads, stores = [], [], []
    for c in range(count):
        source = grads.at[c, pl.ds(large, small)]
        small_loads.append(pltpu.make_async_copy(source, low_pack.at[c], pack_sem.at[c]))
        source = grads.at[c, pl.ds(0, large)]
        loads.append(pltpu.make_async_copy(source, low.at[c], in_sem.at[c]))
        if c < half:
            target = gwo.at[0, pl.ds(c * large, large)]
        else:
            k = c - half
            target = gwi.at[0, pl.ds(k % runs * large, large), pl.ds(k // runs * d, d)]
        stores.append(pltpu.make_async_copy(wide.at[c], target, out_sem.at[c]))
    backs = [
        pltpu.make_async_copy(pack.at[pl.ds(n * rows, rows)], ref, back_sem.at[n])
        for n, ref in enumerate((gq, gk, gv, go))
    ]
    for copy in small_loads + loads:
        copy.start()
    for c in range(count):
        small_loads[c].wait()
        pack[c * small : (c + 1) * small, :] = low_pack[c].astype(F32)
    for copy in backs:
        copy.start()
    router[...] = pack[4 * rows : 4 * rows + 4, 0:rows]
    gain1[...] = pack[4 * rows + 4 : 4 * rows + 5, 0:rows]
    gain2[...] = pack[4 * rows + 5 : 4 * rows + 6, 0:rows]
    for c in range(count):
        loads[c].wait()
        wide[c] = low[c].astype(F32)
        stores[c].start()
    for copy in stores + backs:
        copy.wait()


def place(grads, f, rows):
    count, tall, d = grads.shape
    large = 2 * f // count
    small = tall - large
    return pl.pallas_call(
        place_kernel,
        out_shape=(
            pltpu.HBM((1, f, d), F32),
            pltpu.HBM((1, d, f), F32),
            *[pltpu.HBM((rows, d), F32)] * 4,
            jax.ShapeDtypeStruct((4, rows), F32),
            jax.ShapeDtypeStruct((1, rows), F32),
            jax.ShapeDtypeStruct((1, rows), F32),
        ),
        in_specs=[FAR_SPEC],
        out_specs=(*[FAR_SPEC] * 6, *[VMEM_SPEC] * 3),
        scratch_shapes=[
            pltpu.VMEM((count, large, d), BF16),
            pltpu.VMEM((count, large, d), F32),
            pltpu.VMEM((count, small, d), BF16),
            pltpu.VMEM((count * small, d), F32),
            pltpu.SemaphoreType.DMA((count,)),
            pltpu.SemaphoreType.DMA((count,)),
            pltpu.SemaphoreType.DMA((count,)),
            pltpu.SemaphoreType.DMA((4,)),
        ],
        compiler_params=params(40),
        cost_estimate=cost(1e6, 12e6),
    )(stay(grads))


def expert_out_kernel(zn, zf, w2_far, y0, y1, y2, y3, w2, near, far, sem):
    block = y0.shape[0]
    step = w2.shape[1]
    for j in range(w2.shape[0]):
        pltpu.make_async_copy(w2_far.at[pl.ds(j * step, step)], w2.at[j], sem.at[j]).start()
    near[...] = jnp.zeros(near.shape, F32)
    far[...] = jnp.zeros(far.shape, F32)

    @pl.loop(0, w2.shape[0])
    def _(j):
        here = pl.ds(pl.multiple_of(j * step, LANES), step)
        pltpu.make_async_copy(w2_far.at[here], w2.at[j], sem.at[j]).wait()
        near[...] += nn(zn[:, here], w2[j])
        far[...] += nn(zf[:, here], w2[j])

    y0[...] = near[0:block, :].astype(BF16)
    y1[...] = near[block:, :].astype(BF16)
    y2[...] = far[0:block, :].astype(BF16)
    y3[...] = far[block:, :].astype(BF16)


def expert_out(zn, zf, w2):
    both, f = zn.shape
    d = w2.shape[1]
    step = f // 4
    return pl.pallas_call(
        expert_out_kernel,
        out_shape=[jax.ShapeDtypeStruct((both // 2, d), BF16)] * 4,
        in_specs=[VMEM_SPEC] * 2 + [FAR_SPEC],
        out_specs=[VMEM_SPEC] * 4,
        scratch_shapes=[pltpu.VMEM((4, step, d), BF16)]
        + [pltpu.VMEM((both, d), F32)] * 2
        + [pltpu.SemaphoreType.DMA((4,))],
        compiler_params=params(24),
        cost_estimate=cost(4 * d * f * both, 16e6),
    )(zn, zf, stay(w2))


def attn_bwd_kernel(
    idx, tok, g, da0, da1, da2, h1, qkv, p, o, a1, wfull, rt, gra, grb,
    gtok, pack_send, pack_keep,
    da, dattn_all, dqkv, gains, grads, *, seq,
):
    i = pl.program_id(0)
    pad, d = tok.shape[1], tok.shape[2]
    rows = d // 4

    @pl.when(i == 0)
    def _():
        da[...] = da0[...].astype(F32) + da1[...].astype(F32) + da2[...].astype(F32)
        dattn_all[...] = jnp.zeros(dattn_all.shape, BF16)
        dqkv[...] = jnp.zeros(dqkv.shape, BF16)
        gains[...] = jnp.zeros(gains.shape, F32)

    here = pl.ds(pl.multiple_of(i * pad, TAIL), pad)
    valid = lax.broadcasted_iota(jnp.int32, (pad, 1), 0) < seq
    n2, r2 = norm_stats(h1[0])
    din = da[here, :]
    gains[1:2, :] += jnp.sum(din * n2, axis=0, keepdims=True)
    dh1 = g[here, :].astype(F32) + norm_back(din * rt[5:6, :], n2, r2)
    dattn = dh1.astype(BF16)
    dattn_all[here, :] = dattn
    do = nt(dattn, wfull[:, 3 * d : 4 * d]).astype(BF16)
    pairs = range(HEADS // 2)
    lanes = [slice(LANES * hp, LANES * (hp + 1)) for hp in pairs]
    klanes = [slice(d + LANES * hp, d + LANES * (hp + 1)) for hp in pairs]
    vlanes = [slice(2 * d + LANES * hp, 2 * d + LANES * (hp + 1)) for hp in pairs]
    do2 = [split_heads(do[:, lanes[hp]]) for hp in pairs]
    dp = [nt(do2[hp], qkv[0, :, vlanes[hp]]) for hp in pairs]
    for hp in pairs:
        dqkv[here, vlanes[hp]] = tn(p[0, hp], do2[hp])[0:pad].astype(BF16)
    wide = [p[0, hp].astype(F32) for hp in pairs]
    inner = [jnp.sum(dp[hp] * wide[hp], axis=-1, keepdims=True) for hp in pairs]
    ds = [(wide[hp] * (dp[hp] - inner[hp])).astype(BF16) for hp in pairs]
    for hp in pairs:
        dq = join_heads(nn(ds[hp], qkv[0, :, klanes[hp]]))
        dqkv[here, lanes[hp]] = (dq * HEAD_DIM**-0.5).astype(BF16)
        dk = tn(ds[hp], split_heads(qkv[0, 0:pad, lanes[hp]]))
        dqkv[here, klanes[hp]] = dk[0:pad].astype(BF16)
    din1 = nt(dqkv[here, :], wfull[:, 0 : 3 * d])
    x = jnp.where(valid, tok[0].astype(F32), 0.0)
    n1, r1 = norm_stats(x)
    gains[0:1, :] += jnp.sum(din1 * n1, axis=0, keepdims=True)
    gtok[0] = (dh1 + norm_back(din1 * rt[4:5, :], n1, r1)).astype(BF16)

    @pl.when(i == pl.num_programs(0) - 1)
    def _():
        grads[:, 0 : 3 * d] = tn(a1[...], dqkv[...]).astype(BF16)
        grads[:, 3 * d : 4 * d] = tn(o[...], dattn_all[...]).astype(BF16)
        row = lax.broadcasted_iota(jnp.int32, (TAIL, d), 0)
        tail = jnp.where(row < 4, gra[...] + grb[...], 0.0)
        tail = jnp.where(row == 4, gains[0:1, :], tail)
        gains[...] = jnp.where(row == 5, gains[1:2, :], tail)
        for n, (ref, slot) in enumerate(
            ((pack_keep, 0), (pack_send, 0), (pack_keep, 1), (pack_send, 1))
        ):
            at = pl.multiple_of(idx[n] * rows, rows)
            for m in range(4):
                ref[slot, m * rows : (m + 1) * rows, :] = grads[pl.ds(at, rows), m * d : (m + 1) * d]
            ref[slot, 4 * rows :, :] = jnp.zeros((ref.shape[1] - 4 * rows, d), BF16)
            ref[slot, 4 * rows : 4 * rows + TAIL, 0:rows] = gains[:, pl.ds(at, rows)].astype(BF16)


def attn_bwd(idx, tokens, g, das, h1, qkv, p, o, a1, wfull, rt, grs, seq, pad, pack_rows):
    images, _, d = tokens.shape
    block = a1.shape[0]
    keys = qkv.shape[1]
    image = lambda i: (i, 0, 0)
    return pl.pallas_call(
        functools.partial(attn_bwd_kernel, seq=seq),
        grid=(images,),
        out_shape=(
            jax.ShapeDtypeStruct(tokens.shape, BF16),
            jax.ShapeDtypeStruct((2, pack_rows, d), BF16),
            jax.ShapeDtypeStruct((2, pack_rows, d), BF16),
        ),
        in_specs=[SMEM_SPEC, pl.BlockSpec((1, pad, d), image), whole(g.shape)]
        + [whole((block, d)), VMEM_SPEC, VMEM_SPEC]
        + [
            pl.BlockSpec((1, pad, d), image),
            pl.BlockSpec((1, keys, 3 * d), image),
            pl.BlockSpec((1, HEADS // 2, 2 * pad, keys), lambda i: (i, 0, 0, 0)),
            whole((block, d)),
            whole((block, d)),
            whole((d, 4 * d)),
            whole((TAIL, d)),
            whole((TAIL, d)),
            whole((TAIL, d)),
        ],
        out_specs=(
            pl.BlockSpec((1, pad, d), image),
            whole((2, pack_rows, d)),
            whole((2, pack_rows, d)),
        ),
        scratch_shapes=[
            pltpu.VMEM((block, d), F32),
            pltpu.VMEM((block, d), BF16),
            pltpu.VMEM((block, 3 * d), BF16),
            pltpu.VMEM((TAIL, d), F32),
            pltpu.VMEM((d, 4 * d), BF16),
        ],
        compiler_params=params(40),
        cost_estimate=cost(LONG, 15e6),
    )(
        idx, stay(tokens), stay(g), stay(das[0]), *das[1:],
        *(stay(kept) for kept in (h1, qkv, p, o, a1, wfull)), rt, *grs,
    )


def output_kernel(h1, y0, y1, y2, ssq, out, sums, moe):
    i = pl.program_id(0)
    pad = h1.shape[1]

    @pl.when(i == 0)
    def _():
        moe[...] = y0[...].astype(F32) + y1[...].astype(F32) + y2[...].astype(F32)
        sums[...] = jnp.zeros(sums.shape, F32)
        sums[1:2, :] = fold_lanes(ssq[0:1, :])

    branch = moe[pl.ds(pl.multiple_of(i * pad, TAIL), pad), :]
    result = h1[0] + branch
    sums[0:1, :] += fold_lanes(jnp.sum(result * result, axis=0, keepdims=True))
    sums[2:3, :] += fold_lanes(jnp.sum(branch * branch, axis=0, keepdims=True))
    out[0] = result.astype(BF16)


def output(h1, ys, ssq, seq):
    images, pad, d = h1.shape
    block = ys[0].shape[0]
    return pl.pallas_call(
        output_kernel,
        grid=(images,),
        out_shape=(
            jax.ShapeDtypeStruct((images, seq, d), BF16),
            jax.ShapeDtypeStruct((8, LANES), F32),
        ),
        in_specs=[pl.BlockSpec((1, pad, d), lambda i: (i, 0, 0))] + [VMEM_SPEC] * 4,
        out_specs=(pl.BlockSpec((1, pad, d), lambda i: (i, 0, 0)), whole((8, LANES))),
        scratch_shapes=[pltpu.VMEM((block, d), F32)],
        compiler_params=params(16),
        cost_estimate=cost(10 * block * d, 5e6),
    )(stay(h1), *ys, ssq)


def scatter_rows(a, axes, groups):
    count = len(groups[0])
    parts = a.reshape(count, a.shape[0] // count, a.shape[1])
    return lax.all_to_all(parts, axes, 0, 0, tiled=True, axis_index_groups=groups)


def add_rows(parts):
    return jnp.sum(parts.astype(F32), axis=0).astype(BF16)


def local(
    tokens,
    cotangent,
    gain_one,
    w_query,
    w_key,
    w_value,
    w_output,
    gain_two,
    w_router,
    w_in,
    w_out,
    routes,
):
    images, seq, d = tokens.shape
    experts = lax.axis_size("shard")
    pad = round_up(seq, TAIL)
    keys = round_up(seq, LANES)
    block = round_up(images * pad, LANES)
    rows = w_query.shape[0]
    me = lax.axis_index("shard")
    reps = lax.axis_size("rep")
    everyone = ("shard", "rep")
    ring = [*range(0, reps, 2), *range(reps - 1, 0, -2)]
    rings = [[s * reps + r for r in ring] for s in range(experts)]
    idx = jnp.stack([me, me ^ 1, me ^ 2, me ^ 3]).astype(jnp.int32)
    core = lambda a: lax.ppermute(a, "shard", [(s, s ^ 1) for s in range(experts)])
    chip = lambda a: lax.ppermute(a, "shard", [(s, s ^ 2) for s in range(experts)])

    operands = (
        w_query, w_key, w_value, w_output,
        gain_one.reshape(1, rows), gain_two.reshape(1, rows), w_router.T,
    )
    wp = pl.pallas_call(
        pack_weights_kernel,
        grid=(1,),
        out_shape=pltpu.VMEM((rows + HEAD, 4 * d), BF16),
        in_specs=[whole(a.shape) for a in operands],
        out_specs=VMEM_SPEC,
        compiler_params=params(40),
        cost_estimate=cost(1e6, 3e6),
    )(*(stay(a) for a in operands))
    chosen = (routes[:, :, :, None] == jnp.arange(experts, dtype=jnp.int32)).any(axis=2)
    chosen = jnp.pad(chosen, ((0, 0), (0, pad - seq), (0, 0)))
    chosen = chosen.reshape(images * pad, experts).T
    chosen = jnp.pad(chosen, ((0, 0), (0, round_up(block, d) - images * pad)))
    chosen = chosen.reshape(experts, -1, d).transpose(1, 0, 2).reshape(-1, d)
    masks = jnp.pad(chosen, ((0, TAIL - chosen.shape[0]), (0, 0))).astype(BF16)
    gp = pl.pallas_call(
        functools.partial(pack_cotangent_kernel, seq=seq, pad=pad),
        grid=(1,),
        out_shape=jax.ShapeDtypeStruct((block + TAIL, d), BF16),
        in_specs=[whole(cotangent.shape), whole(masks.shape)],
        out_specs=whole((block + TAIL, d)),
        compiler_params=params(40),
        cost_estimate=cost(1e6, 1e6),
    )(stay(cotangent), masks)
    wx = after(chip(wp), gp)
    gx = chip(gp)
    packs = (wp, core(wp), wx, core(wx))
    gs = (gp, core(gp), gx, core(gx))
    w1, w2 = w_in[0], w_out[0]
    wfull, rt, qkv, p, o, a1, h1, a2, ssq = attn_fwd(
        idx, tokens, packs, seq, pad, keys, block
    )
    ax = chip(a2)
    zn, dun, da, dac, grn, an, gn = expert(
        idx, (a2, core(after(a2, gx))), gs[:2], w1, w2, rt, True
    )
    ax = after(ax, zn)
    zf, duf, dax, daxc, grf, af, gf = expert(
        idx, (ax, core(ax)), gs[2:], w1, w2, rt, False
    )
    da_far = dax + core(daxc)
    grads_part = expert_grads(zn, zf, after(gn, da_far), gf, an, af, dun, duf)
    grads_slice = lax.psum_scatter(
        grads_part, everyone, scatter_dimension=0, tiled=True, axis_index_groups=rings
    )
    grad_tokens, send, keep = attn_bwd(
        idx, tokens, gp, (da, core(dac), chip(da_far)), after(h1, grads_part),
        qkv, p, o, a1, wfull, rt, (grn, grf), seq, pad, round_up(4 * rows + TAIL, 8 * reps),
    )
    got = core(send)
    pack_far = keep[1] + got[1]
    y, yc, yx, yxc = expert_out(after(zn, pack_far), zf, w2)
    pack = (
        after(keep, y)[0].astype(F32) + got[0].astype(F32) + chip(pack_far).astype(F32)
    ).astype(BF16)
    y_far = after(yx, pack) + core(yxc)
    pack = scatter_rows(pack, everyone, rings)
    grads = jnp.concatenate([grads_slice, add_rows(pack)], axis=0)
    grads = lax.all_gather(grads, everyone, axis=0, axis_index_groups=rings)
    out, sums = output(h1, (y, core(yc), chip(y_far)), ssq, seq)
    sums = jnp.broadcast_to(after(sums, pack)[None], (experts * reps, *sums.shape))
    sums = lax.all_to_all(sums, everyone, 0, 0, tiled=True)
    totals = jnp.sum(sums, axis=(0, 2))
    gwo, gwi, gq, gk, gv, go, router, gain1, gain2 = place(grads, w1.shape[1], rows)
    roots = jnp.sqrt(totals / float(experts * reps * images * seq * d))
    return (
        out,
        grad_tokens,
        gain1.reshape(rows),
        gq,
        gk,
        gv,
        go,
        gain2.reshape(rows),
        router.T,
        gwi,
        gwo,
        roots[0],
        roots[1],
        roots[2],
    )


def solution(mesh):
    spread = P(("shard", "rep"), None, None)
    matrix = P("shard", None)
    stack = P("shard", None, None)
    vector = P("shard")
    return jax.shard_map(
        local,
        mesh=mesh,
        in_specs=(
            spread, spread, vector, matrix, matrix, matrix, matrix, vector, matrix, stack, stack, spread,
        ),
        out_specs=(
            spread, spread, vector, matrix, matrix, matrix, matrix, vector, matrix, stack, stack, P(), P(), P(),
        ),
        check_vma=False,
    )
```

```python
import functools

import jax
import jax.numpy as jnp
from jax import lax
from jax.experimental import pallas as pl
from jax.experimental.pallas import tpu as pltpu
from jax.sharding import PartitionSpec as P

HEADS = 8
HEAD_DIM = 64
EPSILON = 1e-06
LANES = 128
TAIL = 16
HEAD = 8
LONG = 1e11

BF16 = jnp.bfloat16
F32 = jnp.float32

LOG2E = 1.4426950408889634
ROOT_HALF = 0.7071067811865476
INV_ROOT_2PI = 0.3989422804014327


def round_up(value, multiple):
    return (value + multiple - 1) // multiple * multiple


def nn(a, b):
    return lax.dot_general(a, b, (((1,), (0,)), ((), ())), preferred_element_type=F32)


def nt(a, b):
    return lax.dot_general(a, b, (((1,), (1,)), ((), ())), preferred_element_type=F32)


def tn(a, b):
    return lax.dot_general(a, b, (((0,), (0,)), ((), ())), preferred_element_type=F32)


def norm_stats(values):
    center = values - jnp.mean(values, axis=-1, keepdims=True)
    inverse = lax.rsqrt(jnp.mean(center * center, axis=-1, keepdims=True) + EPSILON)
    return center * inverse, inverse


def norm_back(grad_normed, normed, inverse):
    mean_plain = jnp.mean(grad_normed, axis=-1, keepdims=True)
    mean_cross = jnp.mean(grad_normed * normed, axis=-1, keepdims=True)
    return inverse * (grad_normed - mean_plain - normed * mean_cross)


def gelu_pair(u):
    cdf = 0.5 * lax.erf(u * ROOT_HALF) + 0.5
    return u * cdf, cdf + u * (jnp.exp2(u * u * (-0.5 * LOG2E)) * INV_ROOT_2PI)


def split_heads(pair):
    low = lax.broadcasted_iota(jnp.int32, pair.shape, 1) < HEAD_DIM
    zero = jnp.zeros_like(pair)
    return jnp.concatenate([jnp.where(low, pair, zero), jnp.where(low, zero, pair)], axis=0)


def join_heads(stacked):
    rows = stacked.shape[0] // 2
    low = lax.broadcasted_iota(jnp.int32, (rows, stacked.shape[1]), 1) < HEAD_DIM
    return jnp.where(low, stacked[:rows], stacked[rows:])


def after(value, *first):
    return lax.optimization_barrier((value, *first))[0]


def stay(array):
    return pltpu.with_memory_space_constraint(array, pltpu.HBM)


def params(mebibytes=60):
    return pltpu.CompilerParams(vmem_limit_bytes=mebibytes * 1024 * 1024)


def cost(flops, nbytes, trans=0):
    return pl.CostEstimate(flops=int(flops), bytes_accessed=int(nbytes), transcendentals=int(trans))


def whole(shape):
    return pl.BlockSpec(shape, lambda *_: (0,) * len(shape))


SMEM_SPEC = pl.BlockSpec(memory_space=pltpu.SMEM)
VMEM_SPEC = pl.BlockSpec(memory_space=pltpu.VMEM)
FAR_SPEC = pl.BlockSpec(memory_space=pl.ANY)


def pack_weights_kernel(wq, wk, wv, wo, g1, g2, wr, wp):
    rows, d = wq.shape
    for n, w in enumerate((wq, wk, wv, wo)):
        wp[0:rows, n * d : (n + 1) * d] = w[...]
    blank = jnp.zeros((HEAD - wr.shape[0], LANES), F32)
    head = jnp.concatenate([wr[...].astype(F32), blank], axis=0)
    row = lax.broadcasted_iota(jnp.int32, (HEAD, LANES), 0)
    head = jnp.where(row == 4, g1[...].astype(F32), head)
    head = jnp.where(row == 5, g2[...].astype(F32), head)
    wp[rows:, :] = jnp.zeros((HEAD, wp.shape[1]), BF16)
    wp[rows:, 0:LANES] = head.astype(BF16)


def pack_cotangent_kernel(cot, masks, gp):
    seq = cot.shape[1]
    gp[...] = jnp.zeros(gp.shape, BF16)
    for i in range(cot.shape[0]):
        gp[i * seq : (i + 1) * seq, :] = cot[i]
    gp[gp.shape[0] - TAIL :, :] = masks[...]


def attn_fwd_kernel(
    idx, tok, w0, w1, w2, w3, wfull, rt, qkv, p, o, a1, h1, a2, ssq, *, seq, h1_images
):
    i = pl.program_id(0)
    pad, d = tok.shape[1], tok.shape[2]
    keys = qkv.shape[1]
    rows = w0.shape[0] - HEAD

    @pl.when(i == 0)
    def _():
        for n, w in enumerate((w0, w1, w2, w3)):
            at = pl.multiple_of(idx[n] * rows, rows)
            wfull[pl.ds(at, rows), :] = w[0:rows, :]
            rt[0:HEAD, pl.ds(at, rows)] = w[rows:, 0:rows].astype(F32)
            rt[HEAD:, pl.ds(at, rows)] = jnp.zeros((TAIL - HEAD, rows), F32)
        for ref in (o, a1, a2):
            ref[...] = jnp.zeros(ref.shape, ref.dtype)
        ssq[...] = jnp.zeros(ssq.shape, F32)

    here = pl.ds(pl.multiple_of(i * pad, TAIL), pad)
    valid = lax.broadcasted_iota(jnp.int32, (pad, 1), 0) < seq
    x = jnp.where(valid, tok[0].astype(F32), 0.0)
    n1, _ = norm_stats(x)
    in_one = (n1 * rt[4:5, :]).astype(BF16)
    a1[here, :] = in_one
    proj = nn(in_one, wfull[:, 0 : 3 * d])
    qkv[0, 0:pad, 0:d] = (proj[:, 0:d].astype(BF16).astype(F32) * HEAD_DIM**-0.5).astype(BF16)
    qkv[0, 0:pad, d:] = proj[:, d:].astype(BF16)
    qkv[0, pad:keys, :] = jnp.zeros((keys - pad, 3 * d), BF16)
    column = lax.broadcasted_iota(jnp.int32, (1, keys), 1) < seq
    pairs = range(HEADS // 2)
    lanes = [slice(LANES * hp, LANES * (hp + 1)) for hp in pairs]
    scores = [
        nt(split_heads(qkv[0, 0:pad, lanes[hp]]), qkv[0, :, d + LANES * hp : d + LANES * (hp + 1)])
        for hp in pairs
    ]
    scores = [jnp.where(column, score, -1e30) for score in scores]
    tops = [jnp.max(score, axis=-1, keepdims=True) for score in scores]
    raised = [jnp.exp(score - top) for score, top in zip(scores, tops)]
    totals = [1.0 / jnp.sum(each, axis=-1, keepdims=True) for each in raised]
    for hp in pairs:
        p[0, hp] = (raised[hp] * totals[hp]).astype(BF16)
    for hp in pairs:
        mixed = nn(p[0, hp], qkv[0, :, 2 * d + LANES * hp : 2 * d + LANES * (hp + 1)])
        o[here, lanes[hp]] = join_heads(mixed).astype(BF16)
    attn = jnp.where(valid, nn(o[here, :], wfull[:, 3 * d : 4 * d]), 0.0)
    ssq[0:1, :] += jnp.sum(attn * attn, axis=0, keepdims=True)
    after = x + attn
    h1[0] = after
    n2, _ = norm_stats(after)
    in_two = (n2 * rt[5:6, :]).astype(BF16)
    for n in range(h1_images):

        @pl.when(i == n)
        def _(n=n):
            a2[n * seq : (n + 1) * seq, :] = in_two[0:seq]


def attn_fwd(idx, tokens, packs, seq, pad, keys, block, padded):
    images, _, d = tokens.shape
    out_shape = (
        pltpu.HBM((d, 4 * d), BF16),
        jax.ShapeDtypeStruct((TAIL, d), F32),
        pltpu.HBM((images, keys, 3 * d), BF16),
        pltpu.HBM((images, HEADS // 2, 2 * pad, keys), BF16),
        pltpu.HBM((padded, d), BF16),
        pltpu.HBM((padded, d), BF16),
        pltpu.HBM((images, pad, d), F32),
        pltpu.VMEM((block, d), BF16),
        jax.ShapeDtypeStruct((8, d), F32),
    )
    return pl.pallas_call(
        functools.partial(attn_fwd_kernel, seq=seq, h1_images=images),
        grid=(images,),
        out_shape=out_shape,
        in_specs=[SMEM_SPEC, pl.BlockSpec((1, pad, d), lambda i: (i, 0, 0))]
        + [VMEM_SPEC] * 4,
        out_specs=(
            whole((d, 4 * d)),
            whole((TAIL, d)),
            pl.BlockSpec((1, keys, 3 * d), lambda i: (i, 0, 0)),
            pl.BlockSpec((1, HEADS // 2, 2 * pad, keys), lambda i: (i, 0, 0, 0)),
            whole((padded, d)),
            whole((padded, d)),
            pl.BlockSpec((1, pad, d), lambda i: (i, 0, 0)),
            VMEM_SPEC,
            whole((8, d)),
        ),
        compiler_params=params(40),
        cost_estimate=cost(1, 1),
    )(idx, stay(tokens), *packs)


def chosen_row(idx, ref, block, width):
    masks = ref[block:, :].astype(F32)
    d = masks.shape[1]
    row = lax.broadcasted_iota(jnp.int32, masks.shape, 0)
    parts = [
        jnp.sum(jnp.where(row == 4 * n + idx[0], masks, 0.0), axis=0, keepdims=True)
        for n in range((block + d - 1) // d)
    ]
    parts.append(jnp.zeros((1, width - d * len(parts)), F32))
    return jnp.concatenate(parts, axis=1)


def route(idx, a2s, rt, ga, gb, block):
    width = a2s.shape[0]
    row = lax.broadcasted_iota(jnp.int32, (TAIL, width), 0)
    logits = jnp.where(row < 4, nt(rt[...].astype(BF16), a2s[...]), -1e30)
    raised = jnp.exp(logits - jnp.max(logits, axis=0, keepdims=True))
    share = raised / jnp.sum(raised, axis=0, keepdims=True)
    chosen = chosen_row(idx, ga, block, width)
    chosen += pltpu.roll(chosen_row(idx, gb, block, width), block, 1)
    mine = jnp.sum(jnp.where(row == idx[0], share, 0.0), axis=0, keepdims=True)
    return jnp.where(row == HEAD, chosen * mine, share).T


def fold_lanes(wide):
    parts = [wide[:, n : n + LANES] for n in range(0, wide.shape[1], LANES)]
    return sum(parts[1:], parts[0])


def gather_rows(a2a, a2b, ga, gb, a2s, gs):
    block = a2a.shape[0]
    for ref, first, second in ((a2s, a2a, a2b), (gs, ga, gb)):
        ref[0:block, :] = first[0:block, :]
        ref[block : 2 * block, :] = second[0:block, :]
        ref[2 * block :, :] = jnp.zeros((ref.shape[0] - 2 * block, ref.shape[1]), BF16)


def finish_rows(idx, probs, dcomb, total, a2s, rt, da, db, gr):
    block = da.shape[0]
    lane = lax.broadcasted_iota(jnp.int32, probs.shape, 1)
    own = (lane == idx[0]).astype(F32)
    inner = jnp.sum(dcomb[...], axis=1, keepdims=True)
    dlogits = jnp.where(lane < 4, inner * (own - probs[...]), 0.0).astype(BF16)
    gr[...] = tn(dlogits, a2s[...])
    result = (total[...] + nn(dlogits[0 : 2 * block], rt[...].astype(BF16))).astype(BF16)
    da[...] = result[0:block]
    db[...] = result[block:]


def expert_kernel(
    idx, a2a, a2b, ga, gb, w1_far, w2_far, rt,
    zc, du, da, db, gr, a2s, gs, w1, w2, probs, dcomb, total, sem1, sem2,
):
    block = a2a.shape[0]
    step = w1.shape[2]
    loads = []
    for j in range(w1.shape[0]):
        here = pl.ds(j * step, step)
        loads.append(pltpu.make_async_copy(w1_far.at[:, here], w1.at[j], sem1.at[j]))
        loads.append(pltpu.make_async_copy(w2_far.at[here], w2.at[j], sem2.at[j]))
    for copy in loads:
        copy.start()
    gather_rows(a2a, a2b, ga, gb, a2s, gs)
    probs[...] = route(idx, a2s, rt, ga, gb, block)
    total[...] = jnp.zeros(total.shape, F32)
    dcomb[...] = jnp.zeros(dcomb.shape, F32)
    for ref in (zc, du):
        ref[2 * block :, :] = jnp.zeros((ref.shape[0] - 2 * block, ref.shape[1]), BF16)

    @pl.loop(0, w1.shape[0])
    def _(j):
        here = pl.ds(pl.multiple_of(j * step, LANES), step)
        pltpu.make_async_copy(w1_far.at[:, here], w1.at[j], sem1.at[j]).wait()
        pltpu.make_async_copy(w2_far.at[here], w2.at[j], sem2.at[j]).wait()
        halves = [slice(0, block), slice(block, 2 * block)]
        us = [nn(a2s[r, :], w1[j]) for r in halves]
        dzs = [nt(gs[r, :], w2[j]) for r in halves]
        for r, u, dz in zip(halves, us, dzs):
            act, slope = gelu_pair(u)
            scale = probs[r, HEAD : HEAD + 1]
            mixed = (act * scale).astype(BF16)
            zc[r, here] = mixed
            dcomb[r, :] += fold_lanes(mixed.astype(F32) * dz)
            grad = (slope * scale * dz).astype(BF16)
            du[r, here] = grad
            total[r, :] += nt(grad, w1[j])

    finish_rows(idx, probs, dcomb, total, a2s, rt, da, db, gr)


def expert(idx, a2s, gs, w1, w2, rt, near):
    block, d = a2s[0].shape
    f = w1.shape[1]
    both = 2 * block
    rows = round_up(both, 2 * LANES)
    step = f // 4
    return pl.pallas_call(
        expert_kernel,
        out_shape=(
            pltpu.VMEM((rows, f), BF16),
            pltpu.VMEM((rows, f), BF16),
            pltpu.HBM((block, d), BF16) if near else pltpu.VMEM((block, d), BF16),
            pltpu.VMEM((block, d), BF16),
            jax.ShapeDtypeStruct((TAIL, d), F32),
            pltpu.VMEM((rows, d), BF16),
            pltpu.VMEM((rows, d), BF16),
        ),
        in_specs=[SMEM_SPEC] + [VMEM_SPEC] * 4 + [FAR_SPEC] * 2 + [VMEM_SPEC],
        out_specs=(VMEM_SPEC,) * 2
        + (pl.BlockSpec((block, d), lambda: (0, 0)) if near else VMEM_SPEC,)
        + (VMEM_SPEC,) * 4,
        scratch_shapes=[
            pltpu.VMEM((4, d, step), BF16),
            pltpu.VMEM((4, step, d), BF16),
            pltpu.VMEM((rows, TAIL), F32),
            pltpu.VMEM((rows, LANES), F32),
            pltpu.VMEM((both, d), F32),
            pltpu.SemaphoreType.DMA((4,)),
            pltpu.SemaphoreType.DMA((4,)),
        ],
        compiler_params=params(26),
        cost_estimate=cost(6 * both * d * f, 25e6, 2 * both * f),
    )(idx, *a2s, *gs, stay(w1), stay(w2), rt)


def grads_kernel(zn, zf, gn, gf, an, af, dn, df, out, parts, sem):
    d = gn.shape[1]
    count, tall, _ = parts.shape
    half = count // 2

    @pl.loop(0, half)
    def _(j):
        here = pl.ds(pl.multiple_of(j * tall, LANES), tall)
        parts[j] = (tn(zn[:, here], gn[...]) + tn(zf[:, here], gf[...])).astype(BF16)
        pltpu.make_async_copy(parts.at[j], out.at[here], sem.at[j]).start()

    @pl.loop(half, count)
    def _(j):
        for n in range(tall // d):
            here = pl.ds(pl.multiple_of((j - half) * tall + n * d, LANES), d)
            grad = tn(an[...], dn[:, here]) + tn(af[...], df[:, here])
            parts[j, n * d : (n + 1) * d, :] = grad.astype(BF16)
        here = pl.ds(pl.multiple_of(j * tall, LANES), tall)
        pltpu.make_async_copy(parts.at[j], out.at[here], sem.at[j]).start()

    for j in range(count):
        pltpu.make_async_copy(parts.at[j], out.at[pl.ds(j * tall, tall)], sem.at[j]).wait()


def expert_grads(zn, zf, gn, gf, an, af, dn, df):
    both, f = zn.shape
    d = gn.shape[1]
    return pl.pallas_call(
        grads_kernel,
        out_shape=pltpu.HBM((2 * f, d), BF16),
        in_specs=[VMEM_SPEC] * 8,
        out_specs=FAR_SPEC,
        scratch_shapes=[
            pltpu.VMEM((4, f // 2, d), BF16),
            pltpu.SemaphoreType.DMA((4,)),
        ],
        compiler_params=params(16),
        cost_estimate=cost(8 * both * d * f, 25e6),
    )(zn, zf, gn, gf, an, af, dn, df)


def place_kernel(
    grads, gwo, gwi, gq, gk, gv, go, router, gain1, gain2,
    low, wide, pack, in_sem, out_sem, back_sem,
):
    count, large, d = wide.shape
    small = low.shape[1] - large
    rows = gq.shape[0]
    half, runs = count // 2, d // large
    loads, stores = [], []
    for c in range(count):
        loads.append(pltpu.make_async_copy(grads.at[c], low.at[c], in_sem.at[c]))
        if c < half:
            target = gwo.at[0, pl.ds(c * large, large)]
        else:
            k = c - half
            target = gwi.at[0, pl.ds(k % runs * large, large), pl.ds(k // runs * d, d)]
        stores.append(pltpu.make_async_copy(wide.at[c], target, out_sem.at[c]))
    backs = [
        pltpu.make_async_copy(pack.at[pl.ds(n * rows, rows)], ref, back_sem.at[n])
        for n, ref in enumerate((gq, gk, gv, go))
    ]
    for copy in loads:
        copy.start()
    for c in range(count):
        loads[c].wait()
        wide[c] = low[c, 0:large, :].astype(F32)
        stores[c].start()
    for c in range(count):
        pack[c * small : (c + 1) * small, :] = low[c, large:, :].astype(F32)
    for copy in backs:
        copy.start()
    router[...] = pack[4 * rows : 4 * rows + 4, 0:rows]
    gain1[...] = pack[4 * rows + 4 : 4 * rows + 5, 0:rows]
    gain2[...] = pack[4 * rows + 5 : 4 * rows + 6, 0:rows]
    for copy in stores + backs:
        copy.wait()


def place(grads, f, rows):
    count, tall, d = grads.shape
    large = 2 * f // count
    small = tall - large
    return pl.pallas_call(
        place_kernel,
        out_shape=(
            pltpu.HBM((1, f, d), F32),
            pltpu.HBM((1, d, f), F32),
            *[pltpu.HBM((rows, d), F32)] * 4,
            jax.ShapeDtypeStruct((4, rows), F32),
            jax.ShapeDtypeStruct((1, rows), F32),
            jax.ShapeDtypeStruct((1, rows), F32),
        ),
        in_specs=[FAR_SPEC],
        out_specs=(*[FAR_SPEC] * 6, *[VMEM_SPEC] * 3),
        scratch_shapes=[
            pltpu.VMEM((count, tall, d), BF16),
            pltpu.VMEM((count, large, d), F32),
            pltpu.VMEM((count * small, d), F32),
            pltpu.SemaphoreType.DMA((count,)),
            pltpu.SemaphoreType.DMA((count,)),
            pltpu.SemaphoreType.DMA((4,)),
        ],
        compiler_params=params(40),
        cost_estimate=cost(1e6, 12e6),
    )(stay(grads))


def expert_out_kernel(zn, zf, w2_far, y0, y1, y2, y3, w2, near, far, sem):
    block = y0.shape[0]
    step = w2.shape[1]
    for j in range(w2.shape[0]):
        pltpu.make_async_copy(w2_far.at[pl.ds(j * step, step)], w2.at[j], sem.at[j]).start()
    near[...] = jnp.zeros(near.shape, F32)
    far[...] = jnp.zeros(far.shape, F32)

    @pl.loop(0, w2.shape[0])
    def _(j):
        here = pl.ds(pl.multiple_of(j * step, LANES), step)
        pltpu.make_async_copy(w2_far.at[here], w2.at[j], sem.at[j]).wait()
        near[...] += nn(zn[0 : 2 * block, here], w2[j])
        far[...] += nn(zf[0 : 2 * block, here], w2[j])

    y0[...] = near[0:block, :].astype(BF16)
    y1[...] = near[block:, :].astype(BF16)
    y2[...] = far[0:block, :].astype(BF16)
    y3[...] = far[block:, :].astype(BF16)


def expert_out(zn, zf, w2, block):
    both, f = 2 * block, zn.shape[1]
    d = w2.shape[1]
    step = f // 4
    return pl.pallas_call(
        expert_out_kernel,
        out_shape=[jax.ShapeDtypeStruct((both // 2, d), BF16)] * 4,
        in_specs=[VMEM_SPEC] * 2 + [FAR_SPEC],
        out_specs=[VMEM_SPEC] * 4,
        scratch_shapes=[pltpu.VMEM((4, step, d), BF16)]
        + [pltpu.VMEM((both, d), F32)] * 2
        + [pltpu.SemaphoreType.DMA((4,))],
        compiler_params=params(24),
        cost_estimate=cost(4 * d * f * both, 16e6),
    )(zn, zf, stay(w2))


def unpack_rows(dense, spread, seq, pad):
    spread[...] = jnp.zeros(spread.shape, F32)
    for n in range(dense.shape[0] // seq):
        spread[n * pad : n * pad + seq, :] = dense[n * seq : (n + 1) * seq, :]


def attn_bwd_kernel(
    idx, tok, g, da0, da1, da2, h1, qkv, p, o, a1, wfull, rt, gra, grb,
    gtok, pack_send, pack_keep,
    flat, da, gpad, dattn_all, dqkv, gains, grads, *, seq,
):
    i = pl.program_id(0)
    pad, d = tok.shape[1], tok.shape[2]
    rows = d // 4

    @pl.when(i == 0)
    def _():
        flat[...] = da0[...].astype(F32) + da1[...].astype(F32) + da2[...].astype(F32)
        unpack_rows(flat, da, seq, pad)
        flat[...] = g[0 : flat.shape[0], :].astype(F32)
        unpack_rows(flat, gpad, seq, pad)
        dattn_all[...] = jnp.zeros(dattn_all.shape, BF16)
        dqkv[...] = jnp.zeros(dqkv.shape, BF16)
        gains[...] = jnp.zeros(gains.shape, F32)

    here = pl.ds(pl.multiple_of(i * pad, TAIL), pad)
    valid = lax.broadcasted_iota(jnp.int32, (pad, 1), 0) < seq
    n2, r2 = norm_stats(h1[0])
    din = da[here, :]
    gains[1:2, :] += jnp.sum(din * n2, axis=0, keepdims=True)
    dh1 = gpad[here, :] + norm_back(din * rt[5:6, :], n2, r2)
    dattn = dh1.astype(BF16)
    dattn_all[here, :] = dattn
    do = nt(dattn, wfull[:, 3 * d : 4 * d]).astype(BF16)
    pairs = range(HEADS // 2)
    lanes = [slice(LANES * hp, LANES * (hp + 1)) for hp in pairs]
    klanes = [slice(d + LANES * hp, d + LANES * (hp + 1)) for hp in pairs]
    vlanes = [slice(2 * d + LANES * hp, 2 * d + LANES * (hp + 1)) for hp in pairs]
    do2 = [split_heads(do[:, lanes[hp]]) for hp in pairs]
    dp = [nt(do2[hp], qkv[0, :, vlanes[hp]]) for hp in pairs]
    for hp in pairs:
        dqkv[here, vlanes[hp]] = tn(p[0, hp], do2[hp])[0:pad].astype(BF16)
    wide = [p[0, hp].astype(F32) for hp in pairs]
    inner = [jnp.sum(dp[hp] * wide[hp], axis=-1, keepdims=True) for hp in pairs]
    ds = [(wide[hp] * (dp[hp] - inner[hp])).astype(BF16) for hp in pairs]
    for hp in pairs:
        dq = join_heads(nn(ds[hp], qkv[0, :, klanes[hp]]))
        dqkv[here, lanes[hp]] = (dq * HEAD_DIM**-0.5).astype(BF16)
        dk = tn(ds[hp], split_heads(qkv[0, 0:pad, lanes[hp]]))
        dqkv[here, klanes[hp]] = dk[0:pad].astype(BF16)
    din1 = nt(dqkv[here, :], wfull[:, 0 : 3 * d])
    x = jnp.where(valid, tok[0].astype(F32), 0.0)
    n1, r1 = norm_stats(x)
    gains[0:1, :] += jnp.sum(din1 * n1, axis=0, keepdims=True)
    gtok[0] = (dh1 + norm_back(din1 * rt[4:5, :], n1, r1)).astype(BF16)

    @pl.when(i == pl.num_programs(0) - 1)
    def _():
        grads[:, 0 : 3 * d] = tn(a1[...], dqkv[...]).astype(BF16)
        grads[:, 3 * d : 4 * d] = tn(o[...], dattn_all[...]).astype(BF16)
        row = lax.broadcasted_iota(jnp.int32, (TAIL, d), 0)
        tail = jnp.where(row < 4, gra[...] + grb[...], 0.0)
        tail = jnp.where(row == 4, gains[0:1, :], tail)
        gains[...] = jnp.where(row == 5, gains[1:2, :], tail)
        for n, (ref, slot) in enumerate(
            ((pack_keep, 0), (pack_send, 0), (pack_keep, 1), (pack_send, 1))
        ):
            at = pl.multiple_of(idx[n] * rows, rows)
            for m in range(4):
                ref[slot, m * rows : (m + 1) * rows, :] = grads[pl.ds(at, rows), m * d : (m + 1) * d]
            ref[slot, 4 * rows :, :] = jnp.zeros((ref.shape[1] - 4 * rows, d), BF16)
            ref[slot, 4 * rows : 4 * rows + TAIL, 0:rows] = gains[:, pl.ds(at, rows)].astype(BF16)


def attn_bwd(idx, tokens, g, das, h1, qkv, p, o, a1, wfull, rt, grs, seq, pad, pack_rows):
    images, _, d = tokens.shape
    block, padded = das[0].shape[0], a1.shape[0]
    keys = qkv.shape[1]
    image = lambda i: (i, 0, 0)
    return pl.pallas_call(
        functools.partial(attn_bwd_kernel, seq=seq),
        grid=(images,),
        out_shape=(
            jax.ShapeDtypeStruct(tokens.shape, BF16),
            jax.ShapeDtypeStruct((2, pack_rows, d), BF16),
            jax.ShapeDtypeStruct((2, pack_rows, d), BF16),
        ),
        in_specs=[SMEM_SPEC, pl.BlockSpec((1, pad, d), image), whole(g.shape)]
        + [whole((block, d)), VMEM_SPEC, VMEM_SPEC]
        + [
            pl.BlockSpec((1, pad, d), image),
            pl.BlockSpec((1, keys, 3 * d), image),
            pl.BlockSpec((1, HEADS // 2, 2 * pad, keys), lambda i: (i, 0, 0, 0)),
            whole((padded, d)),
            whole((padded, d)),
            whole((d, 4 * d)),
            whole((TAIL, d)),
            whole((TAIL, d)),
            whole((TAIL, d)),
        ],
        out_specs=(
            pl.BlockSpec((1, pad, d), image),
            whole((2, pack_rows, d)),
            whole((2, pack_rows, d)),
        ),
        scratch_shapes=[
            pltpu.VMEM((block, d), F32),
            pltpu.VMEM((padded, d), F32),
            pltpu.VMEM((padded, d), F32),
            pltpu.VMEM((padded, d), BF16),
            pltpu.VMEM((padded, 3 * d), BF16),
            pltpu.VMEM((TAIL, d), F32),
            pltpu.VMEM((d, 4 * d), BF16),
        ],
        compiler_params=params(40),
        cost_estimate=cost(LONG, 15e6),
    )(
        idx, stay(tokens), stay(g), stay(das[0]), *das[1:],
        *(stay(kept) for kept in (h1, qkv, p, o, a1, wfull)), rt, *grs,
    )


def output_kernel(h1, y0, y1, y2, ssq, out, sums, flat, moe, *, seq):
    i = pl.program_id(0)
    pad = h1.shape[1]

    @pl.when(i == 0)
    def _():
        flat[...] = y0[...].astype(F32) + y1[...].astype(F32) + y2[...].astype(F32)
        unpack_rows(flat, moe, seq, pad)
        sums[...] = jnp.zeros(sums.shape, F32)
        sums[1:2, :] = fold_lanes(ssq[0:1, :])

    branch = moe[pl.ds(pl.multiple_of(i * pad, TAIL), pad), :]
    result = h1[0] + branch
    sums[0:1, :] += fold_lanes(jnp.sum(result * result, axis=0, keepdims=True))
    sums[2:3, :] += fold_lanes(jnp.sum(branch * branch, axis=0, keepdims=True))
    out[0] = result.astype(BF16)


def output(h1, ys, ssq, seq):
    images, pad, d = h1.shape
    block = ys[0].shape[0]
    return pl.pallas_call(
        functools.partial(output_kernel, seq=seq),
        grid=(images,),
        out_shape=(
            jax.ShapeDtypeStruct((images, seq, d), BF16),
            jax.ShapeDtypeStruct((8, LANES), F32),
        ),
        in_specs=[pl.BlockSpec((1, pad, d), lambda i: (i, 0, 0))] + [VMEM_SPEC] * 4,
        out_specs=(pl.BlockSpec((1, pad, d), lambda i: (i, 0, 0)), whole((8, LANES))),
        scratch_shapes=[pltpu.VMEM((block, d), F32), pltpu.VMEM((images * pad, d), F32)],
        compiler_params=params(16),
        cost_estimate=cost(10 * block * d, 5e6),
    )(stay(h1), *ys, ssq)


def scatter_rows(a, axes, groups):
    count = len(groups[0])
    parts = a.reshape(count, a.shape[0] // count, a.shape[1])
    return lax.all_to_all(parts, axes, 0, 0, tiled=True, axis_index_groups=groups)


def add_rows(parts):
    return jnp.sum(parts.astype(F32), axis=0).astype(BF16)


def local(
    tokens,
    cotangent,
    gain_one,
    w_query,
    w_key,
    w_value,
    w_output,
    gain_two,
    w_router,
    w_in,
    w_out,
    routes,
):
    images, seq, d = tokens.shape
    experts = lax.axis_size("shard")
    pad = round_up(seq, TAIL)
    keys = round_up(seq, LANES)
    block = round_up(images * seq, TAIL)
    padded = round_up(images * pad, LANES)
    rows = w_query.shape[0]
    me = lax.axis_index("shard")
    reps = lax.axis_size("rep")
    everyone = ("shard", "rep")
    ring = [*range(0, reps, 2), *range(reps - 1, 0, -2)]
    rings = [[s * reps + r for r in ring] for s in range(experts)]
    idx = jnp.stack([me, me ^ 1, me ^ 2, me ^ 3]).astype(jnp.int32)
    core = lambda a: lax.ppermute(a, "shard", [(s, s ^ 1) for s in range(experts)])
    chip = lambda a: lax.ppermute(a, "shard", [(s, s ^ 2) for s in range(experts)])

    operands = (
        w_query, w_key, w_value, w_output,
        gain_one.reshape(1, rows), gain_two.reshape(1, rows), w_router.T,
    )
    wp = pl.pallas_call(
        pack_weights_kernel,
        grid=(1,),
        out_shape=pltpu.VMEM((rows + HEAD, 4 * d), BF16),
        in_specs=[whole(a.shape) for a in operands],
        out_specs=VMEM_SPEC,
        compiler_params=params(40),
        cost_estimate=cost(1e6, 3e6),
    )(*(stay(a) for a in operands))
    chosen = (routes[:, :, :, None] == jnp.arange(experts, dtype=jnp.int32)).any(axis=2)
    chosen = chosen.reshape(images * seq, experts).T
    chosen = jnp.pad(chosen, ((0, 0), (0, round_up(block, d) - images * seq)))
    chosen = chosen.reshape(experts, -1, d).transpose(1, 0, 2).reshape(-1, d)
    masks = jnp.pad(chosen, ((0, TAIL - chosen.shape[0]), (0, 0))).astype(BF16)
    gp = pl.pallas_call(
        pack_cotangent_kernel,
        grid=(1,),
        out_shape=jax.ShapeDtypeStruct((block + TAIL, d), BF16),
        in_specs=[whole(cotangent.shape), whole(masks.shape)],
        out_specs=whole((block + TAIL, d)),
        compiler_params=params(40),
        cost_estimate=cost(1e6, 1e6),
    )(stay(cotangent), masks)
    wx = after(chip(wp), gp)
    gx = chip(gp)
    packs = (wp, core(wp), wx, core(wx))
    gs = (gp, core(gp), gx, core(gx))
    w1, w2 = w_in[0], w_out[0]
    wfull, rt, qkv, p, o, a1, h1, a2, ssq = attn_fwd(
        idx, tokens, packs, seq, pad, keys, block, padded
    )
    ax = chip(a2)
    zn, dun, da, dac, grn, an, gn = expert(
        idx, (a2, core(after(a2, gx))), gs[:2], w1, w2, rt, True
    )
    ax = after(ax, zn)
    zf, duf, dax, daxc, grf, af, gf = expert(
        idx, (ax, core(ax)), gs[2:], w1, w2, rt, False
    )
    da_far = dax + core(daxc)
    grads_part = expert_grads(zn, zf, after(gn, da_far), gf, an, af, dun, duf)
    grads_slice = lax.psum_scatter(
        grads_part, everyone, scatter_dimension=0, tiled=True, axis_index_groups=rings
    )
    grad_tokens, send, keep = attn_bwd(
        idx, tokens, gp, (da, core(dac), chip(da_far)), after(h1, grads_part),
        qkv, p, o, a1, wfull, rt, (grn, grf), seq, pad, round_up(4 * rows + TAIL, 8 * reps),
    )
    got = core(send)
    pack_far = keep[1] + got[1]
    y, yc, yx, yxc = expert_out(after(zn, pack_far), zf, w2, block)
    pack = (
        after(keep, y)[0].astype(F32) + got[0].astype(F32) + chip(pack_far).astype(F32)
    ).astype(BF16)
    y_far = after(yx, pack) + core(yxc)
    pack = scatter_rows(pack, everyone, rings)
    grads = jnp.concatenate([grads_slice, add_rows(pack)], axis=0)
    grads = lax.all_gather(grads, everyone, axis=0, axis_index_groups=rings)
    out, sums = output(h1, (y, core(yc), chip(y_far)), ssq, seq)
    sums = jnp.broadcast_to(after(sums, pack)[None], (experts * reps, *sums.shape))
    sums = lax.all_to_all(sums, everyone, 0, 0, tiled=True)
    totals = jnp.sum(sums, axis=(0, 2))
    gwo, gwi, gq, gk, gv, go, router, gain1, gain2 = place(grads, w1.shape[1], rows)
    roots = jnp.sqrt(totals / float(experts * reps * images * seq * d))
    return (
        out,
        grad_tokens,
        gain1.reshape(rows),
        gq,
        gk,
        gv,
        go,
        gain2.reshape(rows),
        router.T,
        gwi,
        gwo,
        roots[0],
        roots[1],
        roots[2],
    )


def solution(mesh):
    spread = P(("shard", "rep"), None, None)
    matrix = P("shard", None)
    stack = P("shard", None, None)
    vector = P("shard")
    return jax.shard_map(
        local,
        mesh=mesh,
        in_specs=(
            spread, spread, vector, matrix, matrix, matrix, matrix, vector, matrix, stack, stack, spread,
        ),
        out_specs=(
            spread, spread, vector, matrix, matrix, matrix, matrix, vector, matrix, stack, stack, P(), P(), P(),
        ),
        check_vma=False,
    )
```

```python
import functools

import jax
import jax.numpy as jnp
from jax import lax
from jax.experimental import pallas as pl
from jax.experimental.pallas import tpu as pltpu
from jax.sharding import PartitionSpec as P

HEADS = 8
HEAD_DIM = 64
EPSILON = 1e-06
LANES = 128
TAIL = 16
HEAD = 8
LONG = 1e11

BF16 = jnp.bfloat16
F32 = jnp.float32

LOG2E = 1.4426950408889634
ROOT_HALF = 0.7071067811865476
INV_ROOT_2PI = 0.3989422804014327


def round_up(value, multiple):
    return (value + multiple - 1) // multiple * multiple


def nn(a, b):
    return lax.dot_general(a, b, (((1,), (0,)), ((), ())), preferred_element_type=F32)


def nt(a, b):
    return lax.dot_general(a, b, (((1,), (1,)), ((), ())), preferred_element_type=F32)


def tn(a, b):
    return lax.dot_general(a, b, (((0,), (0,)), ((), ())), preferred_element_type=F32)


def norm_stats(values):
    center = values - jnp.mean(values, axis=-1, keepdims=True)
    inverse = lax.rsqrt(jnp.mean(center * center, axis=-1, keepdims=True) + EPSILON)
    return center * inverse, inverse


def norm_back(grad_normed, normed, inverse):
    mean_plain = jnp.mean(grad_normed, axis=-1, keepdims=True)
    mean_cross = jnp.mean(grad_normed * normed, axis=-1, keepdims=True)
    return inverse * (grad_normed - mean_plain - normed * mean_cross)


def gelu_pair(u):
    cdf = 0.5 * lax.erf(u * ROOT_HALF) + 0.5
    return u * cdf, cdf + u * (jnp.exp2(u * u * (-0.5 * LOG2E)) * INV_ROOT_2PI)


def split_heads(pair):
    low = lax.broadcasted_iota(jnp.int32, pair.shape, 1) < HEAD_DIM
    zero = jnp.zeros_like(pair)
    return jnp.concatenate([jnp.where(low, pair, zero), jnp.where(low, zero, pair)], axis=0)


def join_heads(stacked):
    rows = stacked.shape[0] // 2
    low = lax.broadcasted_iota(jnp.int32, (rows, stacked.shape[1]), 1) < HEAD_DIM
    return jnp.where(low, stacked[:rows], stacked[rows:])


def after(value, *first):
    return lax.optimization_barrier((value, *first))[0]


def stay(array):
    return pltpu.with_memory_space_constraint(array, pltpu.HBM)


def params(mebibytes=60):
    return pltpu.CompilerParams(vmem_limit_bytes=mebibytes * 1024 * 1024)


def cost(flops, nbytes, trans=0):
    return pl.CostEstimate(flops=int(flops), bytes_accessed=int(nbytes), transcendentals=int(trans))


def whole(shape):
    return pl.BlockSpec(shape, lambda *_: (0,) * len(shape))


SMEM_SPEC = pl.BlockSpec(memory_space=pltpu.SMEM)
VMEM_SPEC = pl.BlockSpec(memory_space=pltpu.VMEM)
FAR_SPEC = pl.BlockSpec(memory_space=pl.ANY)


def pack_weights_kernel(wq, wk, wv, wo, g1, g2, wr, wp):
    rows, d = wq.shape
    for n, w in enumerate((wq, wk, wv, wo)):
        wp[0:rows, n * d : (n + 1) * d] = w[...]
    blank = jnp.zeros((HEAD - wr.shape[0], LANES), F32)
    head = jnp.concatenate([wr[...].astype(F32), blank], axis=0)
    row = lax.broadcasted_iota(jnp.int32, (HEAD, LANES), 0)
    head = jnp.where(row == 4, g1[...].astype(F32), head)
    head = jnp.where(row == 5, g2[...].astype(F32), head)
    wp[rows:, :] = jnp.zeros((HEAD, wp.shape[1]), BF16)
    wp[rows:, 0:LANES] = head.astype(BF16)


def pack_cotangent_kernel(cot, masks, gp):
    seq = cot.shape[1]
    gp[...] = jnp.zeros(gp.shape, BF16)
    for i in range(cot.shape[0]):
        gp[i * seq : (i + 1) * seq, :] = cot[i]
    gp[gp.shape[0] - TAIL :, :] = masks[...]


def attn_fwd_kernel(
    idx, tok, w0, w1, w2, w3, wfull, rt, qkv, p, o, a1, h1, a2, ssq, *, seq, h1_images
):
    i = pl.program_id(0)
    pad, d = tok.shape[1], tok.shape[2]
    keys = qkv.shape[1]
    rows = w0.shape[0] - HEAD

    @pl.when(i == 0)
    def _():
        for n, w in enumerate((w0, w1, w2, w3)):
            at = pl.multiple_of(idx[n] * rows, rows)
            wfull[pl.ds(at, rows), :] = w[0:rows, :]
            rt[0:HEAD, pl.ds(at, rows)] = w[rows:, 0:rows].astype(F32)
            rt[HEAD:, pl.ds(at, rows)] = jnp.zeros((TAIL - HEAD, rows), F32)
        for ref in (o, a1, a2):
            ref[...] = jnp.zeros(ref.shape, ref.dtype)
        ssq[...] = jnp.zeros(ssq.shape, F32)

    here = pl.ds(pl.multiple_of(i * pad, TAIL), pad)
    valid = lax.broadcasted_iota(jnp.int32, (pad, 1), 0) < seq
    x = jnp.where(valid, tok[0].astype(F32), 0.0)
    n1, _ = norm_stats(x)
    in_one = (n1 * rt[4:5, :]).astype(BF16)
    a1[here, :] = in_one
    proj = nn(in_one, wfull[:, 0 : 3 * d])
    qkv[0, 0:pad, 0:d] = (proj[:, 0:d].astype(BF16).astype(F32) * HEAD_DIM**-0.5).astype(BF16)
    qkv[0, 0:pad, d:] = proj[:, d:].astype(BF16)
    qkv[0, pad:keys, :] = jnp.zeros((keys - pad, 3 * d), BF16)
    column = lax.broadcasted_iota(jnp.int32, (1, keys), 1) < seq
    pairs = range(HEADS // 2)
    lanes = [slice(LANES * hp, LANES * (hp + 1)) for hp in pairs]
    scores = [
        nt(split_heads(qkv[0, 0:pad, lanes[hp]]), qkv[0, :, d + LANES * hp : d + LANES * (hp + 1)])
        for hp in pairs
    ]
    scores = [jnp.where(column, score, -1e30) for score in scores]
    tops = [jnp.max(score, axis=-1, keepdims=True) for score in scores]
    raised = [jnp.exp(score - top) for score, top in zip(scores, tops)]
    totals = [1.0 / jnp.sum(each, axis=-1, keepdims=True) for each in raised]
    for hp in pairs:
        p[0, hp] = (raised[hp] * totals[hp]).astype(BF16)
    for hp in pairs:
        mixed = nn(p[0, hp], qkv[0, :, 2 * d + LANES * hp : 2 * d + LANES * (hp + 1)])
        o[here, lanes[hp]] = join_heads(mixed).astype(BF16)
    attn = jnp.where(valid, nn(o[here, :], wfull[:, 3 * d : 4 * d]), 0.0)
    ssq[0:1, :] += jnp.sum(attn * attn, axis=0, keepdims=True)
    after = x + attn
    h1[0] = after
    n2, _ = norm_stats(after)
    in_two = (n2 * rt[5:6, :]).astype(BF16)
    for n in range(h1_images):

        @pl.when(i == n)
        def _(n=n):
            a2[n * seq : (n + 1) * seq, :] = in_two[0:seq]


def attn_fwd(idx, tokens, packs, seq, pad, keys, block, padded):
    images, _, d = tokens.shape
    out_shape = (
        pltpu.HBM((d, 4 * d), BF16),
        jax.ShapeDtypeStruct((TAIL, d), F32),
        pltpu.HBM((images, keys, 3 * d), BF16),
        pltpu.HBM((images, HEADS // 2, 2 * pad, keys), BF16),
        pltpu.HBM((padded, d), BF16),
        pltpu.HBM((padded, d), BF16),
        pltpu.HBM((images, pad, d), F32),
        pltpu.VMEM((block, d), BF16),
        jax.ShapeDtypeStruct((8, d), F32),
    )
    return pl.pallas_call(
        functools.partial(attn_fwd_kernel, seq=seq, h1_images=images),
        grid=(images,),
        out_shape=out_shape,
        in_specs=[SMEM_SPEC, pl.BlockSpec((1, pad, d), lambda i: (i, 0, 0))]
        + [VMEM_SPEC] * 4,
        out_specs=(
            whole((d, 4 * d)),
            whole((TAIL, d)),
            pl.BlockSpec((1, keys, 3 * d), lambda i: (i, 0, 0)),
            pl.BlockSpec((1, HEADS // 2, 2 * pad, keys), lambda i: (i, 0, 0, 0)),
            whole((padded, d)),
            whole((padded, d)),
            pl.BlockSpec((1, pad, d), lambda i: (i, 0, 0)),
            VMEM_SPEC,
            whole((8, d)),
        ),
        compiler_params=params(40),
        cost_estimate=cost(1, 1),
    )(idx, stay(tokens), *packs)


def chosen_row(idx, ref, block, width):
    masks = ref[block:, :].astype(F32)
    d = masks.shape[1]
    row = lax.broadcasted_iota(jnp.int32, masks.shape, 0)
    parts = [
        jnp.sum(jnp.where(row == 4 * n + idx[0], masks, 0.0), axis=0, keepdims=True)
        for n in range((block + d - 1) // d)
    ]
    parts.append(jnp.zeros((1, width - d * len(parts)), F32))
    return jnp.concatenate(parts, axis=1)


def route(idx, a2s, rt, ga, gb, block):
    width = a2s.shape[0]
    row = lax.broadcasted_iota(jnp.int32, (TAIL, width), 0)
    logits = jnp.where(row < 4, nt(rt[...].astype(BF16), a2s[...]), -1e30)
    raised = jnp.exp(logits - jnp.max(logits, axis=0, keepdims=True))
    share = raised / jnp.sum(raised, axis=0, keepdims=True)
    chosen = chosen_row(idx, ga, block, width)
    chosen += pltpu.roll(chosen_row(idx, gb, block, width), block, 1)
    mine = jnp.sum(jnp.where(row == idx[0], share, 0.0), axis=0, keepdims=True)
    return jnp.where(row == HEAD, chosen * mine, share).T


def fold_lanes(wide):
    parts = [wide[:, n : n + LANES] for n in range(0, wide.shape[1], LANES)]
    return sum(parts[1:], parts[0])


def gather_rows(a2a, a2b, ga, gb, a2s, gs):
    block = a2a.shape[0]
    for ref, first, second in ((a2s, a2a, a2b), (gs, ga, gb)):
        ref[0:block, :] = first[0:block, :]
        ref[block : 2 * block, :] = second[0:block, :]
        ref[2 * block :, :] = jnp.zeros((ref.shape[0] - 2 * block, ref.shape[1]), BF16)


def finish_rows(idx, probs, dcomb, total, a2s, rt, da, db, gr):
    block = da.shape[0]
    lane = lax.broadcasted_iota(jnp.int32, probs.shape, 1)
    own = (lane == idx[0]).astype(F32)
    inner = jnp.sum(dcomb[...], axis=1, keepdims=True)
    dlogits = jnp.where(lane < 4, inner * (own - probs[...]), 0.0).astype(BF16)
    gr[...] = tn(dlogits, a2s[...])
    result = (total[...] + nn(dlogits[0 : 2 * block], rt[...].astype(BF16))).astype(BF16)
    da[...] = result[0:block]
    db[...] = result[block:]


def expert_kernel(
    idx, a2a, a2b, ga, gb, w1_far, w2_far, rt,
    zc, du, da, db, gr, a2s, gs, w1, w2, probs, dcomb, total, sem1, sem2,
):
    block = a2a.shape[0]
    step = w1.shape[2]
    loads = []
    for j in range(w1.shape[0]):
        here = pl.ds(j * step, step)
        loads.append(pltpu.make_async_copy(w1_far.at[:, here], w1.at[j], sem1.at[j]))
        loads.append(pltpu.make_async_copy(w2_far.at[here], w2.at[j], sem2.at[j]))
    for copy in loads:
        copy.start()
    gather_rows(a2a, a2b, ga, gb, a2s, gs)
    probs[...] = route(idx, a2s, rt, ga, gb, block)
    total[...] = jnp.zeros(total.shape, F32)
    dcomb[...] = jnp.zeros(dcomb.shape, F32)
    for ref in (zc, du):
        ref[2 * block :, :] = jnp.zeros((ref.shape[0] - 2 * block, ref.shape[1]), BF16)

    @pl.loop(0, w1.shape[0])
    def _(j):
        here = pl.ds(pl.multiple_of(j * step, LANES), step)
        pltpu.make_async_copy(w1_far.at[:, here], w1.at[j], sem1.at[j]).wait()
        pltpu.make_async_copy(w2_far.at[here], w2.at[j], sem2.at[j]).wait()
        halves = [slice(0, block), slice(block, 2 * block)]
        us = [nn(a2s[r, :], w1[j]) for r in halves]
        dzs = [nt(gs[r, :], w2[j]) for r in halves]
        for r, u, dz in zip(halves, us, dzs):
            act, slope = gelu_pair(u)
            scale = probs[r, HEAD : HEAD + 1]
            mixed = (act * scale).astype(BF16)
            zc[r, here] = mixed
            dcomb[r, :] += fold_lanes(mixed.astype(F32) * dz)
            grad = (slope * scale * dz).astype(BF16)
            du[r, here] = grad
            total[r, :] += nt(grad, w1[j])

    finish_rows(idx, probs, dcomb, total, a2s, rt, da, db, gr)


def expert(idx, a2s, gs, w1, w2, rt, near):
    block, d = a2s[0].shape
    f = w1.shape[1]
    both = 2 * block
    rows = round_up(both, 2 * LANES)
    step = f // 4
    return pl.pallas_call(
        expert_kernel,
        out_shape=(
            pltpu.VMEM((rows, f), BF16),
            pltpu.VMEM((rows, f), BF16),
            pltpu.HBM((block, d), BF16) if near else pltpu.VMEM((block, d), BF16),
            pltpu.VMEM((block, d), BF16),
            jax.ShapeDtypeStruct((TAIL, d), F32),
            pltpu.VMEM((rows, d), BF16),
            pltpu.VMEM((rows, d), BF16),
        ),
        in_specs=[SMEM_SPEC] + [VMEM_SPEC] * 4 + [FAR_SPEC] * 2 + [VMEM_SPEC],
        out_specs=(VMEM_SPEC,) * 2
        + (pl.BlockSpec((block, d), lambda: (0, 0)) if near else VMEM_SPEC,)
        + (VMEM_SPEC,) * 4,
        scratch_shapes=[
            pltpu.VMEM((4, d, step), BF16),
            pltpu.VMEM((4, step, d), BF16),
            pltpu.VMEM((rows, TAIL), F32),
            pltpu.VMEM((rows, LANES), F32),
            pltpu.VMEM((both, d), F32),
            pltpu.SemaphoreType.DMA((4,)),
            pltpu.SemaphoreType.DMA((4,)),
        ],
        compiler_params=params(26),
        cost_estimate=cost(6 * both * d * f, 25e6, 2 * both * f),
    )(idx, *a2s, *gs, stay(w1), stay(w2), rt)


def grads_kernel(zn, zf, gn, gf, an, af, dn, df, out, parts, sem):
    d = gn.shape[1]
    count, tall, _ = parts.shape
    half = count // 2

    @pl.loop(0, half)
    def _(j):
        here = pl.ds(pl.multiple_of(j * tall, LANES), tall)
        parts[j] = (tn(zn[:, here], gn[...]) + tn(zf[:, here], gf[...])).astype(BF16)
        pltpu.make_async_copy(parts.at[j], out.at[here], sem.at[j]).start()

    @pl.loop(half, count)
    def _(j):
        for n in range(tall // d):
            here = pl.ds(pl.multiple_of((j - half) * tall + n * d, LANES), d)
            grad = tn(an[...], dn[:, here]) + tn(af[...], df[:, here])
            parts[j, n * d : (n + 1) * d, :] = grad.astype(BF16)
        here = pl.ds(pl.multiple_of(j * tall, LANES), tall)
        pltpu.make_async_copy(parts.at[j], out.at[here], sem.at[j]).start()

    for j in range(count):
        pltpu.make_async_copy(parts.at[j], out.at[pl.ds(j * tall, tall)], sem.at[j]).wait()


def expert_grads(zn, zf, gn, gf, an, af, dn, df):
    both, f = zn.shape
    d = gn.shape[1]
    return pl.pallas_call(
        grads_kernel,
        out_shape=pltpu.HBM((2 * f, d), BF16),
        in_specs=[VMEM_SPEC] * 8,
        out_specs=FAR_SPEC,
        scratch_shapes=[
            pltpu.VMEM((4, f // 2, d), BF16),
            pltpu.SemaphoreType.DMA((4,)),
        ],
        compiler_params=params(16),
        cost_estimate=cost(8 * both * d * f, 25e6),
    )(zn, zf, gn, gf, an, af, dn, df)


def place_kernel(grads, gwo, gwi, low, wide, in_sem, out_sem):
    count, large, d = wide.shape
    half, runs = count // 2, d // large
    loads, stores = [], []
    for c in range(count):
        loads.append(pltpu.make_async_copy(grads.at[c], low.at[c], in_sem.at[c]))
        if c < half:
            target = gwo.at[0, pl.ds(c * large, large)]
        else:
            k = c - half
            target = gwi.at[0, pl.ds(k % runs * large, large), pl.ds(k // runs * d, d)]
        stores.append(pltpu.make_async_copy(wide.at[c], target, out_sem.at[c]))
    for copy in loads:
        copy.start()
    for c in range(count):
        loads[c].wait()
        wide[c] = low[c].astype(F32)
        stores[c].start()
    for copy in stores:
        copy.wait()


def place(grads, f):
    count, large, d = grads.shape
    return pl.pallas_call(
        place_kernel,
        out_shape=(pltpu.HBM((1, f, d), F32), pltpu.HBM((1, d, f), F32)),
        in_specs=[FAR_SPEC],
        out_specs=(FAR_SPEC, FAR_SPEC),
        scratch_shapes=[
            pltpu.VMEM((count, large, d), BF16),
            pltpu.VMEM((count, large, d), F32),
            pltpu.SemaphoreType.DMA((count,)),
            pltpu.SemaphoreType.DMA((count,)),
        ],
        compiler_params=params(40),
        cost_estimate=cost(1e6, 12e6),
    )(stay(grads))


def unpack_kernel(pack, gq, gk, gv, go, router, gain1, gain2):
    rows = gq.shape[0]
    for n, ref in enumerate((gq, gk, gv, go)):
        ref[...] = pack[n * rows : (n + 1) * rows, :].astype(F32)
    tail = pack[4 * rows : 4 * rows + TAIL, 0:rows].astype(F32)
    router[...] = tail[0:4]
    gain1[...] = tail[4:5]
    gain2[...] = tail[5:6]


def unpack(pack, rows):
    d = pack.shape[1]
    shapes = [(rows, d)] * 4 + [(4, rows), (1, rows), (1, rows)]
    return pl.pallas_call(
        unpack_kernel,
        out_shape=[jax.ShapeDtypeStruct(shape, F32) for shape in shapes],
        compiler_params=params(40),
        cost_estimate=cost(1e6, 2e6),
    )(pack)


def expert_out_kernel(zn, zf, w2_far, y0, y1, y2, y3, w2, near, far, sem):
    block = y0.shape[0]
    step = w2.shape[1]
    for j in range(w2.shape[0]):
        pltpu.make_async_copy(w2_far.at[pl.ds(j * step, step)], w2.at[j], sem.at[j]).start()
    near[...] = jnp.zeros(near.shape, F32)
    far[...] = jnp.zeros(far.shape, F32)

    @pl.loop(0, w2.shape[0])
    def _(j):
        here = pl.ds(pl.multiple_of(j * step, LANES), step)
        pltpu.make_async_copy(w2_far.at[here], w2.at[j], sem.at[j]).wait()
        near[...] += nn(zn[0 : 2 * block, here], w2[j])
        far[...] += nn(zf[0 : 2 * block, here], w2[j])

    y0[...] = near[0:block, :].astype(BF16)
    y1[...] = near[block:, :].astype(BF16)
    y2[...] = far[0:block, :].astype(BF16)
    y3[...] = far[block:, :].astype(BF16)


def expert_out(zn, zf, w2, block):
    both, f = 2 * block, zn.shape[1]
    d = w2.shape[1]
    step = f // 4
    return pl.pallas_call(
        expert_out_kernel,
        out_shape=[jax.ShapeDtypeStruct((both // 2, d), BF16)] * 4,
        in_specs=[VMEM_SPEC] * 2 + [FAR_SPEC],
        out_specs=[VMEM_SPEC] * 4,
        scratch_shapes=[pltpu.VMEM((4, step, d), BF16)]
        + [pltpu.VMEM((both, d), F32)] * 2
        + [pltpu.SemaphoreType.DMA((4,))],
        compiler_params=params(24),
        cost_estimate=cost(4 * d * f * both, 16e6),
    )(zn, zf, stay(w2))


def unpack_rows(dense, spread, seq, pad):
    spread[...] = jnp.zeros(spread.shape, F32)
    for n in range(dense.shape[0] // seq):
        spread[n * pad : n * pad + seq, :] = dense[n * seq : (n + 1) * seq, :]


def attn_bwd_kernel(
    idx, tok, g, da0, da1, da2, h1, qkv, p, o, a1, wfull, rt, gra, grb,
    gtok, pack_send, pack_keep,
    flat, da, gpad, dattn_all, dqkv, gains, grads, *, seq,
):
    i = pl.program_id(0)
    pad, d = tok.shape[1], tok.shape[2]
    rows = d // 4

    @pl.when(i == 0)
    def _():
        flat[...] = da0[...].astype(F32) + da1[...].astype(F32) + da2[...].astype(F32)
        unpack_rows(flat, da, seq, pad)
        flat[...] = g[0 : flat.shape[0], :].astype(F32)
        unpack_rows(flat, gpad, seq, pad)
        dattn_all[...] = jnp.zeros(dattn_all.shape, BF16)
        dqkv[...] = jnp.zeros(dqkv.shape, BF16)
        gains[...] = jnp.zeros(gains.shape, F32)

    here = pl.ds(pl.multiple_of(i * pad, TAIL), pad)
    valid = lax.broadcasted_iota(jnp.int32, (pad, 1), 0) < seq
    n2, r2 = norm_stats(h1[0])
    din = da[here, :]
    gains[1:2, :] += jnp.sum(din * n2, axis=0, keepdims=True)
    dh1 = gpad[here, :] + norm_back(din * rt[5:6, :], n2, r2)
    dattn = dh1.astype(BF16)
    dattn_all[here, :] = dattn
    do = nt(dattn, wfull[:, 3 * d : 4 * d]).astype(BF16)
    pairs = range(HEADS // 2)
    lanes = [slice(LANES * hp, LANES * (hp + 1)) for hp in pairs]
    klanes = [slice(d + LANES * hp, d + LANES * (hp + 1)) for hp in pairs]
    vlanes = [slice(2 * d + LANES * hp, 2 * d + LANES * (hp + 1)) for hp in pairs]
    do2 = [split_heads(do[:, lanes[hp]]) for hp in pairs]
    dp = [nt(do2[hp], qkv[0, :, vlanes[hp]]) for hp in pairs]
    for hp in pairs:
        dqkv[here, vlanes[hp]] = tn(p[0, hp], do2[hp])[0:pad].astype(BF16)
    wide = [p[0, hp].astype(F32) for hp in pairs]
    inner = [jnp.sum(dp[hp] * wide[hp], axis=-1, keepdims=True) for hp in pairs]
    ds = [(wide[hp] * (dp[hp] - inner[hp])).astype(BF16) for hp in pairs]
    for hp in pairs:
        dq = join_heads(nn(ds[hp], qkv[0, :, klanes[hp]]))
        dqkv[here, lanes[hp]] = (dq * HEAD_DIM**-0.5).astype(BF16)
        dk = tn(ds[hp], split_heads(qkv[0, 0:pad, lanes[hp]]))
        dqkv[here, klanes[hp]] = dk[0:pad].astype(BF16)
    din1 = nt(dqkv[here, :], wfull[:, 0 : 3 * d])
    x = jnp.where(valid, tok[0].astype(F32), 0.0)
    n1, r1 = norm_stats(x)
    gains[0:1, :] += jnp.sum(din1 * n1, axis=0, keepdims=True)
    gtok[0] = (dh1 + norm_back(din1 * rt[4:5, :], n1, r1)).astype(BF16)

    @pl.when(i == pl.num_programs(0) - 1)
    def _():
        grads[:, 0 : 3 * d] = tn(a1[...], dqkv[...]).astype(BF16)
        grads[:, 3 * d : 4 * d] = tn(o[...], dattn_all[...]).astype(BF16)
        row = lax.broadcasted_iota(jnp.int32, (TAIL, d), 0)
        tail = jnp.where(row < 4, gra[...] + grb[...], 0.0)
        tail = jnp.where(row == 4, gains[0:1, :], tail)
        gains[...] = jnp.where(row == 5, gains[1:2, :], tail)
        for n, (ref, slot) in enumerate(
            ((pack_keep, 0), (pack_send, 0), (pack_keep, 1), (pack_send, 1))
        ):
            at = pl.multiple_of(idx[n] * rows, rows)
            for m in range(4):
                ref[slot, m * rows : (m + 1) * rows, :] = grads[pl.ds(at, rows), m * d : (m + 1) * d]
            ref[slot, 4 * rows :, :] = jnp.zeros((ref.shape[1] - 4 * rows, d), BF16)
            ref[slot, 4 * rows : 4 * rows + TAIL, 0:rows] = gains[:, pl.ds(at, rows)].astype(BF16)


def attn_bwd(idx, tokens, g, das, h1, qkv, p, o, a1, wfull, rt, grs, seq, pad, pack_rows):
    images, _, d = tokens.shape
    block, padded = das[0].shape[0], a1.shape[0]
    keys = qkv.shape[1]
    image = lambda i: (i, 0, 0)
    return pl.pallas_call(
        functools.partial(attn_bwd_kernel, seq=seq),
        grid=(images,),
        out_shape=(
            jax.ShapeDtypeStruct(tokens.shape, BF16),
            pltpu.HBM((2, pack_rows, d), BF16),
            pltpu.HBM((2, pack_rows, d), BF16),
        ),
        in_specs=[SMEM_SPEC, pl.BlockSpec((1, pad, d), image), whole(g.shape)]
        + [whole((block, d)), VMEM_SPEC, VMEM_SPEC]
        + [
            pl.BlockSpec((1, pad, d), image),
            pl.BlockSpec((1, keys, 3 * d), image),
            pl.BlockSpec((1, HEADS // 2, 2 * pad, keys), lambda i: (i, 0, 0, 0)),
            whole((padded, d)),
            whole((padded, d)),
            whole((d, 4 * d)),
            whole((TAIL, d)),
            whole((TAIL, d)),
            whole((TAIL, d)),
        ],
        out_specs=(
            pl.BlockSpec((1, pad, d), image),
            whole((2, pack_rows, d)),
            whole((2, pack_rows, d)),
        ),
        scratch_shapes=[
            pltpu.VMEM((block, d), F32),
            pltpu.VMEM((padded, d), F32),
            pltpu.VMEM((padded, d), F32),
            pltpu.VMEM((padded, d), BF16),
            pltpu.VMEM((padded, 3 * d), BF16),
            pltpu.VMEM((TAIL, d), F32),
            pltpu.VMEM((d, 4 * d), BF16),
        ],
        compiler_params=params(40),
        cost_estimate=cost(LONG, 15e6),
    )(
        idx, stay(tokens), stay(g), stay(das[0]), *das[1:],
        *(stay(kept) for kept in (h1, qkv, p, o, a1, wfull)), rt, *grs,
    )


def output_kernel(h1, y0, y1, y2, ssq, out, sums, flat, moe, *, seq):
    i = pl.program_id(0)
    pad = h1.shape[1]

    @pl.when(i == 0)
    def _():
        flat[...] = y0[...].astype(F32) + y1[...].astype(F32) + y2[...].astype(F32)
        unpack_rows(flat, moe, seq, pad)
        sums[...] = jnp.zeros(sums.shape, F32)
        sums[1:2, :] = fold_lanes(ssq[0:1, :])

    branch = moe[pl.ds(pl.multiple_of(i * pad, TAIL), pad), :]
    result = h1[0] + branch
    sums[0:1, :] += fold_lanes(jnp.sum(result * result, axis=0, keepdims=True))
    sums[2:3, :] += fold_lanes(jnp.sum(branch * branch, axis=0, keepdims=True))
    out[0] = result.astype(BF16)


def output(h1, ys, ssq, seq):
    images, pad, d = h1.shape
    block = ys[0].shape[0]
    return pl.pallas_call(
        functools.partial(output_kernel, seq=seq),
        grid=(images,),
        out_shape=(
            jax.ShapeDtypeStruct((images, seq, d), BF16),
            jax.ShapeDtypeStruct((8, LANES), F32),
        ),
        in_specs=[pl.BlockSpec((1, pad, d), lambda i: (i, 0, 0))] + [VMEM_SPEC] * 4,
        out_specs=(pl.BlockSpec((1, pad, d), lambda i: (i, 0, 0)), whole((8, LANES))),
        scratch_shapes=[pltpu.VMEM((block, d), F32), pltpu.VMEM((images * pad, d), F32)],
        compiler_params=params(16),
        cost_estimate=cost(10 * block * d, 5e6),
    )(stay(h1), *ys, ssq)


def scatter_rows(a, axes, groups):
    count = len(groups[0])
    parts = a.reshape(count, a.shape[0] // count, a.shape[1])
    return lax.all_to_all(parts, axes, 0, 0, tiled=True, axis_index_groups=groups)


def add_rows(parts):
    return jnp.sum(parts.astype(F32), axis=0).astype(BF16)


def local(
    tokens,
    cotangent,
    gain_one,
    w_query,
    w_key,
    w_value,
    w_output,
    gain_two,
    w_router,
    w_in,
    w_out,
    routes,
):
    images, seq, d = tokens.shape
    experts = lax.axis_size("shard")
    pad = round_up(seq, TAIL)
    keys = round_up(seq, LANES)
    block = round_up(images * seq, TAIL)
    padded = round_up(images * pad, LANES)
    rows = w_query.shape[0]
    me = lax.axis_index("shard")
    reps = lax.axis_size("rep")
    everyone = ("shard", "rep")
    ring = [*range(0, reps, 2), *range(reps - 1, 0, -2)]
    rings = [[s * reps + r for r in ring] for s in range(experts)]
    idx = jnp.stack([me, me ^ 1, me ^ 2, me ^ 3]).astype(jnp.int32)
    core = lambda a: lax.ppermute(a, "shard", [(s, s ^ 1) for s in range(experts)])
    chip = lambda a: lax.ppermute(a, "shard", [(s, s ^ 2) for s in range(experts)])

    operands = (
        w_query, w_key, w_value, w_output,
        gain_one.reshape(1, rows), gain_two.reshape(1, rows), w_router.T,
    )
    wp = pl.pallas_call(
        pack_weights_kernel,
        grid=(1,),
        out_shape=pltpu.VMEM((rows + HEAD, 4 * d), BF16),
        in_specs=[whole(a.shape) for a in operands],
        out_specs=VMEM_SPEC,
        compiler_params=params(40),
        cost_estimate=cost(1e6, 3e6),
    )(*(stay(a) for a in operands))
    chosen = (routes[:, :, :, None] == jnp.arange(experts, dtype=jnp.int32)).any(axis=2)
    chosen = chosen.reshape(images * seq, experts).T
    chosen = jnp.pad(chosen, ((0, 0), (0, round_up(block, d) - images * seq)))
    chosen = chosen.reshape(experts, -1, d).transpose(1, 0, 2).reshape(-1, d)
    masks = jnp.pad(chosen, ((0, TAIL - chosen.shape[0]), (0, 0))).astype(BF16)
    gp = pl.pallas_call(
        pack_cotangent_kernel,
        grid=(1,),
        out_shape=jax.ShapeDtypeStruct((block + TAIL, d), BF16),
        in_specs=[whole(cotangent.shape), whole(masks.shape)],
        out_specs=whole((block + TAIL, d)),
        compiler_params=params(40),
        cost_estimate=cost(1e6, 1e6),
    )(stay(cotangent), masks)
    wx = after(chip(wp), gp)
    gx = chip(gp)
    packs = (wp, core(wp), wx, core(wx))
    gs = (gp, core(gp), gx, core(gx))
    w1, w2 = w_in[0], w_out[0]
    wfull, rt, qkv, p, o, a1, h1, a2, ssq = attn_fwd(
        idx, tokens, packs, seq, pad, keys, block, padded
    )
    ax = chip(a2)
    zn, dun, da, dac, grn, an, gn = expert(
        idx, (a2, core(after(a2, gx))), gs[:2], w1, w2, rt, True
    )
    ax = after(ax, zn)
    zf, duf, dax, daxc, grf, af, gf = expert(
        idx, (ax, core(ax)), gs[2:], w1, w2, rt, False
    )
    da_far = dax + core(daxc)
    grads_part = expert_grads(zn, zf, after(gn, da_far), gf, an, af, dun, duf)
    grads_slice = lax.psum_scatter(
        grads_part, everyone, scatter_dimension=0, tiled=True, axis_index_groups=rings
    )
    grad_tokens, send, keep = attn_bwd(
        idx, tokens, gp, (da, core(dac), chip(da_far)), after(h1, grads_part),
        qkv, p, o, a1, wfull, rt, (grn, grf), seq, pad, round_up(4 * rows + TAIL, 8 * reps),
    )
    got = core(send)
    pack_far = keep[1] + got[1]
    y, yc, yx, yxc = expert_out(after(zn, pack_far), zf, w2, block)
    pack = (
        after(keep, y)[0].astype(F32) + got[0].astype(F32) + chip(pack_far).astype(F32)
    ).astype(BF16)
    y_far = after(yx, pack) + core(yxc)
    grads = lax.all_gather(
        after(grads_slice, y_far), everyone, axis=0, axis_index_groups=rings
    )
    pack = add_rows(after(scatter_rows(pack, everyone, rings), grads_slice))
    pack = lax.all_gather(pack, everyone, axis=0, tiled=True, axis_index_groups=rings)
    out, sums = output(h1, (y, core(yc), chip(y_far)), ssq, seq)
    sums = jnp.broadcast_to(after(sums, pack)[None], (experts * reps, *sums.shape))
    sums = lax.all_to_all(sums, everyone, 0, 0, tiled=True)
    totals = jnp.sum(sums, axis=(0, 2))
    gq, gk, gv, go, router, gain1, gain2 = unpack(pack, rows)
    gwo, gwi = place(grads, w1.shape[1])
    roots = jnp.sqrt(totals / float(experts * reps * images * seq * d))
    return (
        out,
        grad_tokens,
        gain1.reshape(rows),
        gq,
        gk,
        gv,
        go,
        gain2.reshape(rows),
        router.T,
        gwi,
        gwo,
        roots[0],
        roots[1],
        roots[2],
    )


def solution(mesh):
    spread = P(("shard", "rep"), None, None)
    matrix = P("shard", None)
    stack = P("shard", None, None)
    vector = P("shard")
    return jax.shard_map(
        local,
        mesh=mesh,
        in_specs=(
            spread, spread, vector, matrix, matrix, matrix, matrix, vector, matrix, stack, stack, spread,
        ),
        out_specs=(
            spread, spread, vector, matrix, matrix, matrix, matrix, vector, matrix, stack, stack, P(), P(), P(),
        ),
        check_vma=False,
    )
```

```python
import functools

import jax
import jax.numpy as jnp
from jax import lax
from jax.experimental import pallas as pl
from jax.experimental.pallas import tpu as pltpu
from jax.sharding import PartitionSpec as P

HEADS = 8
HEAD_DIM = 64
EPSILON = 1e-06
LANES = 128
TAIL = 16
HEAD = 8
LONG = 1e11
MEDIUM = 6.4e10

BF16 = jnp.bfloat16
F32 = jnp.float32

LOG2E = 1.4426950408889634
ROOT_HALF = 0.7071067811865476
INV_ROOT_2PI = 0.3989422804014327


def round_up(value, multiple):
    return (value + multiple - 1) // multiple * multiple


def nn(a, b):
    return lax.dot_general(a, b, (((1,), (0,)), ((), ())), preferred_element_type=F32)


def nt(a, b):
    return lax.dot_general(a, b, (((1,), (1,)), ((), ())), preferred_element_type=F32)


def tn(a, b):
    return lax.dot_general(a, b, (((0,), (0,)), ((), ())), preferred_element_type=F32)


def norm_stats(values):
    center = values - jnp.mean(values, axis=-1, keepdims=True)
    inverse = lax.rsqrt(jnp.mean(center * center, axis=-1, keepdims=True) + EPSILON)
    return center * inverse, inverse


def norm_back(grad_normed, normed, inverse):
    mean_plain = jnp.mean(grad_normed, axis=-1, keepdims=True)
    mean_cross = jnp.mean(grad_normed * normed, axis=-1, keepdims=True)
    return inverse * (grad_normed - mean_plain - normed * mean_cross)


def gelu_pair(u):
    cdf = 0.5 * lax.erf(u * ROOT_HALF) + 0.5
    return u * cdf, cdf + u * (jnp.exp2(u * u * (-0.5 * LOG2E)) * INV_ROOT_2PI)


def split_heads(pair):
    low = lax.broadcasted_iota(jnp.int32, pair.shape, 1) < HEAD_DIM
    zero = jnp.zeros_like(pair)
    return jnp.concatenate([jnp.where(low, pair, zero), jnp.where(low, zero, pair)], axis=0)


def join_heads(stacked):
    rows = stacked.shape[0] // 2
    low = lax.broadcasted_iota(jnp.int32, (rows, stacked.shape[1]), 1) < HEAD_DIM
    return jnp.where(low, stacked[:rows], stacked[rows:])


def after(value, *first):
    return lax.optimization_barrier((value, *first))[0]


def stay(array):
    return pltpu.with_memory_space_constraint(array, pltpu.HBM)


def params(mebibytes=60):
    return pltpu.CompilerParams(vmem_limit_bytes=mebibytes * 1024 * 1024)


def cost(flops, nbytes, trans=0):
    return pl.CostEstimate(flops=int(flops), bytes_accessed=int(nbytes), transcendentals=int(trans))


def whole(shape):
    return pl.BlockSpec(shape, lambda *_: (0,) * len(shape))


SMEM_SPEC = pl.BlockSpec(memory_space=pltpu.SMEM)
VMEM_SPEC = pl.BlockSpec(memory_space=pltpu.VMEM)
FAR_SPEC = pl.BlockSpec(memory_space=pl.ANY)


def pack_weights_kernel(wq, wk, wv, wo, g1, g2, wr, wp):
    rows, d = wq.shape
    for n, w in enumerate((wq, wk, wv, wo)):
        wp[0:rows, n * d : (n + 1) * d] = w[...]
    blank = jnp.zeros((HEAD - wr.shape[0], LANES), F32)
    head = jnp.concatenate([wr[...].astype(F32), blank], axis=0)
    row = lax.broadcasted_iota(jnp.int32, (HEAD, LANES), 0)
    head = jnp.where(row == 4, g1[...].astype(F32), head)
    head = jnp.where(row == 5, g2[...].astype(F32), head)
    wp[rows:, :] = jnp.zeros((HEAD, wp.shape[1]), BF16)
    wp[rows:, 0:LANES] = head.astype(BF16)


def pack_cotangent_kernel(cot, masks, gp):
    seq = cot.shape[1]
    gp[...] = jnp.zeros(gp.shape, BF16)
    for i in range(cot.shape[0]):
        gp[i * seq : (i + 1) * seq, :] = cot[i]
    gp[gp.shape[0] - TAIL :, :] = masks[...]


def attn_fwd_kernel(
    idx, tok, w0, w1, w2, w3, wfull, rt, qkv, p, o, a1, h1, a2, ssq, *, seq, h1_images
):
    i = pl.program_id(0)
    pad, d = tok.shape[1], tok.shape[2]
    keys = qkv.shape[1]
    rows = w0.shape[0] - HEAD

    @pl.when(i == 0)
    def _():
        for n, w in enumerate((w0, w1, w2, w3)):
            at = pl.multiple_of(idx[n] * rows, rows)
            wfull[pl.ds(at, rows), :] = w[0:rows, :]
            rt[0:HEAD, pl.ds(at, rows)] = w[rows:, 0:rows].astype(F32)
            rt[HEAD:, pl.ds(at, rows)] = jnp.zeros((TAIL - HEAD, rows), F32)
        for ref in (o, a1, a2):
            ref[...] = jnp.zeros(ref.shape, ref.dtype)
        ssq[...] = jnp.zeros(ssq.shape, F32)

    here = pl.ds(pl.multiple_of(i * pad, TAIL), pad)
    valid = lax.broadcasted_iota(jnp.int32, (pad, 1), 0) < seq
    x = jnp.where(valid, tok[0].astype(F32), 0.0)
    n1, _ = norm_stats(x)
    in_one = (n1 * rt[4:5, :]).astype(BF16)
    a1[here, :] = in_one
    proj = nn(in_one, wfull[:, 0 : 3 * d])
    qkv[0, 0:pad, 0:d] = (proj[:, 0:d].astype(BF16).astype(F32) * HEAD_DIM**-0.5).astype(BF16)
    qkv[0, 0:pad, d:] = proj[:, d:].astype(BF16)
    qkv[0, pad:keys, :] = jnp.zeros((keys - pad, 3 * d), BF16)
    column = lax.broadcasted_iota(jnp.int32, (1, keys), 1) < seq
    pairs = range(HEADS // 2)
    lanes = [slice(LANES * hp, LANES * (hp + 1)) for hp in pairs]
    scores = [
        nt(split_heads(qkv[0, 0:pad, lanes[hp]]), qkv[0, :, d + LANES * hp : d + LANES * (hp + 1)])
        for hp in pairs
    ]
    scores = [jnp.where(column, score, -1e30) for score in scores]
    tops = [jnp.max(score, axis=-1, keepdims=True) for score in scores]
    raised = [jnp.exp(score - top) for score, top in zip(scores, tops)]
    totals = [1.0 / jnp.sum(each, axis=-1, keepdims=True) for each in raised]
    for hp in pairs:
        p[0, hp] = (raised[hp] * totals[hp]).astype(BF16)
    for hp in pairs:
        mixed = nn(p[0, hp], qkv[0, :, 2 * d + LANES * hp : 2 * d + LANES * (hp + 1)])
        o[here, lanes[hp]] = join_heads(mixed).astype(BF16)
    attn = jnp.where(valid, nn(o[here, :], wfull[:, 3 * d : 4 * d]), 0.0)
    ssq[0:1, :] += jnp.sum(attn * attn, axis=0, keepdims=True)
    after = x + attn
    h1[0] = after
    n2, _ = norm_stats(after)
    in_two = (n2 * rt[5:6, :]).astype(BF16)
    for n in range(h1_images):

        @pl.when(i == n)
        def _(n=n):
            a2[n * seq : (n + 1) * seq, :] = in_two[0:seq]


def attn_fwd(idx, tokens, packs, seq, pad, keys, block, padded):
    images, _, d = tokens.shape
    out_shape = (
        pltpu.HBM((d, 4 * d), BF16),
        jax.ShapeDtypeStruct((TAIL, d), F32),
        pltpu.HBM((images, keys, 3 * d), BF16),
        pltpu.HBM((images, HEADS // 2, 2 * pad, keys), BF16),
        pltpu.HBM((padded, d), BF16),
        pltpu.HBM((padded, d), BF16),
        pltpu.HBM((images, pad, d), F32),
        pltpu.VMEM((block, d), BF16),
        jax.ShapeDtypeStruct((8, d), F32),
    )
    return pl.pallas_call(
        functools.partial(attn_fwd_kernel, seq=seq, h1_images=images),
        grid=(images,),
        out_shape=out_shape,
        in_specs=[SMEM_SPEC, pl.BlockSpec((1, pad, d), lambda i: (i, 0, 0))]
        + [VMEM_SPEC] * 4,
        out_specs=(
            whole((d, 4 * d)),
            whole((TAIL, d)),
            pl.BlockSpec((1, keys, 3 * d), lambda i: (i, 0, 0)),
            pl.BlockSpec((1, HEADS // 2, 2 * pad, keys), lambda i: (i, 0, 0, 0)),
            whole((padded, d)),
            whole((padded, d)),
            pl.BlockSpec((1, pad, d), lambda i: (i, 0, 0)),
            VMEM_SPEC,
            whole((8, d)),
        ),
        compiler_params=params(40),
        cost_estimate=cost(1, 1),
    )(idx, stay(tokens), *packs)


def chosen_row(idx, ref, block, width):
    masks = ref[block:, :].astype(F32)
    d = masks.shape[1]
    row = lax.broadcasted_iota(jnp.int32, masks.shape, 0)
    parts = [
        jnp.sum(jnp.where(row == 4 * n + idx[0], masks, 0.0), axis=0, keepdims=True)
        for n in range((block + d - 1) // d)
    ]
    parts.append(jnp.zeros((1, width - d * len(parts)), F32))
    return jnp.concatenate(parts, axis=1)


def route(idx, a2s, rt, ga, gb, block):
    width = a2s.shape[0]
    row = lax.broadcasted_iota(jnp.int32, (TAIL, width), 0)
    logits = jnp.where(row < 4, nt(rt[...].astype(BF16), a2s[...]), -1e30)
    raised = jnp.exp(logits - jnp.max(logits, axis=0, keepdims=True))
    share = raised / jnp.sum(raised, axis=0, keepdims=True)
    chosen = chosen_row(idx, ga, block, width)
    chosen += pltpu.roll(chosen_row(idx, gb, block, width), block, 1)
    mine = jnp.sum(jnp.where(row == idx[0], share, 0.0), axis=0, keepdims=True)
    return jnp.where(row == HEAD, chosen * mine, share).T


def fold_lanes(wide):
    parts = [wide[:, n : n + LANES] for n in range(0, wide.shape[1], LANES)]
    return sum(parts[1:], parts[0])


def gather_rows(a2a, a2b, ga, gb, a2s, gs):
    block = a2a.shape[0]
    for ref, first, second in ((a2s, a2a, a2b), (gs, ga, gb)):
        ref[0:block, :] = first[0:block, :]
        ref[block : 2 * block, :] = second[0:block, :]
        ref[2 * block :, :] = jnp.zeros((ref.shape[0] - 2 * block, ref.shape[1]), BF16)


def finish_rows(idx, probs, dcomb, total, a2s, rt, da, db, gr):
    block = da.shape[0]
    lane = lax.broadcasted_iota(jnp.int32, probs.shape, 1)
    own = (lane == idx[0]).astype(F32)
    inner = jnp.sum(dcomb[...], axis=1, keepdims=True)
    dlogits = jnp.where(lane < 4, inner * (own - probs[...]), 0.0).astype(BF16)
    gr[...] = tn(dlogits, a2s[...])
    result = (total[...] + nn(dlogits[0 : 2 * block], rt[...].astype(BF16))).astype(BF16)
    da[...] = result[0:block]
    db[...] = result[block:]


def expert_kernel(
    idx, a2a, a2b, ga, gb, w1_far, w2_far, rt,
    zc, du, da, db, gr, a2s, gs, w1, w2, probs, dcomb, total, sem1, sem2,
):
    block = a2a.shape[0]
    step = w1.shape[2]
    loads = []
    for j in range(w1.shape[0]):
        here = pl.ds(j * step, step)
        loads.append(pltpu.make_async_copy(w1_far.at[:, here], w1.at[j], sem1.at[j]))
        loads.append(pltpu.make_async_copy(w2_far.at[here], w2.at[j], sem2.at[j]))
    for copy in loads:
        copy.start()
    gather_rows(a2a, a2b, ga, gb, a2s, gs)
    probs[...] = route(idx, a2s, rt, ga, gb, block)
    total[...] = jnp.zeros(total.shape, F32)
    dcomb[...] = jnp.zeros(dcomb.shape, F32)
    for ref in (zc, du):
        ref[2 * block :, :] = jnp.zeros((ref.shape[0] - 2 * block, ref.shape[1]), BF16)

    @pl.loop(0, w1.shape[0])
    def _(j):
        here = pl.ds(pl.multiple_of(j * step, LANES), step)
        pltpu.make_async_copy(w1_far.at[:, here], w1.at[j], sem1.at[j]).wait()
        pltpu.make_async_copy(w2_far.at[here], w2.at[j], sem2.at[j]).wait()
        halves = [slice(0, block), slice(block, 2 * block)]
        us = [nn(a2s[r, :], w1[j]) for r in halves]
        dzs = [nt(gs[r, :], w2[j]) for r in halves]
        for r, u, dz in zip(halves, us, dzs):
            act, slope = gelu_pair(u)
            scale = probs[r, HEAD : HEAD + 1]
            mixed = (act * scale).astype(BF16)
            zc[r, here] = mixed
            dcomb[r, :] += fold_lanes(mixed.astype(F32) * dz)
            grad = (slope * scale * dz).astype(BF16)
            du[r, here] = grad
            total[r, :] += nt(grad, w1[j])

    finish_rows(idx, probs, dcomb, total, a2s, rt, da, db, gr)


def expert(idx, a2s, gs, w1, w2, rt, near):
    block, d = a2s[0].shape
    f = w1.shape[1]
    both = 2 * block
    rows = round_up(both, 2 * LANES)
    step = f // 4
    return pl.pallas_call(
        expert_kernel,
        out_shape=(
            pltpu.VMEM((rows, f), BF16),
            pltpu.VMEM((rows, f), BF16),
            pltpu.HBM((block, d), BF16) if near else pltpu.VMEM((block, d), BF16),
            pltpu.VMEM((block, d), BF16),
            jax.ShapeDtypeStruct((TAIL, d), F32),
            pltpu.VMEM((rows, d), BF16),
            pltpu.VMEM((rows, d), BF16),
        ),
        in_specs=[SMEM_SPEC] + [VMEM_SPEC] * 4 + [FAR_SPEC] * 2 + [VMEM_SPEC],
        out_specs=(VMEM_SPEC,) * 2
        + (pl.BlockSpec((block, d), lambda: (0, 0)) if near else VMEM_SPEC,)
        + (VMEM_SPEC,) * 4,
        scratch_shapes=[
            pltpu.VMEM((4, d, step), BF16),
            pltpu.VMEM((4, step, d), BF16),
            pltpu.VMEM((rows, TAIL), F32),
            pltpu.VMEM((rows, LANES), F32),
            pltpu.VMEM((both, d), F32),
            pltpu.SemaphoreType.DMA((4,)),
            pltpu.SemaphoreType.DMA((4,)),
        ],
        compiler_params=params(26),
        cost_estimate=cost(6 * both * d * f, 25e6, 2 * both * f),
    )(idx, *a2s, *gs, stay(w1), stay(w2), rt)


def grads_kernel(zn, zf, gn, gf, an, af, dn, df, out, parts, sem):
    d = gn.shape[1]
    count, tall, _ = parts.shape
    half = count // 2

    @pl.loop(0, half)
    def _(j):
        here = pl.ds(pl.multiple_of(j * tall, LANES), tall)
        parts[j] = (tn(zn[:, here], gn[...]) + tn(zf[:, here], gf[...])).astype(BF16)
        pltpu.make_async_copy(parts.at[j], out.at[here], sem.at[j]).start()

    @pl.loop(half, count)
    def _(j):
        for n in range(tall // d):
            here = pl.ds(pl.multiple_of((j - half) * tall + n * d, LANES), d)
            grad = tn(an[...], dn[:, here]) + tn(af[...], df[:, here])
            parts[j, n * d : (n + 1) * d, :] = grad.astype(BF16)
        here = pl.ds(pl.multiple_of(j * tall, LANES), tall)
        pltpu.make_async_copy(parts.at[j], out.at[here], sem.at[j]).start()

    for j in range(count):
        pltpu.make_async_copy(parts.at[j], out.at[pl.ds(j * tall, tall)], sem.at[j]).wait()


def expert_grads(zn, zf, gn, gf, an, af, dn, df):
    both, f = zn.shape
    d = gn.shape[1]
    return pl.pallas_call(
        grads_kernel,
        out_shape=pltpu.HBM((2 * f, d), BF16),
        in_specs=[VMEM_SPEC] * 8,
        out_specs=FAR_SPEC,
        scratch_shapes=[
            pltpu.VMEM((4, f // 2, d), BF16),
            pltpu.SemaphoreType.DMA((4,)),
        ],
        compiler_params=params(16),
        cost_estimate=cost(8 * both * d * f, 25e6),
    )(zn, zf, gn, gf, an, af, dn, df)


def place_kernel(grads, gwo, gwi, low, wide, in_sem, out_sem):
    count, large, d = wide.shape
    half, runs = count // 2, d // large
    loads, stores = [], []
    for c in range(count):
        loads.append(pltpu.make_async_copy(grads.at[c], low.at[c], in_sem.at[c]))
        if c < half:
            target = gwo.at[0, pl.ds(c * large, large)]
        else:
            k = c - half
            target = gwi.at[0, pl.ds(k % runs * large, large), pl.ds(k // runs * d, d)]
        stores.append(pltpu.make_async_copy(wide.at[c], target, out_sem.at[c]))
    for copy in loads:
        copy.start()
    for c in range(count):
        loads[c].wait()
        wide[c] = low[c].astype(F32)
        stores[c].start()
    for copy in stores:
        copy.wait()


def place(grads, f):
    count, large, d = grads.shape
    return pl.pallas_call(
        place_kernel,
        out_shape=(pltpu.HBM((1, f, d), F32), pltpu.HBM((1, d, f), F32)),
        in_specs=[FAR_SPEC],
        out_specs=(FAR_SPEC, FAR_SPEC),
        scratch_shapes=[
            pltpu.VMEM((count, large, d), BF16),
            pltpu.VMEM((count, large, d), F32),
            pltpu.SemaphoreType.DMA((count,)),
            pltpu.SemaphoreType.DMA((count,)),
        ],
        compiler_params=params(40),
        cost_estimate=cost(1e6, 12e6),
    )(stay(grads))


def unpack_kernel(pack, gq, gk, gv, go, router, gain1, gain2):
    rows = gq.shape[0]
    for n, ref in enumerate((gq, gk, gv, go)):
        ref[...] = pack[n * rows : (n + 1) * rows, :].astype(F32)
    tail = pack[4 * rows : 4 * rows + TAIL, 0:rows].astype(F32)
    router[...] = tail[0:4]
    gain1[...] = tail[4:5]
    gain2[...] = tail[5:6]


def unpack(pack, rows):
    d = pack.shape[1]
    shapes = [(rows, d)] * 4 + [(4, rows), (1, rows), (1, rows)]
    return pl.pallas_call(
        unpack_kernel,
        out_shape=[jax.ShapeDtypeStruct(shape, F32) for shape in shapes],
        compiler_params=params(40),
        cost_estimate=cost(1e6, 2e6),
    )(pack)


def expert_out_kernel(zn, zf, w2_far, y0, y1, y2, y3, w2, near, far, sem):
    block = y0.shape[0]
    step = w2.shape[1]
    for j in range(w2.shape[0]):
        pltpu.make_async_copy(w2_far.at[pl.ds(j * step, step)], w2.at[j], sem.at[j]).start()
    near[...] = jnp.zeros(near.shape, F32)
    far[...] = jnp.zeros(far.shape, F32)

    @pl.loop(0, w2.shape[0])
    def _(j):
        here = pl.ds(pl.multiple_of(j * step, LANES), step)
        pltpu.make_async_copy(w2_far.at[here], w2.at[j], sem.at[j]).wait()
        near[...] += nn(zn[0 : 2 * block, here], w2[j])
        far[...] += nn(zf[0 : 2 * block, here], w2[j])

    y0[...] = near[0:block, :].astype(BF16)
    y1[...] = near[block:, :].astype(BF16)
    y2[...] = far[0:block, :].astype(BF16)
    y3[...] = far[block:, :].astype(BF16)


def expert_out(zn, zf, w2, block):
    both, f = 2 * block, zn.shape[1]
    d = w2.shape[1]
    step = f // 4
    return pl.pallas_call(
        expert_out_kernel,
        out_shape=[jax.ShapeDtypeStruct((both // 2, d), BF16)] * 4,
        in_specs=[VMEM_SPEC] * 2 + [FAR_SPEC],
        out_specs=[VMEM_SPEC] * 4,
        scratch_shapes=[pltpu.VMEM((4, step, d), BF16)]
        + [pltpu.VMEM((both, d), F32)] * 2
        + [pltpu.SemaphoreType.DMA((4,))],
        compiler_params=params(24),
        cost_estimate=cost(4 * d * f * both, 16e6),
    )(zn, zf, stay(w2))


def unpack_rows(dense, spread, seq, pad):
    spread[...] = jnp.zeros(spread.shape, F32)
    for n in range(dense.shape[0] // seq):
        spread[n * pad : n * pad + seq, :] = dense[n * seq : (n + 1) * seq, :]


def attn_bwd_kernel(
    idx, tok, g, da0, da1, da2, h1, qkv, p, o, a1, wfull, rt, gra, grb,
    gtok, pack_send, pack_keep,
    flat, da, gpad, dattn_all, dqkv, gains, grads, *, seq,
):
    i = pl.program_id(0)
    pad, d = tok.shape[1], tok.shape[2]
    rows = d // 4

    @pl.when(i == 0)
    def _():
        flat[...] = da0[...].astype(F32) + da1[...].astype(F32) + da2[...].astype(F32)
        unpack_rows(flat, da, seq, pad)
        flat[...] = g[0 : flat.shape[0], :].astype(F32)
        unpack_rows(flat, gpad, seq, pad)
        dattn_all[...] = jnp.zeros(dattn_all.shape, BF16)
        dqkv[...] = jnp.zeros(dqkv.shape, BF16)
        gains[...] = jnp.zeros(gains.shape, F32)

    here = pl.ds(pl.multiple_of(i * pad, TAIL), pad)
    valid = lax.broadcasted_iota(jnp.int32, (pad, 1), 0) < seq
    n2, r2 = norm_stats(h1[0])
    din = da[here, :]
    gains[1:2, :] += jnp.sum(din * n2, axis=0, keepdims=True)
    dh1 = gpad[here, :] + norm_back(din * rt[5:6, :], n2, r2)
    dattn = dh1.astype(BF16)
    dattn_all[here, :] = dattn
    do = nt(dattn, wfull[:, 3 * d : 4 * d]).astype(BF16)
    pairs = range(HEADS // 2)
    lanes = [slice(LANES * hp, LANES * (hp + 1)) for hp in pairs]
    klanes = [slice(d + LANES * hp, d + LANES * (hp + 1)) for hp in pairs]
    vlanes = [slice(2 * d + LANES * hp, 2 * d + LANES * (hp + 1)) for hp in pairs]
    do2 = [split_heads(do[:, lanes[hp]]) for hp in pairs]
    dp = [nt(do2[hp], qkv[0, :, vlanes[hp]]) for hp in pairs]
    for hp in pairs:
        dqkv[here, vlanes[hp]] = tn(p[0, hp], do2[hp])[0:pad].astype(BF16)
    wide = [p[0, hp].astype(F32) for hp in pairs]
    inner = [jnp.sum(dp[hp] * wide[hp], axis=-1, keepdims=True) for hp in pairs]
    ds = [(wide[hp] * (dp[hp] - inner[hp])).astype(BF16) for hp in pairs]
    for hp in pairs:
        dq = join_heads(nn(ds[hp], qkv[0, :, klanes[hp]]))
        dqkv[here, lanes[hp]] = (dq * HEAD_DIM**-0.5).astype(BF16)
        dk = tn(ds[hp], split_heads(qkv[0, 0:pad, lanes[hp]]))
        dqkv[here, klanes[hp]] = dk[0:pad].astype(BF16)
    din1 = nt(dqkv[here, :], wfull[:, 0 : 3 * d])
    x = jnp.where(valid, tok[0].astype(F32), 0.0)
    n1, r1 = norm_stats(x)
    gains[0:1, :] += jnp.sum(din1 * n1, axis=0, keepdims=True)
    gtok[0] = (dh1 + norm_back(din1 * rt[4:5, :], n1, r1)).astype(BF16)

    @pl.when(i == pl.num_programs(0) - 1)
    def _():
        grads[:, 0 : 3 * d] = tn(a1[...], dqkv[...]).astype(BF16)
        grads[:, 3 * d : 4 * d] = tn(o[...], dattn_all[...]).astype(BF16)
        row = lax.broadcasted_iota(jnp.int32, (TAIL, d), 0)
        tail = jnp.where(row < 4, gra[...] + grb[...], 0.0)
        tail = jnp.where(row == 4, gains[0:1, :], tail)
        gains[...] = jnp.where(row == 5, gains[1:2, :], tail)
        for n, (ref, slot) in enumerate(
            ((pack_keep, 0), (pack_send, 0), (pack_keep, 1), (pack_send, 1))
        ):
            at = pl.multiple_of(idx[n] * rows, rows)
            for m in range(4):
                ref[slot, m * rows : (m + 1) * rows, :] = grads[pl.ds(at, rows), m * d : (m + 1) * d]
            ref[slot, 4 * rows :, :] = jnp.zeros((ref.shape[1] - 4 * rows, d), BF16)
            ref[slot, 4 * rows : 4 * rows + TAIL, 0:rows] = gains[:, pl.ds(at, rows)].astype(BF16)


def attn_bwd(idx, tokens, g, das, h1, qkv, p, o, a1, wfull, rt, grs, seq, pad, pack_rows):
    images, _, d = tokens.shape
    block, padded = das[0].shape[0], a1.shape[0]
    keys = qkv.shape[1]
    image = lambda i: (i, 0, 0)
    return pl.pallas_call(
        functools.partial(attn_bwd_kernel, seq=seq),
        grid=(images,),
        out_shape=(
            jax.ShapeDtypeStruct(tokens.shape, BF16),
            pltpu.HBM((2, pack_rows, d), BF16),
            pltpu.HBM((2, pack_rows, d), BF16),
        ),
        in_specs=[SMEM_SPEC, pl.BlockSpec((1, pad, d), image), whole(g.shape)]
        + [whole((block, d)), VMEM_SPEC, VMEM_SPEC]
        + [
            pl.BlockSpec((1, pad, d), image),
            pl.BlockSpec((1, keys, 3 * d), image),
            pl.BlockSpec((1, HEADS // 2, 2 * pad, keys), lambda i: (i, 0, 0, 0)),
            whole((padded, d)),
            whole((padded, d)),
            whole((d, 4 * d)),
            whole((TAIL, d)),
            whole((TAIL, d)),
            whole((TAIL, d)),
        ],
        out_specs=(
            pl.BlockSpec((1, pad, d), image),
            whole((2, pack_rows, d)),
            whole((2, pack_rows, d)),
        ),
        scratch_shapes=[
            pltpu.VMEM((block, d), F32),
            pltpu.VMEM((padded, d), F32),
            pltpu.VMEM((padded, d), F32),
            pltpu.VMEM((padded, d), BF16),
            pltpu.VMEM((padded, 3 * d), BF16),
            pltpu.VMEM((TAIL, d), F32),
            pltpu.VMEM((d, 4 * d), BF16),
        ],
        compiler_params=params(40),
        cost_estimate=cost(LONG, 15e6),
    )(
        idx, stay(tokens), stay(g), stay(das[0]), *das[1:],
        *(stay(kept) for kept in (h1, qkv, p, o, a1, wfull)), rt, *grs,
    )


def output_kernel(h1, y0, y1, y2, ssq, out, sums, flat, moe, *, seq):
    i = pl.program_id(0)
    pad = h1.shape[1]

    @pl.when(i == 0)
    def _():
        flat[...] = y0[...].astype(F32) + y1[...].astype(F32) + y2[...].astype(F32)
        unpack_rows(flat, moe, seq, pad)
        sums[...] = jnp.zeros(sums.shape, F32)
        sums[1:2, :] = fold_lanes(ssq[0:1, :])

    branch = moe[pl.ds(pl.multiple_of(i * pad, TAIL), pad), :]
    result = h1[0] + branch
    sums[0:1, :] += fold_lanes(jnp.sum(result * result, axis=0, keepdims=True))
    sums[2:3, :] += fold_lanes(jnp.sum(branch * branch, axis=0, keepdims=True))
    out[0] = result.astype(BF16)


def output(h1, ys, ssq, seq):
    images, pad, d = h1.shape
    block = ys[0].shape[0]
    return pl.pallas_call(
        functools.partial(output_kernel, seq=seq),
        grid=(images,),
        out_shape=(
            jax.ShapeDtypeStruct((images, seq, d), BF16),
            jax.ShapeDtypeStruct((8, LANES), F32),
        ),
        in_specs=[pl.BlockSpec((1, pad, d), lambda i: (i, 0, 0))] + [VMEM_SPEC] * 4,
        out_specs=(pl.BlockSpec((1, pad, d), lambda i: (i, 0, 0)), whole((8, LANES))),
        scratch_shapes=[pltpu.VMEM((block, d), F32), pltpu.VMEM((images * pad, d), F32)],
        compiler_params=params(16),
        cost_estimate=cost(MEDIUM, 5e6),
    )(stay(h1), *ys, ssq)


def scatter_rows(a, axes, groups):
    count = len(groups[0])
    parts = a.reshape(count, a.shape[0] // count, a.shape[1])
    return lax.all_to_all(parts, axes, 0, 0, tiled=True, axis_index_groups=groups)


def add_rows(parts):
    return jnp.sum(parts.astype(F32), axis=0).astype(BF16)


def local(
    tokens,
    cotangent,
    gain_one,
    w_query,
    w_key,
    w_value,
    w_output,
    gain_two,
    w_router,
    w_in,
    w_out,
    routes,
):
    images, seq, d = tokens.shape
    experts = lax.axis_size("shard")
    pad = round_up(seq, TAIL)
    keys = round_up(seq, LANES)
    block = round_up(images * seq, TAIL)
    padded = round_up(images * pad, LANES)
    rows = w_query.shape[0]
    me = lax.axis_index("shard")
    reps = lax.axis_size("rep")
    everyone = ("shard", "rep")
    ring = [*range(0, reps, 2), *range(reps - 1, 0, -2)]
    rings = [[s * reps + r for r in ring] for s in range(experts)]
    idx = jnp.stack([me, me ^ 1, me ^ 2, me ^ 3]).astype(jnp.int32)
    core = lambda a: lax.ppermute(a, "shard", [(s, s ^ 1) for s in range(experts)])
    chip = lambda a: lax.ppermute(a, "shard", [(s, s ^ 2) for s in range(experts)])

    operands = (
        w_query, w_key, w_value, w_output,
        gain_one.reshape(1, rows), gain_two.reshape(1, rows), w_router.T,
    )
    wp = pl.pallas_call(
        pack_weights_kernel,
        grid=(1,),
        out_shape=pltpu.VMEM((rows + HEAD, 4 * d), BF16),
        in_specs=[whole(a.shape) for a in operands],
        out_specs=VMEM_SPEC,
        compiler_params=params(40),
        cost_estimate=cost(1e6, 3e6),
    )(*(stay(a) for a in operands))
    chosen = (routes[:, :, :, None] == jnp.arange(experts, dtype=jnp.int32)).any(axis=2)
    chosen = chosen.reshape(images * seq, experts).T
    chosen = jnp.pad(chosen, ((0, 0), (0, round_up(block, d) - images * seq)))
    chosen = chosen.reshape(experts, -1, d).transpose(1, 0, 2).reshape(-1, d)
    masks = jnp.pad(chosen, ((0, TAIL - chosen.shape[0]), (0, 0))).astype(BF16)
    gp = pl.pallas_call(
        pack_cotangent_kernel,
        grid=(1,),
        out_shape=jax.ShapeDtypeStruct((block + TAIL, d), BF16),
        in_specs=[whole(cotangent.shape), whole(masks.shape)],
        out_specs=whole((block + TAIL, d)),
        compiler_params=params(40),
        cost_estimate=cost(1e6, 1e6),
    )(stay(cotangent), masks)
    wx = after(chip(wp), gp)
    gx = chip(gp)
    packs = (wp, core(wp), wx, core(wx))
    gs = (gp, core(gp), gx, core(gx))
    w1, w2 = w_in[0], w_out[0]
    wfull, rt, qkv, p, o, a1, h1, a2, ssq = attn_fwd(
        idx, tokens, packs, seq, pad, keys, block, padded
    )
    ax = chip(a2)
    zn, dun, da, dac, grn, an, gn = expert(
        idx, (a2, core(after(a2, gx))), gs[:2], w1, w2, rt, True
    )
    ax = after(ax, zn)
    zf, duf, dax, daxc, grf, af, gf = expert(
        idx, (ax, core(ax)), gs[2:], w1, w2, rt, False
    )
    da_far = dax + core(daxc)
    grads_part = expert_grads(zn, zf, after(gn, da_far), gf, an, af, dun, duf)
    grads_slice = lax.psum_scatter(
        grads_part, everyone, scatter_dimension=0, tiled=True, axis_index_groups=rings
    )
    grad_tokens, send, keep = attn_bwd(
        idx, tokens, gp, (da, core(dac), chip(da_far)), after(h1, grads_part),
        qkv, p, o, a1, wfull, rt, (grn, grf), seq, pad, round_up(4 * rows + TAIL, 8 * reps),
    )
    got = core(send)
    pack_far = keep[1] + got[1]
    y, yc, yx, yxc = expert_out(after(zn, pack_far), zf, w2, block)
    pack = (
        after(keep, y)[0].astype(F32) + got[0].astype(F32) + chip(pack_far).astype(F32)
    ).astype(BF16)
    y_far = after(yx, pack) + core(yxc)
    grads = lax.all_gather(
        after(grads_slice, y_far), everyone, axis=0, axis_index_groups=rings
    )
    pack = add_rows(after(scatter_rows(pack, everyone, rings), grads_slice))
    kept = after(h1, pack)
    pack = lax.all_gather(pack, everyone, axis=0, tiled=True, axis_index_groups=rings)
    out, sums = output(kept, (y, core(yc), chip(y_far)), ssq, seq)
    sums = jnp.broadcast_to(after(sums, pack)[None], (experts * reps, *sums.shape))
    sums = lax.all_to_all(sums, everyone, 0, 0, tiled=True)
    totals = jnp.sum(sums, axis=(0, 2))
    gq, gk, gv, go, router, gain1, gain2 = unpack(pack, rows)
    gwo, gwi = place(grads, w1.shape[1])
    roots = jnp.sqrt(totals / float(experts * reps * images * seq * d))
    return (
        out,
        grad_tokens,
        gain1.reshape(rows),
        gq,
        gk,
        gv,
        go,
        gain2.reshape(rows),
        router.T,
        gwi,
        gwo,
        roots[0],
        roots[1],
        roots[2],
    )


def solution(mesh):
    spread = P(("shard", "rep"), None, None)
    matrix = P("shard", None)
    stack = P("shard", None, None)
    vector = P("shard")
    return jax.shard_map(
        local,
        mesh=mesh,
        in_specs=(
            spread, spread, vector, matrix, matrix, matrix, matrix, vector, matrix, stack, stack, spread,
        ),
        out_specs=(
            spread, spread, vector, matrix, matrix, matrix, matrix, vector, matrix, stack, stack, P(), P(), P(),
        ),
        check_vma=False,
    )
```

```python
import functools

import jax
import jax.numpy as jnp
from jax import lax
from jax.experimental import pallas as pl
from jax.experimental.pallas import tpu as pltpu
from jax.sharding import PartitionSpec as P

HEADS = 8
HEAD_DIM = 64
EPSILON = 1e-06
LANES = 128
TAIL = 16
HEAD = 8
LONG = 1e11
MEDIUM = 6.4e10

BF16 = jnp.bfloat16
F32 = jnp.float32

LOG2E = 1.4426950408889634
ROOT_HALF = 0.7071067811865476
INV_ROOT_2PI = 0.3989422804014327


def round_up(value, multiple):
    return (value + multiple - 1) // multiple * multiple


def nn(a, b):
    return lax.dot_general(a, b, (((1,), (0,)), ((), ())), preferred_element_type=F32)


def nt(a, b):
    return lax.dot_general(a, b, (((1,), (1,)), ((), ())), preferred_element_type=F32)


def tn(a, b):
    return lax.dot_general(a, b, (((0,), (0,)), ((), ())), preferred_element_type=F32)


def norm_stats(values):
    center = values - jnp.mean(values, axis=-1, keepdims=True)
    inverse = lax.rsqrt(jnp.mean(center * center, axis=-1, keepdims=True) + EPSILON)
    return center * inverse, inverse


def norm_back(grad_normed, normed, inverse):
    mean_plain = jnp.mean(grad_normed, axis=-1, keepdims=True)
    mean_cross = jnp.mean(grad_normed * normed, axis=-1, keepdims=True)
    return inverse * (grad_normed - mean_plain - normed * mean_cross)


def gelu_pair(u):
    cdf = 0.5 * lax.erf(u * ROOT_HALF) + 0.5
    return u * cdf, cdf + u * (jnp.exp2(u * u * (-0.5 * LOG2E)) * INV_ROOT_2PI)


def split_heads(pair):
    low = lax.broadcasted_iota(jnp.int32, pair.shape, 1) < HEAD_DIM
    zero = jnp.zeros_like(pair)
    return jnp.concatenate([jnp.where(low, pair, zero), jnp.where(low, zero, pair)], axis=0)


def join_heads(stacked):
    rows = stacked.shape[0] // 2
    low = lax.broadcasted_iota(jnp.int32, (rows, stacked.shape[1]), 1) < HEAD_DIM
    return jnp.where(low, stacked[:rows], stacked[rows:])


def after(value, *first):
    return lax.optimization_barrier((value, *first))[0]


def stay(array):
    return pltpu.with_memory_space_constraint(array, pltpu.HBM)


def params(mebibytes=60):
    return pltpu.CompilerParams(vmem_limit_bytes=mebibytes * 1024 * 1024)


def cost(flops, nbytes, trans=0):
    return pl.CostEstimate(flops=int(flops), bytes_accessed=int(nbytes), transcendentals=int(trans))


def whole(shape):
    return pl.BlockSpec(shape, lambda *_: (0,) * len(shape))


SMEM_SPEC = pl.BlockSpec(memory_space=pltpu.SMEM)
VMEM_SPEC = pl.BlockSpec(memory_space=pltpu.VMEM)
FAR_SPEC = pl.BlockSpec(memory_space=pl.ANY)


def pack_weights_kernel(wq, wk, wv, wo, g1, g2, wr, wp):
    rows, d = wq.shape
    for n, w in enumerate((wq, wk, wv, wo)):
        wp[0:rows, n * d : (n + 1) * d] = w[...]
    blank = jnp.zeros((HEAD - wr.shape[0], LANES), F32)
    head = jnp.concatenate([wr[...].astype(F32), blank], axis=0)
    row = lax.broadcasted_iota(jnp.int32, (HEAD, LANES), 0)
    head = jnp.where(row == 4, g1[...].astype(F32), head)
    head = jnp.where(row == 5, g2[...].astype(F32), head)
    wp[rows:, :] = jnp.zeros((HEAD, wp.shape[1]), BF16)
    wp[rows:, 0:LANES] = head.astype(BF16)


def pack_cotangent_kernel(cot, masks, gp):
    seq = cot.shape[1]
    gp[...] = jnp.zeros(gp.shape, BF16)
    for i in range(cot.shape[0]):
        gp[i * seq : (i + 1) * seq, :] = cot[i]
    gp[gp.shape[0] - TAIL :, :] = masks[...]


def attn_fwd_kernel(
    idx, tok, w0, w1, w2, w3, wfull, rt, qkv, p, o, a1, h1, a2, ssq, *, seq, h1_images
):
    i = pl.program_id(0)
    pad, d = tok.shape[1], tok.shape[2]
    keys = qkv.shape[1]
    rows = w0.shape[0] - HEAD

    @pl.when(i == 0)
    def _():
        for n, w in enumerate((w0, w1, w2, w3)):
            at = pl.multiple_of(idx[n] * rows, rows)
            wfull[pl.ds(at, rows), :] = w[0:rows, :]
            rt[0:HEAD, pl.ds(at, rows)] = w[rows:, 0:rows].astype(F32)
            rt[HEAD:, pl.ds(at, rows)] = jnp.zeros((TAIL - HEAD, rows), F32)
        for ref in (o, a1, a2):
            ref[...] = jnp.zeros(ref.shape, ref.dtype)
        ssq[...] = jnp.zeros(ssq.shape, F32)

    here = pl.ds(pl.multiple_of(i * pad, TAIL), pad)
    valid = lax.broadcasted_iota(jnp.int32, (pad, 1), 0) < seq
    x = jnp.where(valid, tok[0].astype(F32), 0.0)
    n1, _ = norm_stats(x)
    in_one = (n1 * rt[4:5, :]).astype(BF16)
    a1[here, :] = in_one
    proj = nn(in_one, wfull[:, 0 : 3 * d])
    qkv[0, 0:pad, 0:d] = (proj[:, 0:d].astype(BF16).astype(F32) * HEAD_DIM**-0.5).astype(BF16)
    qkv[0, 0:pad, d:] = proj[:, d:].astype(BF16)
    qkv[0, pad:keys, :] = jnp.zeros((keys - pad, 3 * d), BF16)
    column = lax.broadcasted_iota(jnp.int32, (1, keys), 1) < seq
    pairs = range(HEADS // 2)
    lanes = [slice(LANES * hp, LANES * (hp + 1)) for hp in pairs]
    scores = [
        nt(split_heads(qkv[0, 0:pad, lanes[hp]]), qkv[0, :, d + LANES * hp : d + LANES * (hp + 1)])
        for hp in pairs
    ]
    scores = [jnp.where(column, score, -1e30) for score in scores]
    tops = [jnp.max(score, axis=-1, keepdims=True) for score in scores]
    raised = [jnp.exp(score - top) for score, top in zip(scores, tops)]
    totals = [1.0 / jnp.sum(each, axis=-1, keepdims=True) for each in raised]
    for hp in pairs:
        p[0, hp] = (raised[hp] * totals[hp]).astype(BF16)
    for hp in pairs:
        mixed = nn(p[0, hp], qkv[0, :, 2 * d + LANES * hp : 2 * d + LANES * (hp + 1)])
        o[here, lanes[hp]] = join_heads(mixed).astype(BF16)
    attn = jnp.where(valid, nn(o[here, :], wfull[:, 3 * d : 4 * d]), 0.0)
    ssq[0:1, :] += jnp.sum(attn * attn, axis=0, keepdims=True)
    after = x + attn
    h1[0] = after
    n2, _ = norm_stats(after)
    in_two = (n2 * rt[5:6, :]).astype(BF16)
    for n in range(h1_images):

        @pl.when(i == n)
        def _(n=n):
            a2[n * seq : (n + 1) * seq, :] = in_two[0:seq]


def attn_fwd(idx, tokens, packs, seq, pad, keys, block, padded):
    images, _, d = tokens.shape
    out_shape = (
        pltpu.HBM((d, 4 * d), BF16),
        jax.ShapeDtypeStruct((TAIL, d), F32),
        pltpu.HBM((images, keys, 3 * d), BF16),
        pltpu.HBM((images, HEADS // 2, 2 * pad, keys), BF16),
        pltpu.HBM((padded, d), BF16),
        pltpu.HBM((padded, d), BF16),
        pltpu.HBM((images, pad, d), F32),
        pltpu.VMEM((block, d), BF16),
        jax.ShapeDtypeStruct((8, d), F32),
    )
    return pl.pallas_call(
        functools.partial(attn_fwd_kernel, seq=seq, h1_images=images),
        grid=(images,),
        out_shape=out_shape,
        in_specs=[SMEM_SPEC, pl.BlockSpec((1, pad, d), lambda i: (i, 0, 0))]
        + [VMEM_SPEC] * 4,
        out_specs=(
            whole((d, 4 * d)),
            whole((TAIL, d)),
            pl.BlockSpec((1, keys, 3 * d), lambda i: (i, 0, 0)),
            pl.BlockSpec((1, HEADS // 2, 2 * pad, keys), lambda i: (i, 0, 0, 0)),
            whole((padded, d)),
            whole((padded, d)),
            pl.BlockSpec((1, pad, d), lambda i: (i, 0, 0)),
            VMEM_SPEC,
            whole((8, d)),
        ),
        compiler_params=params(40),
        cost_estimate=cost(1, 1),
    )(idx, stay(tokens), *packs)


def chosen_row(idx, ref, block, width):
    masks = ref[block:, :].astype(F32)
    d = masks.shape[1]
    row = lax.broadcasted_iota(jnp.int32, masks.shape, 0)
    parts = [
        jnp.sum(jnp.where(row == 4 * n + idx[0], masks, 0.0), axis=0, keepdims=True)
        for n in range((block + d - 1) // d)
    ]
    parts.append(jnp.zeros((1, width - d * len(parts)), F32))
    return jnp.concatenate(parts, axis=1)


def route(idx, a2s, rt, ga, gb, block):
    width = a2s.shape[0]
    row = lax.broadcasted_iota(jnp.int32, (TAIL, width), 0)
    logits = jnp.where(row < 4, nt(rt[...].astype(BF16), a2s[...]), -1e30)
    raised = jnp.exp(logits - jnp.max(logits, axis=0, keepdims=True))
    share = raised / jnp.sum(raised, axis=0, keepdims=True)
    chosen = chosen_row(idx, ga, block, width)
    chosen += pltpu.roll(chosen_row(idx, gb, block, width), block, 1)
    mine = jnp.sum(jnp.where(row == idx[0], share, 0.0), axis=0, keepdims=True)
    return jnp.where(row == HEAD, chosen * mine, share).T


def fold_lanes(wide):
    parts = [wide[:, n : n + LANES] for n in range(0, wide.shape[1], LANES)]
    return sum(parts[1:], parts[0])


def gather_rows(a2a, a2b, ga, gb, a2s, gs):
    block = a2a.shape[0]
    for ref, first, second in ((a2s, a2a, a2b), (gs, ga, gb)):
        ref[0:block, :] = first[0:block, :]
        ref[block : 2 * block, :] = second[0:block, :]
        ref[2 * block :, :] = jnp.zeros((ref.shape[0] - 2 * block, ref.shape[1]), BF16)


def finish_rows(idx, probs, dcomb, total, a2s, rt, da, db, gr):
    block = da.shape[0]
    lane = lax.broadcasted_iota(jnp.int32, probs.shape, 1)
    own = (lane == idx[0]).astype(F32)
    inner = jnp.sum(dcomb[...], axis=1, keepdims=True)
    dlogits = jnp.where(lane < 4, inner * (own - probs[...]), 0.0).astype(BF16)
    gr[...] = tn(dlogits, a2s[...])
    result = (total[...] + nn(dlogits[0 : 2 * block], rt[...].astype(BF16))).astype(BF16)
    da[...] = result[0:block]
    db[...] = result[block:]


def expert_kernel(
    idx, a2a, a2b, ga, gb, w1_far, w2_far, rt,
    zc, du, da, db, gr, a2s, gs, w1, w2, probs, dcomb, total, sem1, sem2,
):
    block = a2a.shape[0]
    step = w1.shape[2]
    loads = []
    for j in range(w1.shape[0]):
        here = pl.ds(j * step, step)
        loads.append(pltpu.make_async_copy(w1_far.at[:, here], w1.at[j], sem1.at[j]))
        loads.append(pltpu.make_async_copy(w2_far.at[here], w2.at[j], sem2.at[j]))
    for copy in loads:
        copy.start()
    gather_rows(a2a, a2b, ga, gb, a2s, gs)
    probs[...] = route(idx, a2s, rt, ga, gb, block)
    total[...] = jnp.zeros(total.shape, F32)
    dcomb[...] = jnp.zeros(dcomb.shape, F32)
    for ref in (zc, du):
        ref[2 * block :, :] = jnp.zeros((ref.shape[0] - 2 * block, ref.shape[1]), BF16)

    @pl.loop(0, w1.shape[0])
    def _(j):
        here = pl.ds(pl.multiple_of(j * step, LANES), step)
        pltpu.make_async_copy(w1_far.at[:, here], w1.at[j], sem1.at[j]).wait()
        pltpu.make_async_copy(w2_far.at[here], w2.at[j], sem2.at[j]).wait()
        halves = [slice(0, block), slice(block, 2 * block)]
        us = [nn(a2s[r, :], w1[j]) for r in halves]
        dzs = [nt(gs[r, :], w2[j]) for r in halves]
        for r, u, dz in zip(halves, us, dzs):
            act, slope = gelu_pair(u)
            scale = probs[r, HEAD : HEAD + 1]
            mixed = (act * scale).astype(BF16)
            zc[r, here] = mixed
            dcomb[r, :] += fold_lanes(mixed.astype(F32) * dz)
            grad = (slope * scale * dz).astype(BF16)
            du[r, here] = grad
            total[r, :] += nt(grad, w1[j])

    finish_rows(idx, probs, dcomb, total, a2s, rt, da, db, gr)


def expert(idx, a2s, gs, w1, w2, rt, near):
    block, d = a2s[0].shape
    f = w1.shape[1]
    both = 2 * block
    rows = round_up(both, 2 * LANES)
    step = f // 4
    return pl.pallas_call(
        expert_kernel,
        out_shape=(
            pltpu.VMEM((rows, f), BF16),
            pltpu.VMEM((rows, f), BF16),
            pltpu.HBM((block, d), BF16) if near else pltpu.VMEM((block, d), BF16),
            pltpu.VMEM((block, d), BF16),
            jax.ShapeDtypeStruct((TAIL, d), F32),
            pltpu.VMEM((rows, d), BF16),
            pltpu.VMEM((rows, d), BF16),
        ),
        in_specs=[SMEM_SPEC] + [VMEM_SPEC] * 4 + [FAR_SPEC] * 2 + [VMEM_SPEC],
        out_specs=(VMEM_SPEC,) * 2
        + (pl.BlockSpec((block, d), lambda: (0, 0)) if near else VMEM_SPEC,)
        + (VMEM_SPEC,) * 4,
        scratch_shapes=[
            pltpu.VMEM((4, d, step), BF16),
            pltpu.VMEM((4, step, d), BF16),
            pltpu.VMEM((rows, TAIL), F32),
            pltpu.VMEM((rows, LANES), F32),
            pltpu.VMEM((both, d), F32),
            pltpu.SemaphoreType.DMA((4,)),
            pltpu.SemaphoreType.DMA((4,)),
        ],
        compiler_params=params(26),
        cost_estimate=cost(6 * both * d * f, 25e6, 2 * both * f),
    )(idx, *a2s, *gs, stay(w1), stay(w2), rt)


def grads_kernel(zn, zf, gn, gf, an, af, dn, df, out, parts, sem):
    d = gn.shape[1]
    count, tall, _ = parts.shape
    half = count // 2

    @pl.loop(0, half)
    def _(j):
        here = pl.ds(pl.multiple_of(j * tall, LANES), tall)
        parts[j] = (tn(zn[:, here], gn[...]) + tn(zf[:, here], gf[...])).astype(BF16)
        pltpu.make_async_copy(parts.at[j], out.at[here], sem.at[j]).start()

    @pl.loop(half, count)
    def _(j):
        for n in range(tall // d):
            here = pl.ds(pl.multiple_of((j - half) * tall + n * d, LANES), d)
            grad = tn(an[...], dn[:, here]) + tn(af[...], df[:, here])
            parts[j, n * d : (n + 1) * d, :] = grad.astype(BF16)
        here = pl.ds(pl.multiple_of(j * tall, LANES), tall)
        pltpu.make_async_copy(parts.at[j], out.at[here], sem.at[j]).start()

    for j in range(count):
        pltpu.make_async_copy(parts.at[j], out.at[pl.ds(j * tall, tall)], sem.at[j]).wait()


def expert_grads(zn, zf, gn, gf, an, af, dn, df):
    both, f = zn.shape
    d = gn.shape[1]
    return pl.pallas_call(
        grads_kernel,
        out_shape=pltpu.HBM((2 * f, d), BF16),
        in_specs=[VMEM_SPEC] * 8,
        out_specs=FAR_SPEC,
        scratch_shapes=[
            pltpu.VMEM((4, f // 2, d), BF16),
            pltpu.SemaphoreType.DMA((4,)),
        ],
        compiler_params=params(16),
        cost_estimate=cost(8 * both * d * f, 25e6),
    )(zn, zf, gn, gf, an, af, dn, df)


def place_kernel(grads, gwo, gwi, low, wide, in_sem, out_sem):
    count, large, d = wide.shape
    half, runs = count // 2, d // large
    loads, stores = [], []
    for c in range(count):
        loads.append(pltpu.make_async_copy(grads.at[c], low.at[c], in_sem.at[c]))
        for n in range(2):
            piece = pl.ds(n * large // 2, large // 2)
            if c < half:
                target = gwo.at[0, pl.ds(c * large + n * large // 2, large // 2)]
            else:
                k = c - half
                start = k % runs * large + n * large // 2
                target = gwi.at[0, pl.ds(start, large // 2), pl.ds(k // runs * d, d)]
            source = wide.at[c, piece]
            stores.append(pltpu.make_async_copy(source, target, out_sem.at[2 * c + n]))
    for copy in loads:
        copy.start()
    for c in range(count):
        loads[c].wait()
        for n in range(2):
            piece = slice(n * large // 2, (n + 1) * large // 2)
            wide[c, piece, :] = low[c, piece, :].astype(F32)
            stores[2 * c + n].start()
    for copy in stores:
        copy.wait()


def place(grads, f):
    count, large, d = grads.shape
    return pl.pallas_call(
        place_kernel,
        out_shape=(pltpu.HBM((1, f, d), F32), pltpu.HBM((1, d, f), F32)),
        in_specs=[FAR_SPEC],
        out_specs=(FAR_SPEC, FAR_SPEC),
        scratch_shapes=[
            pltpu.VMEM((count, large, d), BF16),
            pltpu.VMEM((count, large, d), F32),
            pltpu.SemaphoreType.DMA((count,)),
            pltpu.SemaphoreType.DMA((2 * count,)),
        ],
        compiler_params=params(40),
        cost_estimate=cost(1e6, 12e6),
    )(stay(grads))


def unpack_kernel(pack, gq, gk, gv, go, router, gain1, gain2):
    rows = gq.shape[0]
    for n, ref in enumerate((gq, gk, gv, go)):
        ref[...] = pack[n * rows : (n + 1) * rows, :].astype(F32)
    tail = pack[4 * rows : 4 * rows + TAIL, 0:rows].astype(F32)
    router[...] = tail[0:4]
    gain1[...] = tail[4:5]
    gain2[...] = tail[5:6]


def unpack(pack, rows):
    d = pack.shape[1]
    shapes = [(rows, d)] * 4 + [(4, rows), (1, rows), (1, rows)]
    return pl.pallas_call(
        unpack_kernel,
        out_shape=[jax.ShapeDtypeStruct(shape, F32) for shape in shapes],
        compiler_params=params(40),
        cost_estimate=cost(1e6, 2e6),
    )(pack)


def expert_out_kernel(zn, zf, w2_far, y0, y1, y2, y3, w2, near, far, sem):
    block = y0.shape[0]
    step = w2.shape[1]
    for j in range(w2.shape[0]):
        pltpu.make_async_copy(w2_far.at[pl.ds(j * step, step)], w2.at[j], sem.at[j]).start()
    near[...] = jnp.zeros(near.shape, F32)
    far[...] = jnp.zeros(far.shape, F32)

    @pl.loop(0, w2.shape[0])
    def _(j):
        here = pl.ds(pl.multiple_of(j * step, LANES), step)
        pltpu.make_async_copy(w2_far.at[here], w2.at[j], sem.at[j]).wait()
        near[...] += nn(zn[0 : 2 * block, here], w2[j])
        far[...] += nn(zf[0 : 2 * block, here], w2[j])

    y0[...] = near[0:block, :].astype(BF16)
    y1[...] = near[block:, :].astype(BF16)
    y2[...] = far[0:block, :].astype(BF16)
    y3[...] = far[block:, :].astype(BF16)


def expert_out(zn, zf, w2, block):
    both, f = 2 * block, zn.shape[1]
    d = w2.shape[1]
    step = f // 4
    return pl.pallas_call(
        expert_out_kernel,
        out_shape=[jax.ShapeDtypeStruct((both // 2, d), BF16)] * 4,
        in_specs=[VMEM_SPEC] * 2 + [FAR_SPEC],
        out_specs=[VMEM_SPEC] * 4,
        scratch_shapes=[pltpu.VMEM((4, step, d), BF16)]
        + [pltpu.VMEM((both, d), F32)] * 2
        + [pltpu.SemaphoreType.DMA((4,))],
        compiler_params=params(24),
        cost_estimate=cost(4 * d * f * both, 16e6),
    )(zn, zf, stay(w2))


def unpack_rows(dense, spread, seq, pad):
    spread[...] = jnp.zeros(spread.shape, F32)
    for n in range(dense.shape[0] // seq):
        spread[n * pad : n * pad + seq, :] = dense[n * seq : (n + 1) * seq, :]


def attn_bwd_kernel(
    idx, tok, g, da0, da1, da2, h1, qkv, p, o, a1, wfull, rt, gra, grb,
    gtok, pack_send, pack_keep,
    flat, da, gpad, dattn_all, dqkv, gains, grads, *, seq,
):
    i = pl.program_id(0)
    pad, d = tok.shape[1], tok.shape[2]
    rows = d // 4

    @pl.when(i == 0)
    def _():
        flat[...] = da0[...].astype(F32) + da1[...].astype(F32) + da2[...].astype(F32)
        unpack_rows(flat, da, seq, pad)
        flat[...] = g[0 : flat.shape[0], :].astype(F32)
        unpack_rows(flat, gpad, seq, pad)
        dattn_all[...] = jnp.zeros(dattn_all.shape, BF16)
        dqkv[...] = jnp.zeros(dqkv.shape, BF16)
        gains[...] = jnp.zeros(gains.shape, F32)

    here = pl.ds(pl.multiple_of(i * pad, TAIL), pad)
    valid = lax.broadcasted_iota(jnp.int32, (pad, 1), 0) < seq
    n2, r2 = norm_stats(h1[0])
    din = da[here, :]
    gains[1:2, :] += jnp.sum(din * n2, axis=0, keepdims=True)
    dh1 = gpad[here, :] + norm_back(din * rt[5:6, :], n2, r2)
    dattn = dh1.astype(BF16)
    dattn_all[here, :] = dattn
    do = nt(dattn, wfull[:, 3 * d : 4 * d]).astype(BF16)
    pairs = range(HEADS // 2)
    lanes = [slice(LANES * hp, LANES * (hp + 1)) for hp in pairs]
    klanes = [slice(d + LANES * hp, d + LANES * (hp + 1)) for hp in pairs]
    vlanes = [slice(2 * d + LANES * hp, 2 * d + LANES * (hp + 1)) for hp in pairs]
    do2 = [split_heads(do[:, lanes[hp]]) for hp in pairs]
    dp = [nt(do2[hp], qkv[0, :, vlanes[hp]]) for hp in pairs]
    for hp in pairs:
        dqkv[here, vlanes[hp]] = tn(p[0, hp], do2[hp])[0:pad].astype(BF16)
    wide = [p[0, hp].astype(F32) for hp in pairs]
    inner = [jnp.sum(dp[hp] * wide[hp], axis=-1, keepdims=True) for hp in pairs]
    ds = [(wide[hp] * (dp[hp] - inner[hp])).astype(BF16) for hp in pairs]
    for hp in pairs:
        dq = join_heads(nn(ds[hp], qkv[0, :, klanes[hp]]))
        dqkv[here, lanes[hp]] = (dq * HEAD_DIM**-0.5).astype(BF16)
        dk = tn(ds[hp], split_heads(qkv[0, 0:pad, lanes[hp]]))
        dqkv[here, klanes[hp]] = dk[0:pad].astype(BF16)
    din1 = nt(dqkv[here, :], wfull[:, 0 : 3 * d])
    x = jnp.where(valid, tok[0].astype(F32), 0.0)
    n1, r1 = norm_stats(x)
    gains[0:1, :] += jnp.sum(din1 * n1, axis=0, keepdims=True)
    gtok[0] = (dh1 + norm_back(din1 * rt[4:5, :], n1, r1)).astype(BF16)

    @pl.when(i == pl.num_programs(0) - 1)
    def _():
        grads[:, 0 : 3 * d] = tn(a1[...], dqkv[...]).astype(BF16)
        grads[:, 3 * d : 4 * d] = tn(o[...], dattn_all[...]).astype(BF16)
        row = lax.broadcasted_iota(jnp.int32, (TAIL, d), 0)
        tail = jnp.where(row < 4, gra[...] + grb[...], 0.0)
        tail = jnp.where(row == 4, gains[0:1, :], tail)
        gains[...] = jnp.where(row == 5, gains[1:2, :], tail)
        for n, (ref, slot) in enumerate(
            ((pack_keep, 0), (pack_send, 0), (pack_keep, 1), (pack_send, 1))
        ):
            at = pl.multiple_of(idx[n] * rows, rows)
            for m in range(4):
                ref[slot, m * rows : (m + 1) * rows, :] = grads[pl.ds(at, rows), m * d : (m + 1) * d]
            ref[slot, 4 * rows :, :] = jnp.zeros((ref.shape[1] - 4 * rows, d), BF16)
            ref[slot, 4 * rows : 4 * rows + TAIL, 0:rows] = gains[:, pl.ds(at, rows)].astype(BF16)


def attn_bwd(idx, tokens, g, das, h1, qkv, p, o, a1, wfull, rt, grs, seq, pad, pack_rows):
    images, _, d = tokens.shape
    block, padded = das[0].shape[0], a1.shape[0]
    keys = qkv.shape[1]
    image = lambda i: (i, 0, 0)
    return pl.pallas_call(
        functools.partial(attn_bwd_kernel, seq=seq),
        grid=(images,),
        out_shape=(
            jax.ShapeDtypeStruct(tokens.shape, BF16),
            pltpu.HBM((2, pack_rows, d), BF16),
            pltpu.HBM((2, pack_rows, d), BF16),
        ),
        in_specs=[SMEM_SPEC, pl.BlockSpec((1, pad, d), image), whole(g.shape)]
        + [whole((block, d)), VMEM_SPEC, VMEM_SPEC]
        + [
            pl.BlockSpec((1, pad, d), image),
            pl.BlockSpec((1, keys, 3 * d), image),
            pl.BlockSpec((1, HEADS // 2, 2 * pad, keys), lambda i: (i, 0, 0, 0)),
            whole((padded, d)),
            whole((padded, d)),
            whole((d, 4 * d)),
            whole((TAIL, d)),
            whole((TAIL, d)),
            whole((TAIL, d)),
        ],
        out_specs=(
            pl.BlockSpec((1, pad, d), image),
            whole((2, pack_rows, d)),
            whole((2, pack_rows, d)),
        ),
        scratch_shapes=[
            pltpu.VMEM((block, d), F32),
            pltpu.VMEM((padded, d), F32),
            pltpu.VMEM((padded, d), F32),
            pltpu.VMEM((padded, d), BF16),
            pltpu.VMEM((padded, 3 * d), BF16),
            pltpu.VMEM((TAIL, d), F32),
            pltpu.VMEM((d, 4 * d), BF16),
        ],
        compiler_params=params(40),
        cost_estimate=cost(LONG, 15e6),
    )(
        idx, stay(tokens), stay(g), stay(das[0]), *das[1:],
        *(stay(kept) for kept in (h1, qkv, p, o, a1, wfull)), rt, *grs,
    )


def output_kernel(h1, y0, y1, y2, ssq, out, sums, flat, moe, *, seq):
    i = pl.program_id(0)
    pad = h1.shape[1]

    @pl.when(i == 0)
    def _():
        flat[...] = y0[...].astype(F32) + y1[...].astype(F32) + y2[...].astype(F32)
        unpack_rows(flat, moe, seq, pad)
        sums[...] = jnp.zeros(sums.shape, F32)
        sums[1:2, :] = fold_lanes(ssq[0:1, :])

    branch = moe[pl.ds(pl.multiple_of(i * pad, TAIL), pad), :]
    result = h1[0] + branch
    sums[0:1, :] += fold_lanes(jnp.sum(result * result, axis=0, keepdims=True))
    sums[2:3, :] += fold_lanes(jnp.sum(branch * branch, axis=0, keepdims=True))
    out[0] = result.astype(BF16)


def output(h1, ys, ssq, seq):
    images, pad, d = h1.shape
    block = ys[0].shape[0]
    return pl.pallas_call(
        functools.partial(output_kernel, seq=seq),
        grid=(images,),
        out_shape=(
            jax.ShapeDtypeStruct((images, seq, d), BF16),
            jax.ShapeDtypeStruct((8, LANES), F32),
        ),
        in_specs=[pl.BlockSpec((1, pad, d), lambda i: (i, 0, 0))] + [VMEM_SPEC] * 4,
        out_specs=(pl.BlockSpec((1, pad, d), lambda i: (i, 0, 0)), whole((8, LANES))),
        scratch_shapes=[pltpu.VMEM((block, d), F32), pltpu.VMEM((images * pad, d), F32)],
        compiler_params=params(16),
        cost_estimate=cost(MEDIUM, 5e6),
    )(stay(h1), *ys, ssq)


def scatter_rows(a, axes, groups):
    count = len(groups[0])
    parts = a.reshape(count, a.shape[0] // count, a.shape[1])
    return lax.all_to_all(parts, axes, 0, 0, tiled=True, axis_index_groups=groups)


def add_rows(parts):
    return jnp.sum(parts.astype(F32), axis=0).astype(BF16)


def local(
    tokens,
    cotangent,
    gain_one,
    w_query,
    w_key,
    w_value,
    w_output,
    gain_two,
    w_router,
    w_in,
    w_out,
    routes,
):
    images, seq, d = tokens.shape
    experts = lax.axis_size("shard")
    pad = round_up(seq, TAIL)
    keys = round_up(seq, LANES)
    block = round_up(images * seq, TAIL)
    padded = round_up(images * pad, LANES)
    rows = w_query.shape[0]
    me = lax.axis_index("shard")
    reps = lax.axis_size("rep")
    everyone = ("shard", "rep")
    ring = [*range(0, reps, 2), *range(reps - 1, 0, -2)]
    rings = [[s * reps + r for r in ring] for s in range(experts)]
    idx = jnp.stack([me, me ^ 1, me ^ 2, me ^ 3]).astype(jnp.int32)
    core = lambda a: lax.ppermute(a, "shard", [(s, s ^ 1) for s in range(experts)])
    chip = lambda a: lax.ppermute(a, "shard", [(s, s ^ 2) for s in range(experts)])

    operands = (
        w_query, w_key, w_value, w_output,
        gain_one.reshape(1, rows), gain_two.reshape(1, rows), w_router.T,
    )
    wp = pl.pallas_call(
        pack_weights_kernel,
        grid=(1,),
        out_shape=pltpu.VMEM((rows + HEAD, 4 * d), BF16),
        in_specs=[whole(a.shape) for a in operands],
        out_specs=VMEM_SPEC,
        compiler_params=params(40),
        cost_estimate=cost(1e6, 3e6),
    )(*(stay(a) for a in operands))
    chosen = (routes[:, :, :, None] == jnp.arange(experts, dtype=jnp.int32)).any(axis=2)
    chosen = chosen.reshape(images * seq, experts).T
    chosen = jnp.pad(chosen, ((0, 0), (0, round_up(block, d) - images * seq)))
    chosen = chosen.reshape(experts, -1, d).transpose(1, 0, 2).reshape(-1, d)
    masks = jnp.pad(chosen, ((0, TAIL - chosen.shape[0]), (0, 0))).astype(BF16)
    gp = pl.pallas_call(
        pack_cotangent_kernel,
        grid=(1,),
        out_shape=jax.ShapeDtypeStruct((block + TAIL, d), BF16),
        in_specs=[whole(cotangent.shape), whole(masks.shape)],
        out_specs=whole((block + TAIL, d)),
        compiler_params=params(40),
        cost_estimate=cost(1e6, 1e6),
    )(stay(cotangent), masks)
    wx = after(chip(wp), gp)
    gx = chip(gp)
    packs = (wp, core(wp), wx, core(wx))
    gs = (gp, core(gp), gx, core(gx))
    w1, w2 = w_in[0], w_out[0]
    wfull, rt, qkv, p, o, a1, h1, a2, ssq = attn_fwd(
        idx, tokens, packs, seq, pad, keys, block, padded
    )
    ax = chip(a2)
    zn, dun, da, dac, grn, an, gn = expert(
        idx, (a2, core(after(a2, gx))), gs[:2], w1, w2, rt, True
    )
    ax = after(ax, zn)
    zf, duf, dax, daxc, grf, af, gf = expert(
        idx, (ax, core(ax)), gs[2:], w1, w2, rt, False
    )
    da_far = dax + core(daxc)
    grads_part = expert_grads(zn, zf, after(gn, da_far), gf, an, af, dun, duf)
    grads_slice = lax.psum_scatter(
        grads_part, everyone, scatter_dimension=0, tiled=True, axis_index_groups=rings
    )
    grad_tokens, send, keep = attn_bwd(
        idx, tokens, gp, (da, core(dac), chip(da_far)), after(h1, grads_part),
        qkv, p, o, a1, wfull, rt, (grn, grf), seq, pad, round_up(4 * rows + TAIL, 8 * reps),
    )
    got = core(send)
    pack_far = keep[1] + got[1]
    y, yc, yx, yxc = expert_out(after(zn, pack_far), zf, w2, block)
    pack = (
        after(keep, y)[0].astype(F32) + got[0].astype(F32) + chip(pack_far).astype(F32)
    ).astype(BF16)
    y_far = after(yx, pack) + core(yxc)
    grads = lax.all_gather(
        after(grads_slice, y_far), everyone, axis=0, axis_index_groups=rings
    )
    pack = add_rows(after(scatter_rows(pack, everyone, rings), grads_slice))
    kept = after(h1, pack)
    pack = lax.all_gather(pack, everyone, axis=0, tiled=True, axis_index_groups=rings)
    out, sums = output(kept, (y, core(yc), chip(y_far)), ssq, seq)
    sums = jnp.broadcast_to(after(sums, pack)[None], (experts * reps, *sums.shape))
    sums = lax.all_to_all(sums, everyone, 0, 0, tiled=True)
    totals = jnp.sum(sums, axis=(0, 2))
    gq, gk, gv, go, router, gain1, gain2 = unpack(pack, rows)
    gwo, gwi = place(grads, w1.shape[1])
    roots = jnp.sqrt(totals / float(experts * reps * images * seq * d))
    return (
        out,
        grad_tokens,
        gain1.reshape(rows),
        gq,
        gk,
        gv,
        go,
        gain2.reshape(rows),
        router.T,
        gwi,
        gwo,
        roots[0],
        roots[1],
        roots[2],
    )


def solution(mesh):
    spread = P(("shard", "rep"), None, None)
    matrix = P("shard", None)
    stack = P("shard", None, None)
    vector = P("shard")
    return jax.shard_map(
        local,
        mesh=mesh,
        in_specs=(
            spread, spread, vector, matrix, matrix, matrix, matrix, vector, matrix, stack, stack, spread,
        ),
        out_specs=(
            spread, spread, vector, matrix, matrix, matrix, matrix, vector, matrix, stack, stack, P(), P(), P(),
        ),
        check_vma=False,
    )
```
